256 devices in a mesh: obj: 32 (over z, x), view: 8 (over y, core).
Axes of the slice: x: 4, y: 4, z: 8, core: 2. Of those that a mesh axis runs over, the one named last changes fastest.
Arguments:
- features: bfloat16 [32, 8, 1369, 1024], P('obj', 'view'), may hold values from -6 to 6
- projection: int32 [32, 8, 1369], P('obj'), may hold values from 0 to 1023, as said below
- active_count: int32 [32], P('obj'), may hold values from 512 to 1024, as said below
- in_weight: bfloat16 [1024, 768], replicated, may hold values from -0.1875 to 0.1875
- norm_gain: float32 [768], replicated, may hold values from 0.1 to 1.9
- qkv_weight: bfloat16 [768, 2304], replicated, may hold values from -4 to 4
- out_weight: bfloat16 [768, 768], replicated, may hold values from -0.21875 to 0.21875
- cotangent: bfloat16 [32, 1024, 768], P('obj', 'view'), may hold values from -6 to 6
Outputs:
- latent: bfloat16 [32, 1024, 768], P('obj', 'view')
- in_grad: float32 [1024, 768], P('view')
- qkv_grad: float32 [768, 2304], P('view')
- out_grad: float32 [768, 768], P('view')
The draws below stay inside these ranges and needn't reach their ends.
Inputs may be any that keep to these rules, and one draw needn't show every extreme that they name: `projection`: every entry is below its object's active_count; in every object some live slots receive no patch. `active_count`: slots from this number on are empty: they are no keys, and their rows of latent are zero.
All inputs are finite; a program needn't handle non-finite values.
Results may differ from the reference program's by a relative error of at most 0.02.
Values may be sent and summed in bfloat16 or wider, within the bound.
A program may use at most 64 MiB of HBM per device.

```python
import jax
import jax.numpy as jnp
from jax import lax

FEAT = 1024
WIDTH = 768
HEADS = 12
HEAD_DIM = 64
PATCH = 1369
VOX_DEV = 128
OBJECTS = 32
VIEWS = 8
VOX = 1024
N_VIEW = 8


def shared_counts(key):
    return jax.random.randint(jax.random.fold_in(key, 101), (OBJECTS,), VOX // 2, VOX + 1, dtype=jnp.int32)


def draw_active_count(key, part):
    return shared_counts(key)


def draw_projection(key, part):
    live_counts = shared_counts(key)
    offsets = jax.random.randint(jax.random.fold_in(key, 102), (OBJECTS, 1, 1), 1, 16, dtype=jnp.int32)
    ceiling = jnp.broadcast_to(live_counts[:, None, None], (OBJECTS, VIEWS, PATCH))
    chosen = jax.random.randint(jax.random.fold_in(key, 103), (OBJECTS, VIEWS, PATCH), 0, ceiling, dtype=jnp.int32)
    return jnp.where(chosen % 16 == offsets, chosen - 1, chosen).astype(jnp.int32)


def draw_qkv_weight(key, part):
    drawn = jax.random.normal(jax.random.fold_in(key, 11), (WIDTH, 3 * WIDTH), jnp.float32) * WIDTH ** (-0.5)
    return jnp.clip(drawn, -4.0, 4.0).astype(jnp.bfloat16)


def level_of(stream_key, shape, pieces, low, largest):
    factor_of = 1.0
    for position, blocks in pieces:
        draws = jax.random.uniform(jax.random.fold_in(jax.random.fold_in(stream_key, 6), position), (blocks,), jnp.float32, low / len(pieces), largest / len(pieces))
        factor_of = factor_of * jnp.repeat(jnp.exp(draws), shape[position] // blocks).reshape((-1,) + (1,) * (len(shape) - 1 - position))
    return factor_of


def noise(stream_key, extent, scale, most, shards=(), kind=jnp.bfloat16):
    drawn = scale * jax.random.normal(stream_key, extent, jnp.float32)
    if shards:
        drawn = drawn * level_of(stream_key, extent, shards, -0.22, 0.18)
    return jnp.clip(drawn, -most, most).astype(kind)


def setup_inputs(seed: int = 0) -> dict:
    arg_keys = jax.random.split(jax.random.key(seed), 9)
    features = noise(arg_keys[0], (OBJECTS, VIEWS, PATCH, FEAT), 1.0, 6.0, ((0, 32), (1, 8)))
    projection = draw_projection(jax.random.fold_in(arg_keys[8], 71), 0)
    active_count = draw_active_count(jax.random.fold_in(arg_keys[8], 71), 0)
    in_weight = noise(arg_keys[3], (FEAT, WIDTH), FEAT ** -0.5, 0.1875)
    norm_gain = jnp.clip(1.0 + 0.18 * jax.random.normal(arg_keys[4], (WIDTH,), jnp.float32), 0.1, 1.9)
    qkv_weight = draw_qkv_weight(jax.random.fold_in(arg_keys[8], 71), 0)
    out_weight = noise(arg_keys[6], (WIDTH, WIDTH), WIDTH ** -0.5, 0.21875)
    cotangent = noise(arg_keys[7], (OBJECTS, VOX, WIDTH), 1.0, 6.0, ((0, 32), (1, 8)))
    return {"features": features, "projection": projection, "active_count": active_count, "in_weight": in_weight, "norm_gain": norm_gain, "qkv_weight": qkv_weight, "out_weight": out_weight, "cotangent": cotangent}


def normalize(base_rows):
    center = lax.optimization_barrier(jnp.mean(base_rows, axis=-1, keepdims=True))
    shifted = base_rows - center
    spread = lax.optimization_barrier(jnp.mean(shifted * shifted, axis=-1, keepdims=True))
    inverse = lax.rsqrt(spread + 1e-06)
    return (shifted * inverse, inverse)

def encode_object(feat_views, proj_views, live_count, upstream, in_weight, norm_gain, qkv_weight, out_weight):
    flat_feat = feat_views.reshape(VIEWS * PATCH, FEAT).astype(jnp.float32)
    flat_proj = proj_views.reshape(VIEWS * PATCH).astype(jnp.int32)
    totals = jax.ops.segment_sum(flat_feat, flat_proj, num_segments=VOX)
    counts = jax.ops.segment_sum(jnp.ones((VIEWS * PATCH,), jnp.float32), flat_proj, num_segments=VOX)
    voxels = (totals / jnp.maximum(counts, 1.0)[:, None]).astype(jnp.bfloat16)
    slot_ids = jnp.arange(VOX, dtype=jnp.int32)
    live_rows = (slot_ids < live_count).astype(jnp.float32)
    base_rows = jnp.dot(voxels, in_weight, preferred_element_type=jnp.float32)
    unit_rows, inverse = normalize(base_rows)
    normed = (unit_rows * norm_gain).astype(jnp.bfloat16)
    packed = jnp.dot(normed, qkv_weight, preferred_element_type=jnp.float32).astype(jnp.bfloat16)
    queries = packed[:, :WIDTH].reshape(VOX, HEADS, HEAD_DIM).astype(jnp.float32)
    key_heads = packed[:, WIDTH:2 * WIDTH].reshape(VOX, HEADS, HEAD_DIM).astype(jnp.float32)
    value_heads = packed[:, 2 * WIDTH:].reshape(VOX, HEADS, HEAD_DIM).astype(jnp.float32)
    inv_root = HEAD_DIM ** (-0.5)
    scores = jnp.einsum('qhd,khd->hqk', queries, key_heads) * inv_root
    key_live = live_rows[None, None, :] > 0.5
    masked = jnp.where(key_live, scores, -1e+30)
    row_peak = lax.optimization_barrier(jnp.max(masked, axis=-1, keepdims=True))
    expo_terms = jnp.where(key_live, jnp.exp(masked - row_peak), 0.0)
    weights = expo_terms / lax.optimization_barrier(jnp.sum(expo_terms, axis=-1, keepdims=True))
    prob_rows = weights.astype(jnp.bfloat16)
    mixed_full = jnp.einsum('hqk,khd->qhd', prob_rows.astype(jnp.float32), value_heads)
    attended = mixed_full.reshape(VOX, WIDTH).astype(jnp.bfloat16)
    branch = jnp.dot(attended, out_weight, preferred_element_type=jnp.float32)
    latent = (live_rows[:, None] * (base_rows + branch)).astype(jnp.bfloat16)
    seed_rows = (upstream.astype(jnp.float32) * live_rows[:, None] * (1.0 / OBJECTS)).astype(jnp.bfloat16)
    out_grad = jnp.dot(attended.T, seed_rows, preferred_element_type=jnp.float32)
    grad_attended = jnp.dot(seed_rows, out_weight.T, preferred_element_type=jnp.float32).astype(jnp.bfloat16)
    grad_heads = grad_attended.reshape(VOX, HEADS, HEAD_DIM).astype(jnp.float32)
    grad_probs = jnp.einsum('qhd,khd->hqk', grad_heads, value_heads)
    delta_rows = lax.optimization_barrier(jnp.sum(grad_heads * mixed_full, axis=-1)).T[:, :, None]
    grad_scores = (weights * (grad_probs - delta_rows) * inv_root).astype(jnp.bfloat16)
    grad_queries = jnp.einsum('hqk,khd->qhd', grad_scores.astype(jnp.float32), key_heads).reshape(VOX, WIDTH)
    score_blocks = grad_scores.astype(jnp.float32).reshape(HEADS, N_VIEW, VOX_DEV, VOX)
    prob_blocks = prob_rows.astype(jnp.float32).reshape(HEADS, N_VIEW, VOX_DEV, VOX)
    query_blocks = queries.reshape(N_VIEW, VOX_DEV, HEADS, HEAD_DIM)
    grad_blocks = grad_heads.reshape(N_VIEW, VOX_DEV, HEADS, HEAD_DIM)
    key_parts = jnp.einsum('hbqk,bqhd->bkhd', score_blocks, query_blocks).reshape(N_VIEW, VOX, WIDTH)
    value_parts = jnp.einsum('hbqk,bqhd->bkhd', prob_blocks, grad_blocks).reshape(N_VIEW, VOX, WIDTH)
    block_parts = jnp.concatenate([key_parts, value_parts], axis=2).astype(jnp.bfloat16)
    block_parts = lax.optimization_barrier(block_parts)
    key_grads = lax.optimization_barrier(jnp.sum(block_parts.astype(jnp.float32), axis=0))
    grad_packed = jnp.concatenate([grad_queries, key_grads], axis=1).astype(jnp.bfloat16)
    qkv_grad = jnp.dot(normed.T, grad_packed, preferred_element_type=jnp.float32)
    grad_normed = jnp.dot(grad_packed, qkv_weight.T, preferred_element_type=jnp.float32)
    grad_unit = grad_normed * norm_gain
    grad_branch = inverse * (grad_unit - lax.optimization_barrier(jnp.mean(grad_unit, axis=-1, keepdims=True)) - unit_rows * lax.optimization_barrier(jnp.mean(grad_unit * unit_rows, axis=-1, keepdims=True)))
    grad_base = (seed_rows.astype(jnp.float32) + grad_branch).astype(jnp.bfloat16)
    in_grad = jnp.dot(voxels.T, grad_base, preferred_element_type=jnp.float32)
    return (latent, in_grad, qkv_grad, out_grad)

def reference(features, projection, active_count, in_weight, norm_gain, qkv_weight, out_weight, cotangent):

    def advance(running, items):
        feat_views, proj_views, live_count, upstream = items
        latent, in_part, qkv_part, out_part = encode_object(feat_views, proj_views, live_count, upstream, in_weight, norm_gain, qkv_weight, out_weight)
        return ((running[0] + in_part, running[1] + qkv_part, running[2] + out_part), latent)
    start_sums = (jnp.zeros((FEAT, WIDTH), jnp.float32), jnp.zeros((WIDTH, 3 * WIDTH), jnp.float32), jnp.zeros((WIDTH, WIDTH), jnp.float32))
    sums, latent = lax.scan(advance, start_sums, (features, projection, active_count, cotangent))
    return (latent, sums[0], sums[1], sums[2])
```

```python
import jax
import jax.numpy as jnp
from jax import lax
from jax.experimental import pallas as pl
from jax.experimental.pallas import tpu as pltpu
from jax.sharding import PartitionSpec as P

HEAD_DIM = 64
MESH = pl.DeviceIdType.MESH
F32 = jnp.float32
BF16 = jnp.bfloat16
NEG = -1e30
CHUNKS = 4
QROWS = 256


def dot_nn(a, b):
    return lax.dot_general(a, b, (((1,), (0,)), ((), ())), preferred_element_type=F32)


def dot_nt(a, b):
    return lax.dot_general(a, b, (((1,), (1,)), ((), ())), preferred_element_type=F32)


def dot_tn(a, b):
    return lax.dot_general(a, b, (((0,), (0,)), ((), ())), preferred_element_type=F32)


def make_kernel(sizes):
    patches, feat, width, own, objects, views = sizes
    chips = 4
    heads = 3
    part = heads * HEAD_DIM
    group = chips * own
    slots = 2 * group
    cols = feat // CHUNKS
    vcols = feat // chips
    orows = part // 2

    def kernel(
        feat_hbm, proj_ref, count_ref, in_hbm, gain_ref, qkv_hbm, out_hbm, cot_hbm,
        latent_ref, gin_ref, gmain_ref,
        feat_v, inw, qkvw, outw, cot_v, hot, psend, precv, pown, ysend, yrecv,
        seeds, vox, vcol, base, unit, normed, wown, qs, kvs, gouts, att, attr, afull,
        dkv, dkv_send, dkv_recv, gp, gpr, gpfull, og, og_send, og_recv,
        qg, qg_send, qg_recv, qsum, qrecv, gball, ig, ig_send, ig_recv,
        mx, mxr, mz, mzr, mf, mg, ix, ixr, iz, izr, jf, jg,
        ssem, rsem, lsem,
    ):
        obj = lax.axis_index("obj")
        view = lax.axis_index("view")
        c = view // 2
        k = view % 2
        z = obj // 4
        x = obj % 4

        def at_y(d):
            return (obj, ((c + d) % 4) * 2 + k)

        def at_x(d):
            return (z * 4 + (x + d) % 4, view)

        def at_z(d):
            return (((z + d) % 8) * 4 + x, view)

        mate = (obj, c * 2 + (1 - k))
        used = [0]
        sent = []

        def send(src, dst, device):
            n = used[0]
            used[0] += 1
            cp = pltpu.make_async_remote_copy(
                src_ref=src, dst_ref=dst, send_sem=ssem.at[n], recv_sem=rsem.at[n],
                device_id=device, device_id_type=MESH,
            )
            cp.start()
            sent.append(cp)
            return cp

        def load(n, src, dst):
            cp = pltpu.make_async_copy(src, dst, lsem.at[n])
            cp.start()
            return cp

        barrier = pltpu.get_barrier_semaphore()
        peers = [mate]
        peers += [at_y(d) for d in (1, 2, 3)]
        peers += [at_x(d) for d in (1, 2, 3)]
        peers += [at_z(d) for d in range(1, 8)]
        for p in peers:
            pl.semaphore_signal(barrier, 1, device_id=p, device_id_type=MESH)

        l_cot = load(0, cot_hbm, cot_v)
        l_feat = load(1, feat_hbm, feat_v)
        l_out = load(2, out_hbm, outw)
        l_in = load(3, in_hbm, inw)
        l_qkv = load(4, qkv_hbm, qkvw)

        count = count_ref[0]
        own_ids = view * own + lax.broadcasted_iota(jnp.int32, (own, 1), 0)
        live = jnp.where(own_ids < count, 1.0, 0.0).astype(F32)
        proj_row = proj_ref[pl.ds(view, 1), :]
        for kk in range(2):
            par = k if kk else 1 - k
            for d in range(4):
                ids = (
                    ((c + 4 - d) % 4) * (2 * own)
                    + par * own
                    + lax.broadcasted_iota(jnp.int32, (own, patches), 0)
                )
                hot[kk, own * d : own * (d + 1), :] = jnp.where(ids == proj_row, 1.0, 0.0).astype(BF16)

        l_cot.wait()
        seeds[0:own, :] = (cot_v[...].astype(F32) * live * (1.0 / objects)).astype(BF16)
        pl.semaphore_wait(barrier, len(peers))
        seed_cp = [
            send(seeds.at[pl.ds(0, own)], seeds.at[pl.ds(own * d, own)], at_y(d)) for d in (1, 2, 3)
        ]

        l_feat.wait()
        mate_cp, y_cp = [], []

        def pass_on(j):
            mate_cp[j].wait_recv()
            both = pown[j] + precv[j].astype(F32)
            pown[j] = both
            ysend[j] = both.astype(BF16)
            y_cp.append(
                [
                    send(ysend.at[j, pl.ds(own * d, own)], yrecv.at[d - 1, j], at_y(4 - d))
                    for d in (1, 2, 3)
                ]
            )

        for j in range(CHUNKS):
            block = feat_v[:, cols * j : cols * (j + 1)]
            psend[j] = dot_nn(hot[0], block).astype(BF16)
            mate_cp.append(send(psend.at[j], precv.at[j], mate))
            pown[j] = dot_nn(hot[1], block)
            if j > 0:
                pass_on(j - 1)
        pass_on(CHUNKS - 1)

        number = jnp.zeros((own, 1), F32)
        for w in range(views):
            same = proj_ref[w : w + 1, :] == view * own + lax.broadcasted_iota(
                jnp.int32, (own, patches), 0
            )
            number += jnp.sum(jnp.where(same, 1.0, 0.0), axis=1, keepdims=True)
        number = jnp.maximum(number, 1.0)

        l_qkv.wait()
        for t in range(3):
            window = qkvw[:, pl.ds(pl.multiple_of(width * t + 128 * ((3 * c) // 2), 128), 256)]

            @pl.when(c % 2 == 0)
            def _():
                wown[:, part * t : part * (t + 1)] = window[:, 0:part]

            @pl.when(c % 2 == 1)
            def _():
                wown[:, part * t : part * (t + 1)] = window[:, 64 : 64 + part]

        l_out.wait()
        rows = outw[pl.ds(pl.multiple_of(part * c, 64), part), :]
        gouts[0:own, :] = dot_nt(seeds[0:own, :], rows).astype(BF16)
        for d in (1, 3, 2):
            seed_cp[d - 1].wait_recv()
            gouts[own * d : own * (d + 1), :] = dot_nt(seeds[own * d : own * (d + 1), :], rows).astype(BF16)

        for j in range(CHUNKS):
            total = pown[j, 0:own, :]
            for d in (1, 3, 2):
                y_cp[j][d - 1].wait_recv()
                total += yrecv[d - 1, j].astype(F32)
            vox[:, cols * j : cols * (j + 1)] = (total / number).astype(BF16)
        l_in.wait()
        base_rows = dot_nn(vox[...], inw[...])
        base[...] = base_rows
        shifted = base_rows - jnp.mean(base_rows, axis=1, keepdims=True)
        spread = jnp.mean(shifted * shifted, axis=1, keepdims=True)
        inverse = lax.rsqrt(spread + 1e-06)
        unit_rows = shifted * inverse
        unit[...] = unit_rows
        gain = gain_ref[...]
        normed[0:own, :] = (unit_rows * gain).astype(BF16)
        n_cp = [
            send(normed.at[pl.ds(0, own)], normed.at[pl.ds(own * d, own)], at_y(d)) for d in (1, 2, 3)
        ]
        v_cp = [
            send(
                vox.at[:, pl.ds(pl.multiple_of(vcols * ((c + d) % 4), 128), vcols)],
                vcol.at[pl.ds(own * d, own)],
                at_y(d),
            )
            for d in (1, 2, 3)
        ]
        vcol[0:own, :] = vox[:, pl.ds(pl.multiple_of(vcols * c, 128), vcols)]

        kv_cp = []
        for d in (0, 1, 3, 2):
            if d:
                n_cp[d - 1].wait_recv()
            at = slice(own * d, own * (d + 1))
            packed = dot_nn(normed[at, :], wown[...])
            qs[at, :] = (packed[:, 0:part] * (HEAD_DIM**-0.5)).astype(BF16)
            kvs[at, :] = packed[:, part : 3 * part].astype(BF16)
            kv_cp.append(
                send(kvs.at[pl.ds(own * d, own)], kvs.at[pl.ds(group + own * d, own)], mate)
            )

        lane = lax.broadcasted_iota(jnp.int32, (1, own), 1)
        pieces = []
        for par in (k, 1 - k):
            for d in range(4):
                ids = ((c + 4 - d) % 4) * (2 * own) + par * own + lane
                pieces.append(jnp.where(ids < count, 0.0, NEG).astype(F32))
        bias = jnp.concatenate(pieces, axis=1)
        for cp in kv_cp:
            cp.wait_recv()

        dkv_cp = []
        for h in range(heads):
            hs = slice(HEAD_DIM * h, HEAD_DIM * (h + 1))
            keys = kvs[:, hs]
            values = kvs[:, part + HEAD_DIM * h : part + HEAD_DIM * (h + 1)]
            grad_k = jnp.zeros((slots, HEAD_DIM), F32)
            grad_v = jnp.zeros((slots, HEAD_DIM), F32)
            for b in range(group // QROWS):
                rs = slice(QROWS * b, QROWS * (b + 1))
                q = qs[rs, hs]
                go = gouts[rs, hs]
                s = dot_nt(q, keys) + bias
                e = jnp.exp(s - jnp.max(s, axis=1, keepdims=True))
                w = e * (1.0 / jnp.sum(e, axis=1, keepdims=True))
                p = w.astype(BF16)
                mixed = dot_nn(p, values)
                att[rs, hs] = mixed.astype(BF16)
                delta = jnp.sum(go.astype(F32) * mixed, axis=1, keepdims=True)
                gs = (w * (dot_nt(go, values) - delta)).astype(BF16)
                gp[rs, hs] = (dot_nn(gs, keys) * (HEAD_DIM**-0.5)).astype(BF16)
                grad_k += dot_tn(gs, q)
                grad_v += dot_tn(p, go)
            both = jnp.concatenate([grad_k, grad_v], axis=1)
            dkv[h] = both[0:group]
            dkv_send[h] = both[group:].astype(BF16)
            dkv_cp.append(send(dkv_send.at[h], dkv_recv.at[h], mate))

        a_cp = [
            send(att.at[pl.ds(own * d, own)], attr.at[c], at_y(4 - d)) for d in (1, 2, 3)
        ]
        attr[c] = att[0:own, :]
        og[...] = dot_tn(att[...], seeds[...])
        og_send[...] = og[pl.ds(pl.multiple_of(orows * (1 - k), 32), orows), :].astype(BF16)
        og_cp = send(og_send, og_recv, mate)

        for h in range(heads):
            dkv_cp[h].wait_recv()
            both = dkv[h] + dkv_recv[h].astype(F32)
            gp[:, part + HEAD_DIM * h : part + HEAD_DIM * (h + 1)] = both[:, 0:HEAD_DIM].astype(BF16)
            gp[:, 2 * part + HEAD_DIM * h : 2 * part + HEAD_DIM * (h + 1)] = both[:, HEAD_DIM:].astype(BF16)
        g_cp = [send(gp.at[pl.ds(own * d, own)], gpr.at[c], at_y(4 - d)) for d in (1, 2, 3)]
        gpr[c] = gp[0:own, :]

        whole = dot_tn(normed[...], gp[...])
        for t in range(8):
            qg[t] = whole[orows * t : orows * (t + 1), :]
        for t in range(4):
            qg_send[t] = qg[2 * t + (1 - k)].astype(BF16)
        qg_cp = send(qg_send, qg_recv, mate)

        for t in range(4):
            a_at = slice(part * t, part * (t + 1))
            if t == 0:
                for cp in a_cp:
                    cp.wait_recv()
            afull[:, a_at] = attr[t]
        branch = dot_nn(afull[...], outw[...])
        latent_ref[...] = (live * (base[...] + branch)).astype(BF16)

        og_cp.wait_recv()
        og_sum = (
            og[pl.ds(pl.multiple_of(orows * k, 32), orows), :] + og_recv[...].astype(F32)
        ).astype(BF16)
        for r in range(4):
            mx[3, r] = og_sum[24 * r : 24 * (r + 1), :]

        qg_cp.wait_recv()
        for t in range(4):
            qsum[t] = (qg[2 * t + k] + qg_recv[t].astype(F32)).astype(BF16)
        t_cp = [send(qsum.at[(c + d) % 4], qrecv.at[c], at_y(d)) for d in (1, 2, 3)]
        qrecv[c] = qsum[c]

        for cp in g_cp:
            cp.wait_recv()
        for t in range(4):
            for s3 in range(3):
                gpfull[:, width * s3 + part * t : width * s3 + part * (t + 1)] = gpr[
                    t, :, part * s3 : part * (s3 + 1)
                ]
        grad_unit = dot_nt(gpfull[...], qkvw[...]) * gain
        unit_rows = unit[...]
        branch_grad = inverse * (
            grad_unit
            - jnp.mean(grad_unit, axis=1, keepdims=True)
            - unit_rows * jnp.mean(grad_unit * unit_rows, axis=1, keepdims=True)
        )
        gball[0:own, :] = (seeds[0:own, :].astype(F32) + branch_grad).astype(BF16)
        b_cp = [
            send(gball.at[pl.ds(0, own)], gball.at[pl.ds(own * d, own)], at_y(d)) for d in (1, 2, 3)
        ]

        for cp in t_cp:
            cp.wait_recv()
        for t in range(4):
            for s3 in range(3):
                for r in range(4):
                    mx[s3, r, :, part * t : part * (t + 1)] = qrecv[
                        t, 24 * r : 24 * (r + 1), part * s3 : part * (s3 + 1)
                    ]

        def x_scatter(buf, recv):
            return [send(buf.at[(x + d) % 4], recv.at[d - 1], at_x(d)) for d in (1, 2, 3)]

        def x_sum(buf, recv, cps, out):
            for cp in cps:
                cp.wait_recv()
            out[...] = (
                buf[x].astype(F32)
                + recv[0].astype(F32)
                + recv[1].astype(F32)
                + recv[2].astype(F32)
            ).astype(BF16)

        half = width // 2

        def z_piece(buf, where):
            return buf.at[where // 2, :, pl.ds(pl.multiple_of(half * (where % 2), 128), half)]

        def z_scatter(buf, recv):
            return [send(z_piece(buf, (z + d) % 8), recv.at[d - 1], at_z(d)) for d in range(1, 8)]

        def z_sum(buf, recv, cps, out):
            total = z_piece(buf, z)[...].astype(F32)
            for d in range(1, 8):
                cps[d - 1].wait_recv()
                total += recv[d - 1].astype(F32)
            out[...] = total.astype(BF16)

        def z_gather(fin, full):
            cps = [send(fin, z_piece(full.at[x], z), at_z(d)) for d in range(1, 8)]
            full[x, z // 2, :, pl.ds(pl.multiple_of(half * (z % 2), 128), half)] = fin[...]
            return cps

        def x_gather(full, cps):
            for cp in cps:
                cp.wait_recv()
            return [send(full.at[x], full.at[x], at_x(d)) for d in (1, 2, 3)]

        mx_cp = x_scatter(mx, mxr)

        for cp in v_cp + b_cp:
            cp.wait_recv()
        ig[...] = dot_tn(vcol[...], gball[...])
        ig_send[...] = ig[pl.ds(pl.multiple_of(own * (1 - k), 128), own), :].astype(BF16)
        ig_cp = send(ig_send, ig_recv, mate)
        ig_cp.wait_recv()
        ig_sum = (
            ig[pl.ds(pl.multiple_of(own * k, 128), own), :] + ig_recv[...].astype(F32)
        ).astype(BF16)
        for t in range(4):
            for r in range(4):
                ix[t, r] = ig_sum[32 * t + 8 * r : 32 * t + 8 * (r + 1), :]
        ix_cp = x_scatter(ix, ixr)

        x_sum(mx, mxr, mx_cp, mz)
        mz_cp = z_scatter(mz, mzr)
        x_sum(ix, ixr, ix_cp, iz)
        iz_cp = z_scatter(iz, izr)
        z_sum(mz, mzr, mz_cp, mf)
        mg_cp = z_gather(mf, mg)
        z_sum(iz, izr, iz_cp, jf)
        jg_cp = z_gather(jf, jg)
        mo_cp = x_gather(mg, mg_cp)
        jo_cp = x_gather(jg, jg_cp)
        for cp in mo_cp:
            cp.wait_recv()
        gmain_ref[...] = mg[...]
        for cp in jo_cp:
            cp.wait_recv()
        gin_ref[...] = jg[...]
        for cp in sent:
            cp.wait_send()

    scratch = [
        ((patches, feat), BF16), ((feat, width), BF16), ((width, 3 * width), BF16),
        ((width, width), BF16), ((own, width), BF16), ((2, group, patches), BF16),
        ((CHUNKS, group, cols), BF16), ((CHUNKS, group, cols), BF16), ((CHUNKS, group, cols), F32),
        ((CHUNKS, group, cols), BF16), ((3, CHUNKS, own, cols), BF16),
        ((group, width), BF16), ((own, feat), BF16), ((group, vcols), BF16),
        ((own, width), F32), ((own, width), F32), ((group, width), BF16),
        ((width, 3 * part), BF16), ((group, part), BF16), ((slots, 2 * part), BF16),
        ((group, part), BF16), ((group, part), BF16), ((4, own, part), BF16), ((own, width), BF16),
        ((heads, group, 128), F32), ((heads, group, 128), BF16), ((heads, group, 128), BF16),
        ((group, 3 * part), BF16), ((4, own, 3 * part), BF16), ((own, 3 * width), BF16),
        ((part, width), F32), ((orows, width), BF16), ((orows, width), BF16),
        ((8, orows, 3 * part), F32), ((4, orows, 3 * part), BF16), ((4, orows, 3 * part), BF16),
        ((4, orows, 3 * part), BF16), ((4, orows, 3 * part), BF16),
        ((group, width), BF16), ((2 * own, width), F32), ((own, width), BF16), ((own, width), BF16),
        ((4, 4, 24, width), BF16), ((3, 4, 24, width), BF16), ((4, 24, width), BF16),
        ((7, 24, width // 2), BF16), ((24, width // 2), BF16), ((4, 4, 24, width), BF16),
        ((4, 4, 8, width), BF16), ((3, 4, 8, width), BF16), ((4, 8, width), BF16),
        ((7, 8, width // 2), BF16), ((8, width // 2), BF16), ((4, 4, 8, width), BF16),
    ]
    return kernel, scratch


def per_device(
    features, projection, active_count, in_weight, norm_gain, qkv_weight, out_weight, cotangent
):
    patches, feat = features.shape[2:]
    own, width = cotangent.shape[1:]
    views = projection.shape[1]
    objects = lax.axis_size("obj")
    kernel, scratch = make_kernel((patches, feat, width, own, objects, views))
    vmem = pl.BlockSpec(memory_space=pltpu.VMEM)
    hbm = pl.BlockSpec(memory_space=pl.ANY)
    latent, gin, gmain = pl.pallas_call(
        kernel,
        name="encode",
        out_shape=(
            jax.ShapeDtypeStruct((own, width), BF16),
            jax.ShapeDtypeStruct((4, 4, 8, width), BF16),
            jax.ShapeDtypeStruct((4, 4, 24, width), BF16),
        ),
        in_specs=[hbm, vmem, pl.BlockSpec(memory_space=pltpu.SMEM), hbm, vmem, hbm, hbm, hbm],
        out_specs=(vmem, vmem, vmem),
        scratch_shapes=[pltpu.VMEM(s, t) for s, t in scratch]
        + [
            pltpu.SemaphoreType.DMA((96,)),
            pltpu.SemaphoreType.DMA((96,)),
            pltpu.SemaphoreType.DMA((5,)),
        ],
        compiler_params=pltpu.CompilerParams(
            collective_id=0, has_side_effects=True, vmem_limit_bytes=62 * 1024 * 1024
        ),
    )(
        features.reshape(patches, feat),
        projection.reshape(views, patches),
        active_count,
        in_weight,
        norm_gain.reshape(1, width),
        qkv_weight,
        out_weight,
        cotangent.reshape(own, width),
    )
    gmain = gmain.reshape(4, 96, width)
    qkv_grad = jnp.concatenate([gmain[0], gmain[1], gmain[2]], axis=1).astype(F32)
    return (
        latent[None],
        gin.reshape(own, width).astype(F32),
        qkv_grad,
        gmain[3].astype(F32),
    )


def solution(mesh):
    return jax.shard_map(
        per_device,
        mesh=mesh,
        in_specs=(
            P("obj", "view", None, None),
            P("obj", None, None),
            P("obj"),
            P(),
            P(),
            P(),
            P(),
            P("obj", "view", None),
        ),
        out_specs=(P("obj", "view", None), P("view", None), P("view", None), P("view", None)),
        check_vma=False,
    )
```

```python
import jax
import jax.numpy as jnp
from jax import lax
from jax.experimental import pallas as pl
from jax.experimental.pallas import tpu as pltpu
from jax.sharding import PartitionSpec as P

HEAD_DIM = 64
MESH = pl.DeviceIdType.MESH
F32 = jnp.float32
BF16 = jnp.bfloat16
NEG = -1e30
CHUNKS = 4
QROWS = 256


def dot_nn(a, b):
    return lax.dot_general(a, b, (((1,), (0,)), ((), ())), preferred_element_type=F32)


def dot_nt(a, b):
    return lax.dot_general(a, b, (((1,), (1,)), ((), ())), preferred_element_type=F32)


def dot_tn(a, b):
    return lax.dot_general(a, b, (((0,), (0,)), ((), ())), preferred_element_type=F32)


def make_kernel(sizes):
    patches, feat, width, own, objects, views = sizes
    chips = 4
    heads = 3
    part = heads * HEAD_DIM
    group = chips * own
    slots = 2 * group
    cols = feat // CHUNKS
    vcols = feat // chips
    orows = part // 2

    def kernel(
        feat_hbm, proj_ref, count_ref, in_hbm, gain_ref, qkv_hbm, out_hbm, cot_hbm,
        latent_ref, gin_ref, gmain_ref,
        feat_v, inw, qkvw, outw, cot_v, hot, psend, precv, pown, ysend, rrecv, yrecv,
        seeds, vox, vcol, base, unit, normed, turned, wown, qs, kvs, gsend, gouts, att, attr, afull,
        dkv, dkv_send, dkv_recv, gp, gpr, gpfull, og, og_send, og_recv,
        qg, qg_send, qg_recv, qsum, qrecv, joined, gball, ig, ig_send, ig_recv,
        mx, mxr, mz, mzr, mf, mg, ix, ixr, iz, izr, jf, jg,
        ssem, rsem, lsem,
    ):
        obj = lax.axis_index("obj")
        view = lax.axis_index("view")
        c = view // 2
        k = view % 2
        z = obj // 4
        x = obj % 4

        def at_y(d):
            return (obj, ((c + d) % 4) * 2 + k)

        def at_x(d):
            return (z * 4 + (x + d) % 4, view)

        def at_z(d):
            return (((z + d) % 8) * 4 + x, view)

        mate = (obj, c * 2 + (1 - k))
        used = [0]
        sent = []

        def send(src, dst, device):
            n = used[0]
            used[0] += 1
            cp = pltpu.make_async_remote_copy(
                src_ref=src, dst_ref=dst, send_sem=ssem.at[n], recv_sem=rsem.at[n],
                device_id=device, device_id_type=MESH,
            )
            cp.start()
            sent.append(cp)
            return cp

        def load(n, src, dst):
            cp = pltpu.make_async_copy(src, dst, lsem.at[n])
            cp.start()
            return cp

        def rows_of(d, half=None):
            if half is None:
                return pl.ds(own * d, own)
            return pl.ds(own * d + own // 2 * half, own // 2)

        def gather_start(buf):
            out = {}
            for to, slot, order in ((1, 1, (0, 1)), (3, 3, (1, 0))):
                for half in order:
                    out[slot, half] = send(
                        buf.at[rows_of(0, half)], buf.at[rows_of(slot, half)], at_y(to)
                    )
            return out

        def gather_pass(buf, cps):
            cps[1, 0].wait_recv()
            cps[2, 0] = send(buf.at[rows_of(1, 0)], buf.at[rows_of(2, 0)], at_y(1))
            cps[3, 1].wait_recv()
            cps[2, 1] = send(buf.at[rows_of(3, 1)], buf.at[rows_of(2, 1)], at_y(3))

        def gather_wait(cps, slot):
            for half in ((1,), (0, 1), (0,))[slot - 1]:
                cps[slot, half].wait_recv()

        barrier = pltpu.get_barrier_semaphore()
        peers = [mate]
        peers += [at_y(d) for d in (1, 2, 3)]
        peers += [at_x(d) for d in (1, 2, 3)]
        peers += [at_z(d) for d in range(1, 8)]
        for p in peers:
            pl.semaphore_signal(barrier, 1, device_id=p, device_id_type=MESH)

        l_feat = load(1, feat_hbm, feat_v)
        l_cot = load(0, cot_hbm, cot_v)
        l_out = load(2, out_hbm, outw)
        l_in = load(3, in_hbm, inw)
        l_qkv = load(4, qkv_hbm, qkvw)

        count = count_ref[0]
        own_ids = view * own + lax.broadcasted_iota(jnp.int32, (own, 1), 0)
        live = jnp.where(own_ids < count, 1.0, 0.0).astype(F32)
        proj_row = proj_ref[pl.ds(view, 1), :]
        for kk in range(2):
            par = k if kk else 1 - k
            for d in range(4):
                ids = (
                    ((c + 4 - d) % 4) * (2 * own)
                    + par * own
                    + lax.broadcasted_iota(jnp.int32, (own, patches), 0)
                )
                hot[kk, own * d : own * (d + 1), :] = jnp.where(ids == proj_row, 1.0, 0.0).astype(BF16)

        mate_cp, relay_cp, y_cp = [], [], []

        def sums(j, kk):
            return dot_nn(hot[kk], feat_v[:, cols * j : cols * (j + 1)])

        def combine(j):
            mate_cp[j].wait_recv()
            both = pown[j] + precv[j].astype(F32)
            pown[j] = both
            far = slice(2 * own, 3 * own)
            ysend[j, far, :] = both[far, :].astype(BF16)
            relay_cp.append(
                [
                    send(
                        ysend.at[j, rows_of(2), pl.ds(cols // 2 * s, cols // 2)],
                        rrecv.at[s, j],
                        at_y((1, 3)[s]),
                    )
                    for s in range(2)
                ]
            )

        def forward(j):
            cps = []
            for s, d in ((0, 3), (1, 1)):
                relay_cp[j][s].wait_recv()
                block = pown[j, own * d : own * (d + 1), :]
                at = slice(own * d, own * (d + 1))
                mid = cols // 2
                passed = rrecv[s, j].astype(F32)
                if s == 0:
                    ysend[j, at, 0:mid] = (block[:, 0:mid] + passed).astype(BF16)
                    ysend[j, at, mid:] = block[:, mid:].astype(BF16)
                else:
                    ysend[j, at, 0:mid] = block[:, 0:mid].astype(BF16)
                    ysend[j, at, mid:] = (block[:, mid:] + passed).astype(BF16)
                cps.append(send(ysend.at[j, rows_of(d)], yrecv.at[s, j], at_y(4 - d)))
            y_cp.append(cps)

        l_feat.wait()
        psend[0] = sums(0, 0).astype(BF16)
        pl.semaphore_wait(barrier, len(peers))
        mate_cp.append(send(psend.at[0], precv.at[0], mate))
        l_cot.wait()
        seeds[0:own, :] = (cot_v[...].astype(F32) * live * (1.0 / objects)).astype(BF16)
        l_out.wait()
        for t in range(4):
            gsend[t] = dot_nt(seeds[0:own, :], outw[part * t : part * (t + 1), :]).astype(BF16)
        o_cp = [send(gsend.at[(c + d) % 4], gouts.at[rows_of(d)], at_y(d)) for d in (1, 2, 3)]
        gouts[0:own, :] = gsend[c]
        pown[0] = sums(0, 1)
        for j in range(1, CHUNKS):
            psend[j] = sums(j, 0).astype(BF16)
            mate_cp.append(send(psend.at[j], precv.at[j], mate))
            combine(j - 1)
            pown[j] = sums(j, 1)
            if j > 1:
                forward(j - 2)
        combine(CHUNKS - 1)
        forward(CHUNKS - 2)

        number = jnp.zeros((own, 1), F32)
        for w in range(views):
            same = proj_ref[w : w + 1, :] == view * own + lax.broadcasted_iota(
                jnp.int32, (own, patches), 0
            )
            number += jnp.sum(jnp.where(same, 1.0, 0.0), axis=1, keepdims=True)
        number = jnp.maximum(number, 1.0)
        forward(CHUNKS - 1)

        l_qkv.wait()
        for t in range(3):
            window = qkvw[:, pl.ds(pl.multiple_of(width * t + 128 * ((3 * c) // 2), 128), 256)]

            @pl.when(c % 2 == 0)
            def _():
                wown[:, part * t : part * (t + 1)] = window[:, 0:part]

            @pl.when(c % 2 == 1)
            def _():
                wown[:, part * t : part * (t + 1)] = window[:, 64 : 64 + part]

        for j in range(CHUNKS):
            total = pown[j, 0:own, :]
            for s in range(2):
                y_cp[j][s].wait_recv()
                total += yrecv[s, j].astype(F32)
            vox[:, cols * j : cols * (j + 1)] = (total / number).astype(BF16)
        l_in.wait()
        base_rows = dot_nn(vox[...], inw[...])
        base[...] = base_rows
        shifted = base_rows - jnp.mean(base_rows, axis=1, keepdims=True)
        spread = jnp.mean(shifted * shifted, axis=1, keepdims=True)
        inverse = lax.rsqrt(spread + 1e-06)
        unit_rows = shifted * inverse
        unit[...] = unit_rows
        gain = gain_ref[...].reshape(1, width)
        normed[0:own, :] = (unit_rows * gain).astype(BF16)
        n_cp = gather_start(normed)

        kv_cp = []

        def project(d):
            at = slice(own * d, own * (d + 1))
            packed = dot_nn(normed[at, :], wown[...])
            qs[at, :] = (packed[:, 0:part] * (HEAD_DIM**-0.5)).astype(BF16)
            kvs[at, :] = packed[:, part : 3 * part].astype(BF16)
            kv_cp.append(
                send(kvs.at[rows_of(d)], kvs.at[pl.ds(group + own * d, own)], mate)
            )
            turned[:, at] = normed[at, :].T

        project(0)
        gather_pass(normed, n_cp)
        s_cp = gather_start(seeds)
        for d in (1, 3):
            gather_wait(n_cp, d)
            project(d)
        gather_wait(n_cp, 2)
        project(2)
        gather_pass(seeds, s_cp)
        v_cp = [
            send(
                vox.at[:, pl.ds(pl.multiple_of(vcols * ((c + d) % 4), 128), vcols)],
                vcol.at[rows_of(d)],
                at_y(d),
            )
            for d in (1, 2, 3)
        ]
        vcol[0:own, :] = vox[:, pl.ds(pl.multiple_of(vcols * c, 128), vcols)]

        lane = lax.broadcasted_iota(jnp.int32, (1, own), 1)
        pieces = []
        for par in (k, 1 - k):
            for d in range(4):
                ids = ((c + 4 - d) % 4) * (2 * own) + par * own + lane
                pieces.append(jnp.where(ids < count, 0.0, NEG).astype(F32))
        bias = jnp.concatenate(pieces, axis=1)
        for cp in kv_cp:
            cp.wait_recv()
        for cp in o_cp:
            cp.wait_recv()

        dkv_cp, g_cp, qg_cp, t_cp = [], [], [], []

        def attend(h):
            hs = slice(HEAD_DIM * h, HEAD_DIM * (h + 1))
            keys = kvs[:, hs]
            values = kvs[:, part + HEAD_DIM * h : part + HEAD_DIM * (h + 1)]
            grad_k = jnp.zeros((slots, HEAD_DIM), F32)
            grad_v = jnp.zeros((slots, HEAD_DIM), F32)
            for b in range(group // QROWS):
                rs = slice(QROWS * b, QROWS * (b + 1))
                q = qs[rs, hs]
                go = gouts[rs, hs]
                s = dot_nt(q, keys) + bias
                e = jnp.exp(s - jnp.max(s, axis=1, keepdims=True))
                w = e * (1.0 / jnp.sum(e, axis=1, keepdims=True))
                p = w.astype(BF16)
                mixed = dot_nn(p, values)
                att[rs, hs] = mixed.astype(BF16)
                delta = jnp.sum(go.astype(F32) * mixed, axis=1, keepdims=True)
                gs = (w * (dot_nt(go, values) - delta)).astype(BF16)
                gp[h, rs, 0:HEAD_DIM] = (dot_nn(gs, keys) * (HEAD_DIM**-0.5)).astype(BF16)
                grad_k += dot_tn(gs, q)
                grad_v += dot_tn(p, go)
            both = jnp.concatenate([grad_k, grad_v], axis=1)
            dkv_send[h] = both[group:].astype(BF16)
            dkv_cp.append(send(dkv_send.at[h], dkv_recv.at[h], mate))
            dkv[h] = both[0:group]

        def finish(h):
            dkv_cp[h].wait_recv()
            both = dkv[h] + dkv_recv[h].astype(F32)
            gp[h, :, HEAD_DIM:] = both.astype(BF16)
            for d in (2, 1, 3):
                g_cp.append(send(gp.at[h, rows_of(d)], gpr.at[c, h], at_y(4 - d)))
            gpr[c, h] = gp[h, 0:own, :]
            whole = dot_nn(turned[...], gp[h])
            for t in range(8):
                qg[h, t] = whole[orows * t : orows * (t + 1), :]
            for t in range(4):
                qg_send[h, t] = qg[h, 2 * t + (1 - k)].astype(BF16)
            qg_cp.append(send(qg_send.at[h], qg_recv.at[h], mate))

        def swap(h):
            qg_cp[h].wait_recv()
            for t in range(4):
                qsum[h, t] = (qg[h, 2 * t + k] + qg_recv[h, t].astype(F32)).astype(BF16)
            for d in (2, 1, 3):
                t_cp.append(send(qsum.at[h, (c + d) % 4], qrecv.at[c, h], at_y(d)))
            qrecv[c, h] = qsum[h, c]

        attend(0)
        attend(1)
        finish(0)
        attend(2)
        finish(1)
        swap(0)
        for d in (1, 3, 2):
            gather_wait(s_cp, d)
        og[...] = dot_tn(att[...], seeds[...])
        og_send[...] = og[pl.ds(pl.multiple_of(orows * (1 - k), 32), orows), :].astype(BF16)
        og_cp = send(og_send, og_recv, mate)
        finish(2)
        swap(1)
        swap(2)
        a_cp = [send(att.at[rows_of(d)], attr.at[c], at_y(4 - d)) for d in (1, 2, 3)]
        attr[c] = att[0:own, :]

        og_cp.wait_recv()
        og_sum = (
            og[pl.ds(pl.multiple_of(orows * k, 32), orows), :] + og_recv[...].astype(F32)
        ).astype(BF16)
        for r in range(4):
            mx[3, r] = og_sum[24 * r : 24 * (r + 1), :]

        for cp in g_cp:
            cp.wait_recv()
        for t in range(4):
            for h in range(3):
                for s3 in range(3):
                    at = width * s3 + part * t + HEAD_DIM * h
                    gpfull[:, at : at + HEAD_DIM] = gpr[
                        t, h, :, HEAD_DIM * s3 : HEAD_DIM * (s3 + 1)
                    ]
        grad_unit = dot_nt(gpfull[...], qkvw[...]) * gain
        unit_rows = unit[...]
        branch_grad = inverse * (
            grad_unit
            - jnp.mean(grad_unit, axis=1, keepdims=True)
            - unit_rows * jnp.mean(grad_unit * unit_rows, axis=1, keepdims=True)
        )
        gball[0:own, :] = (seeds[0:own, :].astype(F32) + branch_grad).astype(BF16)
        b_cp = gather_start(gball)

        for cp in t_cp:
            cp.wait_recv()
        for s3 in range(3):
            for t in range(4):
                for h in range(3):
                    at = part * t + HEAD_DIM * h
                    joined[s3, :, at : at + HEAD_DIM] = qrecv[
                        t, h, :, HEAD_DIM * s3 : HEAD_DIM * (s3 + 1)
                    ]
            for r in range(4):
                mx[s3, r] = joined[s3, 24 * r : 24 * (r + 1), :]

        def x_scatter(buf, recv):
            return [send(buf.at[(x + d) % 4], recv.at[d - 1], at_x(d)) for d in (2, 1, 3)]

        def x_sum(buf, recv, cps, out):
            for cp in cps:
                cp.wait_recv()
            out[...] = (
                buf[x].astype(F32)
                + recv[0].astype(F32)
                + recv[1].astype(F32)
                + recv[2].astype(F32)
            ).astype(BF16)

        half = width // 2
        z_order = (4, 3, 5, 2, 6, 1, 7)

        def z_piece(buf, where):
            return buf.at[where // 2, :, pl.ds(pl.multiple_of(half * (where % 2), 128), half)]

        def z_scatter(buf, recv):
            return [send(z_piece(buf, (z + d) % 8), recv.at[d - 1], at_z(d)) for d in z_order]

        def z_sum(buf, recv, cps, out):
            total = z_piece(buf, z)[...].astype(F32)
            for cp in cps:
                cp.wait_recv()
            for d in range(1, 8):
                total += recv[d - 1].astype(F32)
            out[...] = total.astype(BF16)

        def z_gather(fin, full):
            cps = [send(fin, z_piece(full.at[x], z), at_z(d)) for d in z_order]
            full[x, z // 2, :, pl.ds(pl.multiple_of(half * (z % 2), 128), half)] = fin[...]
            return cps

        def x_gather(full, cps):
            for cp in cps:
                cp.wait_recv()
            return [send(full.at[x], full.at[x], at_x(d)) for d in (2, 1, 3)]

        mx_cp = x_scatter(mx, mxr)
        gather_pass(gball, b_cp)
        for cp in a_cp:
            cp.wait_recv()
        for t in range(4):
            afull[:, part * t : part * (t + 1)] = attr[t]
        branch = dot_nn(afull[...], outw[...])
        latent_ref[...] = (live * (base[...] + branch)).astype(BF16)

        for cp in v_cp:
            cp.wait_recv()
        for d in (1, 3, 2):
            gather_wait(b_cp, d)
        ig[...] = dot_tn(vcol[...], gball[...])
        ig_send[...] = ig[pl.ds(pl.multiple_of(own * (1 - k), 128), own), :].astype(BF16)
        ig_cp = send(ig_send, ig_recv, mate)
        x_sum(mx, mxr, mx_cp, mz)
        mz_cp = z_scatter(mz, mzr)
        ig_cp.wait_recv()
        ig_sum = (
            ig[pl.ds(pl.multiple_of(own * k, 128), own), :] + ig_recv[...].astype(F32)
        ).astype(BF16)
        for t in range(4):
            for r in range(4):
                ix[t, r] = ig_sum[32 * t + 8 * r : 32 * t + 8 * (r + 1), :]
        ix_cp = x_scatter(ix, ixr)

        x_sum(ix, ixr, ix_cp, iz)
        iz_cp = z_scatter(iz, izr)
        z_sum(mz, mzr, mz_cp, mf)
        mg_cp = z_gather(mf, mg)
        z_sum(iz, izr, iz_cp, jf)
        jg_cp = z_gather(jf, jg)
        mo_cp = x_gather(mg, mg_cp)
        jo_cp = x_gather(jg, jg_cp)
        for cp in mo_cp:
            cp.wait_recv()
        gmain_ref[...] = mg[...]
        for cp in jo_cp:
            cp.wait_recv()
        gin_ref[...] = jg[...]
        for cp in sent:
            cp.wait_send()

    scratch = [
        ((patches, feat), BF16), ((feat, width), BF16), ((width, 3 * width), BF16),
        ((width, width), BF16), ((own, width), BF16), ((2, group, patches), BF16),
        ((CHUNKS, group, cols), BF16), ((CHUNKS, group, cols), BF16), ((CHUNKS, group, cols), F32),
        ((CHUNKS, group, cols), BF16), ((2, CHUNKS, own, cols // 2), BF16),
        ((2, CHUNKS, own, cols), BF16),
        ((group, width), BF16), ((own, feat), BF16), ((group, vcols), BF16),
        ((own, width), F32), ((own, width), F32), ((group, width), BF16), ((width, group), BF16),
        ((width, 3 * part), BF16), ((group, part), BF16), ((slots, 2 * part), BF16),
        ((4, own, part), BF16), ((group, part), BF16), ((group, part), BF16),
        ((4, own, part), BF16), ((own, width), BF16),
        ((heads, group, 128), F32), ((heads, group, 128), BF16), ((heads, group, 128), BF16),
        ((heads, group, part), BF16), ((4, heads, own, part), BF16), ((own, 3 * width), BF16),
        ((part, width), F32), ((orows, width), BF16), ((orows, width), BF16),
        ((heads, 8, orows, part), F32), ((heads, 4, orows, part), BF16),
        ((heads, 4, orows, part), BF16), ((heads, 4, orows, part), BF16),
        ((4, heads, orows, part), BF16), ((3, orows, width), BF16),
        ((group, width), BF16), ((2 * own, width), F32), ((own, width), BF16), ((own, width), BF16),
        ((4, 4, 24, width), BF16), ((3, 4, 24, width), BF16), ((4, 24, width), BF16),
        ((7, 24, width // 2), BF16), ((24, width // 2), BF16), ((4, 4, 24, width), BF16),
        ((4, 4, 8, width), BF16), ((3, 4, 8, width), BF16), ((4, 8, width), BF16),
        ((7, 8, width // 2), BF16), ((8, width // 2), BF16), ((4, 4, 8, width), BF16),
    ]
    return kernel, scratch


def write_out(latent_ref, gin_ref, gmain_ref, latent_out, in_out, qkv_out, out_out):
    width = latent_ref.shape[1]
    latent_out[...] = latent_ref[...]
    for t in range(4):
        for r in range(4):
            at = slice(32 * t + 8 * r, 32 * t + 8 * (r + 1))
            in_out[at, :] = gin_ref[t, r].astype(F32)
    for r in range(4):
        at = slice(24 * r, 24 * (r + 1))
        for s in range(3):
            qkv_out[at, width * s : width * (s + 1)] = gmain_ref[s, r].astype(F32)
        out_out[at, :] = gmain_ref[3, r].astype(F32)


def per_device(
    features, projection, active_count, in_weight, norm_gain, qkv_weight, out_weight, cotangent
):
    patches, feat = features.shape[2:]
    own, width = cotangent.shape[1:]
    views = projection.shape[1]
    objects = lax.axis_size("obj")
    kernel, scratch = make_kernel((patches, feat, width, own, objects, views))
    vmem = pl.BlockSpec(memory_space=pltpu.VMEM)
    hbm = pl.BlockSpec(memory_space=pl.ANY)
    latent, gin, gmain = pl.pallas_call(
        kernel,
        name="encode",
        out_shape=(
            jax.ShapeDtypeStruct((own, width), BF16),
            jax.ShapeDtypeStruct((4, 4, 8, width), BF16),
            jax.ShapeDtypeStruct((4, 4, 24, width), BF16),
        ),
        in_specs=[hbm, vmem, pl.BlockSpec(memory_space=pltpu.SMEM), hbm, vmem, hbm, hbm, hbm],
        out_specs=(vmem, vmem, vmem),
        scratch_shapes=[pltpu.VMEM(s, t) for s, t in scratch]
        + [
            pltpu.SemaphoreType.DMA((128,)),
            pltpu.SemaphoreType.DMA((128,)),
            pltpu.SemaphoreType.DMA((5,)),
        ],
        compiler_params=pltpu.CompilerParams(
            collective_id=0, has_side_effects=True, vmem_limit_bytes=62 * 1024 * 1024
        ),
    )(
        features.reshape(patches, feat),
        projection.reshape(views, patches),
        active_count,
        in_weight,
        norm_gain,
        qkv_weight,
        out_weight,
        cotangent.reshape(own, width),
    )
    latent, in_grad, qkv_grad, out_grad = pl.pallas_call(
        write_out,
        name="write_out",
        out_shape=(
            jax.ShapeDtypeStruct((own, width), BF16),
            jax.ShapeDtypeStruct((own, width), F32),
            jax.ShapeDtypeStruct((96, 3 * width), F32),
            jax.ShapeDtypeStruct((96, width), F32),
        ),
        in_specs=[vmem, vmem, vmem],
        out_specs=(vmem, vmem, vmem, vmem),
    )(latent, gin, gmain)
    return (latent[None], in_grad, qkv_grad, out_grad)


def solution(mesh):
    return jax.shard_map(
        per_device,
        mesh=mesh,
        in_specs=(
            P("obj", "view", None, None),
            P("obj", None, None),
            P("obj"),
            P(),
            P(),
            P(),
            P(),
            P("obj", "view", None),
        ),
        out_specs=(P("obj", "view", None), P("view", None), P("view", None), P("view", None)),
        check_vma=False,
    )
```

```python
import jax
import jax.numpy as jnp
from jax import lax
from jax.experimental import pallas as pl
from jax.experimental.pallas import tpu as pltpu
from jax.sharding import PartitionSpec as P

HEAD_DIM = 64
MESH = pl.DeviceIdType.MESH
F32 = jnp.float32
BF16 = jnp.bfloat16
NEG = -1e30
CHUNKS = 4
QROWS = 256


def dot_nn(a, b):
    return lax.dot_general(a, b, (((1,), (0,)), ((), ())), preferred_element_type=F32)


def dot_nt(a, b):
    return lax.dot_general(a, b, (((1,), (1,)), ((), ())), preferred_element_type=F32)


def dot_tn(a, b):
    return lax.dot_general(a, b, (((0,), (0,)), ((), ())), preferred_element_type=F32)


class Group:
    def __init__(self, like, send_sem, recv_sem):
        self.like, self.send_sem, self.recv_sem = like, send_sem, recv_sem

    def wait_send(self):
        pltpu.make_async_copy(self.like, self.like, self.send_sem).wait()

    def wait_recv(self):
        pltpu.make_async_copy(self.like, self.like, self.recv_sem).wait()


def make_kernel(sizes):
    patches, feat, width, own, objects, views = sizes
    chips = 4
    heads = 3
    part = heads * HEAD_DIM
    group = chips * own
    slots = 2 * group
    cols = feat // CHUNKS
    vcols = feat // chips
    orows = part // 2

    def kernel(
        feat_hbm, proj_hbm, count_hbm, in_hbm, gain_hbm, qkv_hbm, out_hbm, cot_hbm,
        latent_hbm, gin_hbm, gmain_hbm,
        proj_ref, gain_ref, latent_v, feat_v, inw, qkvw, outw, cot_v, hot, psend, precv, pown, ysend, rrecv, yrecv,
        seeds, vox, vcol, base, unit, normed, turned, wown, qs, kvs, gsend, gouts, att, afull,
        dkv, dkv_send, dkv_recv, gp, gq, gpr, gpfull, og, og_send, og_recv,
        qg, qg_send, qg_recv, qsum, qlast, qrecv, qrlast, gball, ig, ig_send, ig_recv,
        mx, mxr, mz, mzr, mf, mg, ix, ixr, jf, jg,
        count_ref, ssem, rsem, lsem, ready,
    ):
        obj = lax.axis_index("obj")
        view = lax.axis_index("view")
        c = view // 2
        k = view % 2
        z = obj // 4
        x = obj % 4

        def at_y(d):
            return (obj, ((c + d) % 4) * 2 + k)

        def at_x(d):
            return (z * 4 + (x + d) % 4, view)

        def at_z(d):
            return (((z + d) % 8) * 4 + x, view)

        def at_o(dz, dx):
            return (((z + dz) % 8) * 4 + (x + dx) % 4, view)

        others = [(dz, dx) for dz in (4, 3, 5, 2, 6, 1, 7, 0) for dx in (2, 1, 3, 0) if dz or dx]
        mate = (obj, c * 2 + (1 - k))
        used = [0]
        sent = []

        def send(src, dst, device):
            n = used[0]
            used[0] += 1
            cp = pltpu.make_async_remote_copy(
                src_ref=src, dst_ref=dst, send_sem=ssem.at[n], recv_sem=rsem.at[n],
                device_id=device, device_id_type=MESH,
            )
            cp.start()
            sent.append(cp)
            return cp

        def send_all(triples, like):
            n = used[0]
            used[0] += 1
            for src, dst, device in triples:
                pltpu.make_async_remote_copy(
                    src_ref=src, dst_ref=dst, send_sem=ssem.at[n], recv_sem=rsem.at[n],
                    device_id=device, device_id_type=MESH,
                ).start()
            group = Group(like, ssem.at[n], rsem.at[n])
            sent.append(group)
            return group

        def load(n, src, dst):
            cp = pltpu.make_async_copy(src, dst, lsem.at[n])
            cp.start()
            return cp

        def rows_of(d, half=None):
            if half is None:
                return pl.ds(own * d, own)
            return pl.ds(own * d + own // 2 * half, own // 2)

        def gather_start(buf):
            out = {}
            for to, slot, order in ((1, 1, (0, 1)), (3, 3, (1, 0))):
                for half in order:
                    out[slot, half] = send(
                        buf.at[rows_of(0, half)], buf.at[rows_of(slot, half)], at_y(to)
                    )
            return out

        def gather_pass(buf, cps):
            cps[1, 0].wait_recv()
            cps[2, 0] = send(buf.at[rows_of(1, 0)], buf.at[rows_of(2, 0)], at_y(1))
            cps[3, 1].wait_recv()
            cps[2, 1] = send(buf.at[rows_of(3, 1)], buf.at[rows_of(2, 1)], at_y(3))

        def gather_wait(cps, slot):
            for half in ((1,), (0, 1), (0,))[slot - 1]:
                cps[slot, half].wait_recv()

        barrier = pltpu.get_barrier_semaphore()
        peers = [mate]
        peers += [at_y(d) for d in (1, 2, 3)]
        peers += [at_x(d) for d in (1, 2, 3)]
        peers += [at_z(d) for d in range(1, 8)]
        for p in peers:
            pl.semaphore_signal(barrier, 1, device_id=p, device_id_type=MESH)

        l_proj = load(5, proj_hbm, proj_ref)
        l_count = load(6, count_hbm, count_ref)
        l_cot = load(0, cot_hbm, cot_v)
        l_feat = [
            load(10 + j, feat_hbm.at[:, pl.ds(cols * j, cols)], feat_v.at[j]) for j in range(CHUNKS)
        ]
        l_out = load(2, out_hbm, outw)
        l_in = load(3, in_hbm, inw)
        l_gain = load(7, gain_hbm, gain_ref)
        l_qkv = load(4, qkv_hbm, qkvw)

        l_proj.wait()
        l_count.wait()
        count = count_ref[0]
        own_ids = view * own + lax.broadcasted_iota(jnp.int32, (own, 1), 0)
        live = jnp.where(own_ids < count, 1.0, 0.0).astype(F32)
        proj_row = proj_ref[pl.ds(view, 1), :]
        for kk in range(2):
            par = k if kk else 1 - k
            for d in range(4):
                ids = (
                    ((c + 4 - d) % 4) * (2 * own)
                    + par * own
                    + lax.broadcasted_iota(jnp.int32, (own, patches), 0)
                )
                hot[kk, own * d : own * (d + 1), :] = jnp.where(ids == proj_row, 1.0, 0.0).astype(BF16)

        mate_cp, relay_cp, y_cp = [], [], []

        def sums(j, kk):
            return dot_nn(hot[kk], feat_v[j])

        def combine(j):
            mate_cp[j].wait_recv()
            both = pown[j] + precv[j].astype(F32)
            pown[j] = both
            far = slice(2 * own, 3 * own)
            ysend[j, far, :] = both[far, :].astype(BF16)
            relay_cp.append(
                send_all(
                    [
                        (
                            ysend.at[j, rows_of(2), pl.ds(cols // 2 * s, cols // 2)],
                            rrecv.at[j, s],
                            at_y((1, 3)[s]),
                        )
                        for s in range(2)
                    ],
                    rrecv.at[j],
                )
            )

        def forward(j):
            relay_cp[j].wait_recv()
            mid = cols // 2
            for s, d in ((0, 3), (1, 1)):
                at = slice(own * d, own * (d + 1))
                block = pown[j, at, :]
                passed = rrecv[j, s].astype(F32)
                if s == 0:
                    ysend[j, at, 0:mid] = (block[:, 0:mid] + passed).astype(BF16)
                    ysend[j, at, mid:] = block[:, mid:].astype(BF16)
                else:
                    ysend[j, at, 0:mid] = block[:, 0:mid].astype(BF16)
                    ysend[j, at, mid:] = (block[:, mid:] + passed).astype(BF16)
            y_cp.append(
                send_all(
                    [
                        (ysend.at[j, rows_of(d)], yrecv.at[j, s], at_y(4 - d))
                        for s, d in ((0, 3), (1, 1))
                    ],
                    yrecv.at[j],
                )
            )

        l_cot.wait()
        seeds[0:own, :] = (cot_v[...].astype(F32) * live * (1.0 / objects)).astype(BF16)
        l_feat[0].wait()
        psend[0] = sums(0, 0).astype(BF16)
        pl.semaphore_wait(barrier, len(peers))
        mate_cp.append(send(psend.at[0], precv.at[0], mate))
        for p in range(1, 4):
            pl.semaphore_signal(ready, 1, device_id=at_x(p), device_id_type=MESH)
        l_out.wait()
        for t in range(4):
            gsend[t] = dot_nt(seeds[0:own, :], outw[part * t : part * (t + 1), :]).astype(BF16)
        o_cp = send_all(
            [(gsend.at[(c + d) % 4], gouts.at[rows_of(d)], at_y(d)) for d in (2, 1, 3)],
            gouts.at[pl.ds(0, 3 * own)],
        )
        gouts[0:own, :] = gsend[c]
        pown[0] = sums(0, 1)
        for j in range(1, CHUNKS):
            l_feat[j].wait()
            psend[j] = sums(j, 0).astype(BF16)
            mate_cp.append(send(psend.at[j], precv.at[j], mate))
            combine(j - 1)
            pown[j] = sums(j, 1)
            if j > 1:
                forward(j - 2)
        combine(CHUNKS - 1)
        forward(CHUNKS - 2)

        number = jnp.zeros((own, 1), F32)
        for w in range(views):
            same = proj_ref[w : w + 1, :] == view * own + lax.broadcasted_iota(
                jnp.int32, (own, patches), 0
            )
            number += jnp.sum(jnp.where(same, 1.0, 0.0), axis=1, keepdims=True)
        number = jnp.maximum(number, 1.0)
        forward(CHUNKS - 1)

        l_qkv.wait()
        for t in range(3):
            window = qkvw[:, pl.ds(pl.multiple_of(width * t + 128 * ((3 * c) // 2), 128), 256)]

            @pl.when(c % 2 == 0)
            def _():
                wown[:, part * t : part * (t + 1)] = window[:, 0:part]

            @pl.when(c % 2 == 1)
            def _():
                wown[:, part * t : part * (t + 1)] = window[:, 64 : 64 + part]

        for j in range(CHUNKS):
            total = pown[j, 0:own, :]
            y_cp[j].wait_recv()
            total += yrecv[j, 0].astype(F32) + yrecv[j, 1].astype(F32)
            vox[:, cols * j : cols * (j + 1)] = (total / number).astype(BF16)
        l_in.wait()
        base_rows = dot_nn(vox[...], inw[...])
        base[...] = base_rows
        shifted = base_rows - jnp.mean(base_rows, axis=1, keepdims=True)
        spread = jnp.mean(shifted * shifted, axis=1, keepdims=True)
        inverse = lax.rsqrt(spread + 1e-06)
        unit_rows = shifted * inverse
        unit[...] = unit_rows
        l_gain.wait()
        gain = gain_ref[...].reshape(1, width)
        normed[0:own, :] = (unit_rows * gain).astype(BF16)
        n_cp = gather_start(normed)

        kv_n = used[0]
        used[0] += 1

        def share(d):
            pltpu.make_async_remote_copy(
                src_ref=kvs.at[rows_of(d)], dst_ref=kvs.at[pl.ds(group + own * d, own)],
                send_sem=ssem.at[kv_n], recv_sem=rsem.at[kv_n],
                device_id=mate, device_id_type=MESH,
            ).start()

        kv_cp = Group(kvs.at[pl.ds(0, group)], ssem.at[kv_n], rsem.at[kv_n])
        sent.append(kv_cp)

        def project(d):
            at = slice(own * d, own * (d + 1))
            packed = dot_nn(normed[at, :], wown[...])
            qs[at, :] = (packed[:, 0:part] * (HEAD_DIM**-0.5)).astype(BF16)
            kvs[at, :] = packed[:, part : 3 * part].astype(BF16)
            share(d)
            turned[:, at] = normed[at, :].T

        project(0)
        gather_pass(normed, n_cp)
        for d in (1, 3):
            gather_wait(n_cp, d)
            project(d)
        gather_wait(n_cp, 2)
        project(2)
        s_cp = gather_start(seeds)

        lane = lax.broadcasted_iota(jnp.int32, (1, own), 1)
        pieces = []
        for par in (k, 1 - k):
            for d in range(4):
                ids = ((c + 4 - d) % 4) * (2 * own) + par * own + lane
                pieces.append(jnp.where(ids < count, 0.0, NEG).astype(F32))
        bias = jnp.concatenate(pieces, axis=1)
        kv_cp.wait_recv()
        o_cp.wait_recv()

        dkv_cp, g_cp, qg_cp, t_cp = [], [], [], []

        def attend(h):
            hs = slice(HEAD_DIM * h, HEAD_DIM * (h + 1))
            keys = kvs[:, hs]
            values = kvs[:, part + HEAD_DIM * h : part + HEAD_DIM * (h + 1)]
            grad_k = jnp.zeros((slots, HEAD_DIM), F32)
            grad_v = jnp.zeros((slots, HEAD_DIM), F32)
            for b in range(group // QROWS):
                rs = slice(QROWS * b, QROWS * (b + 1))
                q = qs[rs, hs]
                go = gouts[rs, hs]
                s = dot_nt(q, keys) + bias
                e = jnp.exp(s - jnp.max(s, axis=1, keepdims=True))
                w = e * (1.0 / jnp.sum(e, axis=1, keepdims=True))
                p = w.astype(BF16)
                mixed = dot_nn(p, values)
                att[rs, hs] = mixed.astype(BF16)
                delta = jnp.sum(go.astype(F32) * mixed, axis=1, keepdims=True)
                gs = (w * (dot_nt(go, values) - delta)).astype(BF16)
                grad_q = (dot_nn(gs, keys) * (HEAD_DIM**-0.5)).astype(BF16)
                gq[h, rs, 0:HEAD_DIM] = grad_q
                gp[h, rs, 0:128] = jnp.concatenate([grad_q, mixed.astype(BF16)], axis=1)
                grad_k += dot_tn(gs, q)
                grad_v += dot_tn(p, go)
            both = jnp.concatenate([grad_k, grad_v], axis=1)
            dkv_send[h] = both[group:].astype(BF16)
            dkv_cp.append(send(dkv_send.at[h], dkv_recv.at[h], mate))
            dkv[h] = both[0:group]

        def finish(h):
            dkv_cp[h].wait_recv()
            both = dkv[h] + dkv_recv[h].astype(F32)
            both = both.astype(BF16)
            gp[h, :, 128:] = both
            gq[h, :, HEAD_DIM:] = both
            g_cp.append(
                send_all(
                    [(gp.at[h, rows_of(d)], gpr.at[c, h], at_y(4 - d)) for d in (2, 1, 3)],
                    gp.at[h, pl.ds(0, 3 * own)],
                )
            )
            gpr[c, h] = gp[h, 0:own, :]
            whole = dot_nn(turned[...], gq[h])
            for t in range(8):
                qg[h, t] = whole[orows * t : orows * (t + 1), :]
            for t in range(4):
                qg_send[h, t] = qg[h, 2 * t + (1 - k)].astype(BF16)
            qg_cp.append(send(qg_send.at[h], qg_recv.at[h], mate))

        def swap(h):
            qg_cp[h].wait_recv()
            for t in range(4):
                block = (qg[h, 2 * t + k] + qg_recv[h, t].astype(F32)).astype(BF16)
                if h < 2:
                    qsum[t, :, part * h : part * (h + 1)] = block
                else:
                    qlast[t] = block
            if h:
                buf, recv = (qsum, qrecv) if h == 1 else (qlast, qrlast)
                t_cp.append(
                    send_all(
                        [(buf.at[(c + d) % 4], recv.at[c], at_y(d)) for d in (2, 1, 3)],
                        recv.at[pl.ds(0, 3)],
                    )
                )
                recv[c] = buf[c]

        def x_scatter(h):
            return send_all(
                [(mx.at[h, (x + d) % 4], mxr.at[h, d - 1], at_x(d)) for d in (2, 1, 3)],
                mxr.at[h],
            )

        def join(h):
            for t in range(4):
                for r in range(4):
                    rows = slice(24 * r, 24 * (r + 1))
                    if h < 2:
                        block = qrecv[t, rows, part * h : part * (h + 1)]
                    else:
                        block = qrlast[t, rows, :]
                    mx[h, r, :, part * t : part * (t + 1)] = block
            mx_cp.append(x_scatter(h))

        def place(h):
            g_cp[h].wait_recv()
            for t in range(4):
                for s3, lo in ((0, 0), (1, 128), (2, 192)):
                    at = width * s3 + part * t + HEAD_DIM * h
                    gpfull[:, at : at + HEAD_DIM] = gpr[t, h, :, lo : lo + HEAD_DIM]
                at = part * t + HEAD_DIM * h
                afull[:, at : at + HEAD_DIM] = gpr[t, h, :, HEAD_DIM : 2 * HEAD_DIM]

        attend(0)
        gather_pass(seeds, s_cp)
        v_cp = send_all(
            [
                (
                    vox.at[:, pl.ds(pl.multiple_of(vcols * ((c + d) % 4), 128), vcols)],
                    vcol.at[rows_of(d)],
                    at_y(d),
                )
                for d in (1, 2, 3)
            ],
            vcol.at[pl.ds(0, 3 * own)],
        )
        vcol[0:own, :] = vox[:, pl.ds(pl.multiple_of(vcols * c, 128), vcols)]
        attend(1)
        finish(0)
        attend(2)
        finish(1)
        swap(0)
        for d in (1, 3, 2):
            gather_wait(s_cp, d)
        og[...] = dot_tn(att[...], seeds[...])
        og_send[...] = og[pl.ds(pl.multiple_of(orows * (1 - k), 32), orows), :].astype(BF16)
        og_cp = send(og_send, og_recv, mate)
        finish(2)
        swap(1)
        swap(2)
        place(0)
        place(1)
        og_cp.wait_recv()
        og_sum = (
            og[pl.ds(pl.multiple_of(orows * k, 32), orows), :] + og_recv[...].astype(F32)
        ).astype(BF16)
        for r in range(4):
            mx[3, r] = og_sum[24 * r : 24 * (r + 1), :]
        mx_cp = [x_scatter(3)]
        place(2)
        grad_unit = dot_nt(gpfull[...], qkvw[...]) * gain
        unit_rows = unit[...]
        branch_grad = inverse * (
            grad_unit
            - jnp.mean(grad_unit, axis=1, keepdims=True)
            - unit_rows * jnp.mean(grad_unit * unit_rows, axis=1, keepdims=True)
        )
        gball[0:own, :] = (seeds[0:own, :].astype(F32) + branch_grad).astype(BF16)
        b_cp = gather_start(gball)

        t_cp[0].wait_recv()
        join(0)
        join(1)
        t_cp[1].wait_recv()
        join(2)

        half = width // 2
        z_order = (4, 3, 5, 2, 6, 1, 7)

        def z_piece(buf, where):
            return buf.at[where // 2, :, pl.ds(pl.multiple_of(half * (where % 2), 128), half)]

        gather_pass(gball, b_cp)
        branch = dot_nn(afull[...], outw[...])
        latent_v[...] = (live * (base[...] + branch)).astype(BF16)
        l_latent = load(8, latent_v, latent_hbm)

        for cp in mx_cp:
            cp.wait_recv()
        for h in range(4):
            mz[h] = (
                mx[h, x].astype(F32)
                + mxr[h, 0].astype(F32)
                + mxr[h, 1].astype(F32)
                + mxr[h, 2].astype(F32)
            ).astype(BF16)
        mz_cp = send_all(
            [(z_piece(mz, (z + d) % 8), mzr.at[d - 1], at_z(d)) for d in z_order], mzr
        )
        v_cp.wait_recv()
        for d in (1, 3, 2):
            gather_wait(b_cp, d)
        ig[...] = dot_tn(vcol[...], gball[...])
        ig_send[...] = ig[pl.ds(pl.multiple_of(own * (1 - k), 128), own), :].astype(BF16)
        ig_cp = send(ig_send, ig_recv, mate)
        ig_cp.wait_recv()
        ig_sum = (
            ig[pl.ds(pl.multiple_of(own * k, 128), own), :] + ig_recv[...].astype(F32)
        ).astype(BF16)
        for r in range(16):
            for s in range(2):
                ix[2 * r + s] = ig_sum[8 * r : 8 * (r + 1), half * s : half * (s + 1)]
        pl.semaphore_wait(ready, 3)
        ix_cp = send_all(
            [(ix.at[at_o(*f)[0]], ixr.at[n], at_o(*f)) for n, f in enumerate(others)], ixr
        )

        mz_cp.wait_recv()
        total = z_piece(mz, z)[...].astype(F32)
        for d in range(7):
            total += mzr[d].astype(F32)
        mf[...] = total.astype(BF16)
        mg_cp = send_all([(mf, z_piece(mg.at[x], z), at_z(d)) for d in z_order], mzr)
        mg[x, z // 2, :, pl.ds(pl.multiple_of(half * (z % 2), 128), half)] = mf[...]
        ix_cp.wait_recv()
        total = ix[obj].astype(F32)
        for n in range(len(others)):
            total += ixr[n].astype(F32)
        jf[...] = total.astype(BF16)
        jg_cp = send_all([(jf, jg.at[obj], at_o(*f)) for f in others], ixr)
        jg[obj] = jf[...]
        mg_cp.wait_recv()
        mo_cp = send_all([(mg.at[x], mg.at[x], at_x(d)) for d in (2, 1, 3)], mg.at[pl.ds(0, 3)])
        jg_cp.wait_recv()
        l_gin = load(9, jg, gin_hbm)
        mo_cp.wait_recv()
        l_main = load(0, mg, gmain_hbm)
        for cp in sent:
            cp.wait_send()
        l_latent.wait()
        l_gin.wait()
        l_main.wait()

    scratch = [
        ((views, patches), jnp.int32), ((width,), F32), ((own, width), BF16),
        ((CHUNKS, patches, cols), BF16), ((feat, width), BF16), ((width, 3 * width), BF16),
        ((width, width), BF16), ((own, width), BF16), ((2, group, patches), BF16),
        ((CHUNKS, group, cols), BF16), ((CHUNKS, group, cols), BF16), ((CHUNKS, group, cols), F32),
        ((CHUNKS, group, cols), BF16), ((CHUNKS, 2, own, cols // 2), BF16),
        ((CHUNKS, 2, own, cols), BF16),
        ((group, width), BF16), ((own, feat), BF16), ((group, vcols), BF16),
        ((own, width), F32), ((own, width), F32), ((group, width), BF16), ((width, group), BF16),
        ((width, 3 * part), BF16), ((group, part), BF16), ((slots, 2 * part), BF16),
        ((4, own, part), BF16), ((group, part), BF16), ((group, part), BF16), ((own, width), BF16),
        ((heads, group, 128), F32), ((heads, group, 128), BF16), ((heads, group, 128), BF16),
        ((heads, group, 256), BF16), ((heads, group, part), BF16), ((4, heads, own, 256), BF16),
        ((own, 3 * width), BF16),
        ((part, width), F32), ((orows, width), BF16), ((orows, width), BF16),
        ((heads, 8, orows, part), F32), ((heads, 4, orows, part), BF16),
        ((heads, 4, orows, part), BF16),
        ((4, orows, 2 * part), BF16), ((4, orows, part), BF16),
        ((4, orows, 2 * part), BF16), ((4, orows, part), BF16),
        ((group, width), BF16), ((2 * own, width), F32), ((own, width), BF16), ((own, width), BF16),
        ((4, 4, 24, width), BF16), ((4, 3, 24, width), BF16), ((4, 24, width), BF16),
        ((7, 24, width // 2), BF16), ((24, width // 2), BF16), ((4, 4, 24, width), BF16),
        ((objects, 8, width // 2), BF16), ((objects - 1, 8, width // 2), BF16),
        ((8, width // 2), BF16), ((objects, 8, width // 2), BF16),
    ]
    return kernel, scratch


def write_out(
    latent_hbm, gin_hbm, gmain_hbm, latent_out, in_out, qkv_out, out_out,
    latent_v, gin_v, gmain_v, in_v, qkv_v, out_v, lsem, osem,
):
    width = latent_v.shape[1]
    half = width // 2
    part = width // 4
    loads = [pltpu.make_async_copy(gmain_hbm.at[r], gmain_v.at[r], lsem.at[r]) for r in range(4)]
    loads.append(pltpu.make_async_copy(gin_hbm, gin_v, lsem.at[4]))
    loads.append(pltpu.make_async_copy(latent_hbm, latent_v, lsem.at[5]))
    for cp in loads:
        cp.start()
    stores = []

    def store(src, dst):
        cp = pltpu.make_async_copy(src, dst, osem.at[len(stores)])
        cp.start()
        stores.append(cp)

    for r in range(4):
        loads[r].wait()
        at = slice(24 * r, 24 * (r + 1))
        for s in range(3):
            for t in range(4):
                for h in range(3):
                    to = width * s + part * t + HEAD_DIM * h
                    fr = part * t + HEAD_DIM * s
                    qkv_v[at, to : to + HEAD_DIM] = gmain_v[r, h, :, fr : fr + HEAD_DIM].astype(F32)
        store(qkv_v.at[pl.ds(24 * r, 24)], qkv_out.at[pl.ds(24 * r, 24)])
        out_v[at, :] = gmain_v[r, 3].astype(F32)
    store(out_v, out_out)
    loads[4].wait()
    for r in range(16):
        for s in range(2):
            in_v[8 * r : 8 * (r + 1), half * s : half * (s + 1)] = gin_v[2 * r + s].astype(F32)
    store(in_v, in_out)
    loads[5].wait()
    store(latent_v, latent_out)
    for cp in stores:
        cp.wait()


def per_device(
    features, projection, active_count, in_weight, norm_gain, qkv_weight, out_weight, cotangent
):
    patches, feat = features.shape[2:]
    own, width = cotangent.shape[1:]
    views = projection.shape[1]
    objects = lax.axis_size("obj")
    kernel, scratch = make_kernel((patches, feat, width, own, objects, views))
    hbm = pl.BlockSpec(memory_space=pl.ANY)
    latent, gin, gmain = pl.pallas_call(
        kernel,
        name="encode",
        out_shape=(
            jax.ShapeDtypeStruct((own, width), BF16),
            jax.ShapeDtypeStruct((objects, 8, width // 2), BF16),
            jax.ShapeDtypeStruct((4, 4, 24, width), BF16),
        ),
        in_specs=[hbm] * 8,
        out_specs=(hbm, hbm, hbm),
        scratch_shapes=[pltpu.VMEM(s, t) for s, t in scratch]
        + [
            pltpu.SMEM((1,), jnp.int32),
            pltpu.SemaphoreType.DMA((56,)),
            pltpu.SemaphoreType.DMA((56,)),
            pltpu.SemaphoreType.DMA((10 + CHUNKS,)),
            pltpu.SemaphoreType.REGULAR,
        ],
        compiler_params=pltpu.CompilerParams(
            collective_id=0, has_side_effects=True, vmem_limit_bytes=62 * 1024 * 1024
        ),
    )(
        features.reshape(patches, feat),
        projection.reshape(views, patches),
        active_count,
        in_weight,
        norm_gain,
        qkv_weight,
        out_weight,
        cotangent.reshape(own, width),
    )
    latent, in_grad, qkv_grad, out_grad = pl.pallas_call(
        write_out,
        name="write_out",
        out_shape=(
            jax.ShapeDtypeStruct((own, width), BF16),
            jax.ShapeDtypeStruct((own, width), F32),
            jax.ShapeDtypeStruct((96, 3 * width), F32),
            jax.ShapeDtypeStruct((96, width), F32),
        ),
        in_specs=[hbm, hbm, hbm],
        out_specs=(hbm, hbm, hbm, hbm),
        scratch_shapes=[
            pltpu.VMEM((own, width), BF16),
            pltpu.VMEM((objects, 8, width // 2), BF16),
            pltpu.VMEM((4, 4, 24, width), BF16),
            pltpu.VMEM((own, width), F32),
            pltpu.VMEM((96, 3 * width), F32),
            pltpu.VMEM((96, width), F32),
            pltpu.SemaphoreType.DMA((6,)),
            pltpu.SemaphoreType.DMA((7,)),
        ],
    )(latent, gin, gmain)
    return (latent[None], in_grad, qkv_grad, out_grad)


def solution(mesh):
    return jax.shard_map(
        per_device,
        mesh=mesh,
        in_specs=(
            P("obj", "view", None, None),
            P("obj", None, None),
            P("obj"),
            P(),
            P(),
            P(),
            P(),
            P("obj", "view", None),
        ),
        out_specs=(P("obj", "view", None), P("view", None), P("view", None), P("view", None)),
        check_vma=False,
    )
```

```python
import jax
import jax.numpy as jnp
from jax import lax
from jax.experimental import pallas as pl
from jax.experimental.pallas import tpu as pltpu
from jax.sharding import PartitionSpec as P

HEAD_DIM = 64
MESH = pl.DeviceIdType.MESH
F32 = jnp.float32
BF16 = jnp.bfloat16
NEG = -1e30
CHUNKS = 4
QROWS = 256


def dot_nn(a, b):
    return lax.dot_general(a, b, (((1,), (0,)), ((), ())), preferred_element_type=F32)


def dot_nt(a, b):
    return lax.dot_general(a, b, (((1,), (1,)), ((), ())), preferred_element_type=F32)


def dot_tn(a, b):
    return lax.dot_general(a, b, (((0,), (0,)), ((), ())), preferred_element_type=F32)


class Group:
    def __init__(self, like, send_sem, recv_sem):
        self.like, self.send_sem, self.recv_sem = like, send_sem, recv_sem

    def wait_send(self):
        pltpu.make_async_copy(self.like, self.like, self.send_sem).wait()

    def wait_recv(self):
        pltpu.make_async_copy(self.like, self.like, self.recv_sem).wait()


def make_kernel(sizes):
    patches, feat, width, own, objects, views = sizes
    chips = 4
    heads = 3
    part = heads * HEAD_DIM
    group = chips * own
    slots = 2 * group
    cols = feat // CHUNKS
    vcols = feat // chips
    orows = part // 2

    def kernel(
        feat_hbm, proj_hbm, count_hbm, in_hbm, gain_hbm, qkv_hbm, out_hbm, cot_hbm,
        latent_hbm, gin_hbm, gmain_hbm,
        proj_ref, gain_ref, latent_v, feat_v, inw, qkvw, outw, cot_v, hot, psend, precv, pown, ysend, psum, rrecv, yrecv, ylast,
        seeds, vox, vcol, base, unit, normed, turned, wown, qs, kvs, gsend, gouts, wback, att, afull,
        dkv, dkv_send, dkv_recv, gp, gq, gpr, og, og_send, og_recv,
        qg, qg_send, qg_recv, qx, qxr, qxl, qxlr, qt, qr, ox, oxr, gball, ig, ig_send, ig_recv,
        mz, mzr, mf, mg, ix, ixr, iz, izr, jf, jg,
        count_ref, ssem, rsem, lsem, ready,
    ):
        obj = lax.axis_index("obj")
        view = lax.axis_index("view")
        c = view // 2
        k = view % 2
        z = obj // 4
        x = obj % 4

        def at_y(d):
            return (obj, ((c + d) % 4) * 2 + k)

        def at_x(d):
            return (z * 4 + (x + d) % 4, view)

        def at_z(d):
            return (((z + d) % 8) * 4 + x, view)

        def at_o(dz, dx):
            return (((z + dz) % 8) * 4 + (x + dx) % 4, view)

        others = [(dz, dx) for dz in (4, 3, 5, 2, 6, 1, 7, 0) for dx in (2, 1, 3, 0) if dz or dx]
        mate = (obj, c * 2 + (1 - k))
        used = [0]
        sent = []

        def send(src, dst, device):
            n = used[0]
            used[0] += 1
            cp = pltpu.make_async_remote_copy(
                src_ref=src, dst_ref=dst, send_sem=ssem.at[n], recv_sem=rsem.at[n],
                device_id=device, device_id_type=MESH,
            )
            cp.start()
            sent.append(cp)
            return cp

        def send_all(triples, like):
            n = used[0]
            used[0] += 1
            for src, dst, device in triples:
                pltpu.make_async_remote_copy(
                    src_ref=src, dst_ref=dst, send_sem=ssem.at[n], recv_sem=rsem.at[n],
                    device_id=device, device_id_type=MESH,
                ).start()
            group = Group(like, ssem.at[n], rsem.at[n])
            sent.append(group)
            return group

        def load(n, src, dst):
            cp = pltpu.make_async_copy(src, dst, lsem.at[n])
            cp.start()
            return cp

        def rows_of(d, half=None):
            if half is None:
                return pl.ds(own * d, own)
            return pl.ds(own * d + own // 2 * half, own // 2)

        def gather_start(buf):
            out = {}
            for to, slot, order in ((1, 1, (0, 1)), (3, 3, (1, 0))):
                for half in order:
                    out[slot, half] = send(
                        buf.at[rows_of(0, half)], buf.at[rows_of(slot, half)], at_y(to)
                    )
            return out

        def gather_pass(buf, cps):
            cps[1, 0].wait_recv()
            cps[2, 0] = send(buf.at[rows_of(1, 0)], buf.at[rows_of(2, 0)], at_y(1))
            cps[3, 1].wait_recv()
            cps[2, 1] = send(buf.at[rows_of(3, 1)], buf.at[rows_of(2, 1)], at_y(3))

        def gather_wait(cps, slot):
            for half in ((1,), (0, 1), (0,))[slot - 1]:
                cps[slot, half].wait_recv()

        barrier = pltpu.get_barrier_semaphore()
        peers = [mate]
        peers += [at_y(d) for d in (1, 2, 3)]
        peers += [at_x(d) for d in (1, 2, 3)]
        peers += [at_z(d) for d in range(1, 8)]
        for p in peers:
            pl.semaphore_signal(barrier, 1, device_id=p, device_id_type=MESH)

        l_proj = load(5, proj_hbm, proj_ref)
        l_count = load(6, count_hbm, count_ref)
        l_cot = load(0, cot_hbm, cot_v)
        l_feat = [
            load(10 + j, feat_hbm.at[:, pl.ds(cols * j, cols)], feat_v.at[j]) for j in range(CHUNKS)
        ]
        l_out = load(2, out_hbm, outw)
        l_in = load(3, in_hbm, inw)
        l_gain = load(7, gain_hbm, gain_ref)
        l_qkv = load(4, qkv_hbm, qkvw)

        l_proj.wait()
        l_count.wait()
        count = count_ref[0]
        own_ids = view * own + lax.broadcasted_iota(jnp.int32, (own, 1), 0)
        live = jnp.where(own_ids < count, 1.0, 0.0).astype(F32)
        proj_row = proj_ref[pl.ds(view, 1), :]
        for kk in range(2):
            par = k if kk else 1 - k
            for d in range(4):
                ids = (
                    ((c + 4 - d) % 4) * (2 * own)
                    + par * own
                    + lax.broadcasted_iota(jnp.int32, (own, patches), 0)
                )
                hot[kk, own * d : own * (d + 1), :] = jnp.where(ids == proj_row, 1.0, 0.0).astype(BF16)

        mate_cp, relay_cp, y_cp = [], {}, {}

        def sums(j, kk):
            return dot_nn(hot[kk], feat_v[j])

        last = CHUNKS - 1

        def combine(j):
            raw = sums(j, 1)
            mate_cp[j].wait_recv()
            both = raw + precv[j].astype(F32)
            pown[j] = both[0:own, :]
            ysend[j, own:, :] = both[own:, :].astype(BF16)
            if j == last:
                y_cp[j] = send_all(
                    [(ysend.at[j, rows_of(d)], ylast.at[d - 1], at_y(4 - d)) for d in (2, 3, 1)],
                    ylast,
                )
                return
            relay_cp[j] = send_all(
                [
                    (
                        ysend.at[j, rows_of(2), pl.ds(cols // 2 * s, cols // 2)],
                        rrecv.at[j, s],
                        at_y((1, 3)[s]),
                    )
                    for s in range(2)
                ],
                rrecv.at[j],
            )
            mid = cols // 2
            psum[j, 0] = both[3 * own :, 0:mid]
            psum[j, 1] = both[own : 2 * own, mid:]

        def forward(j):
            relay_cp[j].wait_recv()
            mid = cols // 2
            for s, d in ((0, 3), (1, 1)):
                ysend[j, own * d : own * (d + 1), mid * s : mid * (s + 1)] = (
                    psum[j, s] + rrecv[j, s].astype(F32)
                ).astype(BF16)
            y_cp[j] = send_all(
                [
                    (ysend.at[j, rows_of(d)], yrecv.at[j, s], at_y(4 - d))
                    for s, d in ((0, 3), (1, 1))
                ],
                yrecv.at[j],
            )

        l_cot.wait()
        seeds[0:own, :] = (cot_v[...].astype(F32) * live * (1.0 / objects)).astype(BF16)
        l_feat[0].wait()
        psend[0] = sums(0, 0).astype(BF16)
        pl.semaphore_wait(barrier, len(peers))
        mate_cp.append(send(psend.at[0], precv.at[0], mate))
        for p in range(1, 4):
            pl.semaphore_signal(ready, 1, device_id=at_x(p), device_id_type=MESH)
        for j in range(1, CHUNKS):
            l_feat[j].wait()
            psend[j] = sums(j, 0).astype(BF16)
            mate_cp.append(send(psend.at[j], precv.at[j], mate))
            combine(j - 1)
            if j > 1:
                forward(j - 2)
        combine(last)
        forward(last - 1)

        number = jnp.zeros((own, 1), F32)
        for w in range(views):
            same = proj_ref[w : w + 1, :] == view * own + lax.broadcasted_iota(
                jnp.int32, (own, patches), 0
            )
            number += jnp.sum(jnp.where(same, 1.0, 0.0), axis=1, keepdims=True)
        number = jnp.maximum(number, 1.0)

        l_qkv.wait()
        for t in range(3):
            window = qkvw[:, pl.ds(pl.multiple_of(width * t + 128 * ((3 * c) // 2), 128), 256)]

            @pl.when(c % 2 == 0)
            def _():
                wown[:, part * t : part * (t + 1)] = window[:, 0:part]

            @pl.when(c % 2 == 1)
            def _():
                wown[:, part * t : part * (t + 1)] = window[:, 64 : 64 + part]

        for t in range(4):
            for h in range(heads):
                at = part * t + HEAD_DIM * h
                w_q = qkvw[:, at : at + HEAD_DIM]
                wback[t, h, :, 0:128] = jnp.concatenate([w_q, jnp.zeros_like(w_q)], axis=1)
                wback[t, h, :, 128:] = jnp.concatenate(
                    [qkvw[:, s * width + at : s * width + at + HEAD_DIM] for s in (1, 2)], axis=1
                )

        l_out.wait()
        for t in range(4):
            gsend[t] = dot_nt(seeds[0:own, :], outw[part * t : part * (t + 1), :]).astype(BF16)
        o_cp = send_all(
            [(gsend.at[(c + d) % 4], gouts.at[rows_of(d)], at_y(d)) for d in (2, 1, 3)],
            gouts.at[pl.ds(0, 3 * own)],
        )
        gouts[0:own, :] = gsend[c]
        for j in range(CHUNKS):
            total = pown[j]
            y_cp[j].wait_recv()
            if j == last:
                for d in range(3):
                    total += ylast[d].astype(F32)
            else:
                total += yrecv[j, 0].astype(F32) + yrecv[j, 1].astype(F32)
            vox[:, cols * j : cols * (j + 1)] = (total / number).astype(BF16)
        l_in.wait()
        base_rows = dot_nn(vox[...], inw[...])
        base[...] = base_rows
        shifted = base_rows - jnp.mean(base_rows, axis=1, keepdims=True)
        spread = jnp.mean(shifted * shifted, axis=1, keepdims=True)
        inverse = lax.rsqrt(spread + 1e-06)
        unit_rows = shifted * inverse
        unit[...] = unit_rows
        l_gain.wait()
        gain = gain_ref[...].reshape(1, width)
        normed[0:own, :] = (unit_rows * gain).astype(BF16)
        n_cp = gather_start(normed)

        kv_n = used[0]
        used[0] += 1

        def share(d):
            pltpu.make_async_remote_copy(
                src_ref=kvs.at[rows_of(d)], dst_ref=kvs.at[pl.ds(group + own * d, own)],
                send_sem=ssem.at[kv_n], recv_sem=rsem.at[kv_n],
                device_id=mate, device_id_type=MESH,
            ).start()

        kv_cp = Group(kvs.at[pl.ds(0, group)], ssem.at[kv_n], rsem.at[kv_n])
        sent.append(kv_cp)

        def project(d):
            at = slice(own * d, own * (d + 1))
            packed = dot_nn(normed[at, :], wown[...])
            qs[at, :] = (packed[:, 0:part] * (HEAD_DIM**-0.5)).astype(BF16)
            kvs[at, :] = packed[:, part : 3 * part].astype(BF16)
            share(d)
            turned[:, at] = normed[at, :].T

        project(0)
        gather_pass(normed, n_cp)
        for d in (1, 3):
            gather_wait(n_cp, d)
            project(d)
        gather_wait(n_cp, 2)
        project(2)
        s_cp = gather_start(seeds)

        lane = lax.broadcasted_iota(jnp.int32, (1, own), 1)
        pieces = []
        for par in (k, 1 - k):
            for d in range(4):
                ids = ((c + 4 - d) % 4) * (2 * own) + par * own + lane
                pieces.append(jnp.where(ids < count, 0.0, NEG).astype(F32))
        bias = jnp.concatenate(pieces, axis=1)
        kv_cp.wait_recv()
        o_cp.wait_recv()

        dkv_cp, g_cp, qg_cp, x_cp = [], [], [], []

        def attend(h):
            hs = slice(HEAD_DIM * h, HEAD_DIM * (h + 1))
            keys = kvs[:, hs]
            values = kvs[:, part + HEAD_DIM * h : part + HEAD_DIM * (h + 1)]
            grad_k = jnp.zeros((slots, HEAD_DIM), F32)
            grad_v = jnp.zeros((slots, HEAD_DIM), F32)
            for b in range(group // QROWS):
                rs = slice(QROWS * b, QROWS * (b + 1))
                q = qs[rs, hs]
                go = gouts[rs, hs]
                s = dot_nt(q, keys) + bias
                e = jnp.exp(s - jnp.max(s, axis=1, keepdims=True))
                w = e * (1.0 / jnp.sum(e, axis=1, keepdims=True))
                p = w.astype(BF16)
                mixed = dot_nn(p, values)
                att[rs, hs] = mixed.astype(BF16)
                delta = jnp.sum(go.astype(F32) * mixed, axis=1, keepdims=True)
                gs = (w * (dot_nt(go, values) - delta)).astype(BF16)
                grad_q = (dot_nn(gs, keys) * (HEAD_DIM**-0.5)).astype(BF16)
                gq[h, rs, 0:HEAD_DIM] = grad_q
                gp[h, rs, 0:128] = jnp.concatenate([grad_q, mixed.astype(BF16)], axis=1)
                grad_k += dot_tn(gs, q)
                grad_v += dot_tn(p, go)
            both = jnp.concatenate([grad_k, grad_v], axis=1)
            dkv_send[h] = both[group:].astype(BF16)
            dkv_cp.append(send(dkv_send.at[h], dkv_recv.at[h], mate))
            dkv[h] = both[0:group]

        def finish(h):
            dkv_cp[h].wait_recv()
            both = dkv[h] + dkv_recv[h].astype(F32)
            both = both.astype(BF16)
            gp[h, :, 128:] = both
            gq[h, :, HEAD_DIM:] = both
            g_cp.append(
                send_all(
                    [(gp.at[h, rows_of(d)], gpr.at[c, h], at_y(4 - d)) for d in (2, 1, 3)],
                    gp.at[h, pl.ds(0, 3 * own)],
                )
            )
            gpr[c, h] = gp[h, 0:own, :]
            whole = dot_nn(turned[...], gq[h])
            for t in range(8):
                qg[h, t] = whole[orows * t : orows * (t + 1), :]
            for t in range(4):
                qg_send[h, t] = qg[h, 2 * t + (1 - k)].astype(BF16)
            qg_cp.append(send(qg_send.at[h], qg_recv.at[h], mate))

        def swap(h):
            qg_cp[h].wait_recv()
            for t in range(4):
                block = (qg[h, 2 * t + k] + qg_recv[h, t].astype(F32)).astype(BF16)
                for r in range(4):
                    piece = block[24 * r : 24 * (r + 1), :]
                    if h < 2:
                        qx[r, t, :, part * h : part * (h + 1)] = piece
                    else:
                        qxl[r, t] = piece
            if h:
                buf, recv = (qx, qxr) if h == 1 else (qxl, qxlr)
                x_cp.append(
                    send_all(
                        [(buf.at[(x + d) % 4], recv.at[d - 1], at_x(d)) for d in (2, 1, 3)], recv
                    )
                )

        def turn():
            for n, (buf, recv) in enumerate(((qx, qxr), (qxl, qxlr))):
                x_cp[n].wait_recv()
                for t in range(4):
                    at = slice(2 * part * n, 2 * part + part * n)
                    qt[t, :, at] = (
                        buf[x, t].astype(F32)
                        + recv[0, t].astype(F32)
                        + recv[1, t].astype(F32)
                        + recv[2, t].astype(F32)
                    ).astype(BF16)
            cp = send_all(
                [(qt.at[(c + d) % 4], qr.at[c], at_y(d)) for d in (2, 1, 3)], qr.at[pl.ds(0, 3)]
            )
            qr[c] = qt[c]
            return cp

        def back(h):
            g_cp[h].wait_recv()
            total = jnp.zeros((own, width), F32)
            for t in range(4):
                at = part * t + HEAD_DIM * h
                afull[:, at : at + HEAD_DIM] = gpr[t, h, :, HEAD_DIM : 2 * HEAD_DIM]
                total += dot_nt(gpr[t, h], wback[t, h])
            return total

        attend(0)
        attend(1)
        gather_pass(seeds, s_cp)
        finish(0)
        attend(2)
        finish(1)
        swap(0)
        finish(2)
        v_cp = send_all(
            [
                (
                    vox.at[:, pl.ds(pl.multiple_of(vcols * ((c + d) % 4), 128), vcols)],
                    vcol.at[rows_of(d)],
                    at_y(d),
                )
                for d in (1, 2, 3)
            ],
            vcol.at[pl.ds(0, 3 * own)],
        )
        vcol[0:own, :] = vox[:, pl.ds(pl.multiple_of(vcols * c, 128), vcols)]
        swap(1)
        swap(2)
        early = back(0) + back(1)
        grad_unit = (early + back(2)) * gain
        unit_rows = unit[...]
        branch_grad = inverse * (
            grad_unit
            - jnp.mean(grad_unit, axis=1, keepdims=True)
            - unit_rows * jnp.mean(grad_unit * unit_rows, axis=1, keepdims=True)
        )
        gball[0:own, :] = (seeds[0:own, :].astype(F32) + branch_grad).astype(BF16)
        b_cp = gather_start(gball)

        for d in (1, 3, 2):
            gather_wait(s_cp, d)
        og[...] = dot_tn(att[...], seeds[...])
        og_send[...] = og[pl.ds(pl.multiple_of(orows * (1 - k), 32), orows), :].astype(BF16)
        og_cp = send(og_send, og_recv, mate)
        t_cp = turn()

        half = width // 2
        z_order = (4, 3, 5, 2, 6, 1, 7)

        def z_piece(buf, where):
            return buf.at[where // 2, :, pl.ds(pl.multiple_of(half * (where % 2), 128), half)]

        gather_pass(gball, b_cp)
        og_cp.wait_recv()
        og_sum = (
            og[pl.ds(pl.multiple_of(orows * k, 32), orows), :] + og_recv[...].astype(F32)
        ).astype(BF16)
        for r in range(4):
            ox[r] = og_sum[24 * r : 24 * (r + 1), :]
        ox_cp = send_all([(ox.at[(x + d) % 4], oxr.at[d - 1], at_x(d)) for d in (2, 1, 3)], oxr)
        branch = dot_nn(afull[...], outw[...])
        latent_v[...] = (live * (base[...] + branch)).astype(BF16)
        l_latent = load(8, latent_v, latent_hbm)

        ox_cp.wait_recv()
        mz[3] = (
            ox[x].astype(F32) + oxr[0].astype(F32) + oxr[1].astype(F32) + oxr[2].astype(F32)
        ).astype(BF16)
        t_cp.wait_recv()
        for h in range(heads):
            for t in range(4):
                mz[h, :, part * t : part * (t + 1)] = qr[t, :, part * h : part * (h + 1)]
        mz_cp = send_all(
            [(z_piece(mz, (z + d) % 8), mzr.at[d - 1], at_z(d)) for d in z_order], mzr
        )
        v_cp.wait_recv()
        for d in (1, 3, 2):
            gather_wait(b_cp, d)
        ig[...] = dot_tn(vcol[...], gball[...])
        ig_send[...] = ig[pl.ds(pl.multiple_of(own * (1 - k), 128), own), :].astype(BF16)
        ig_cp = send(ig_send, ig_recv, mate)
        ig_cp.wait_recv()
        ig_sum = (
            ig[pl.ds(pl.multiple_of(own * k, 128), own), :] + ig_recv[...].astype(F32)
        ).astype(BF16)
        for r in range(16):
            for s in range(2):
                p = 2 * r + s
                ix[p // 8, p % 8] = ig_sum[8 * r : 8 * (r + 1), half * s : half * (s + 1)]
        ix_cp = send_all([(ix.at[(x + d) % 4], ixr.at[d - 1], at_x(d)) for d in (2, 1, 3)], ixr)

        mz_cp.wait_recv()
        total = z_piece(mz, z)[...].astype(F32)
        for d in range(7):
            total += mzr[d].astype(F32)
        mf[...] = total.astype(BF16)
        near, far = (1, 7, 2, 6), (3, 4, 5)
        mg_cp = [
            send_all([(mf, z_piece(mg.at[x], z), at_z(d)) for d in ds], mzr.at[pl.ds(0, len(ds))])
            for ds in (near, far)
        ]
        mg[x, z // 2, :, pl.ds(pl.multiple_of(half * (z % 2), 128), half)] = mf[...]
        mo_n = used[0]
        used[0] += 1

        def spread(src, where):
            for d in (2, 1, 3):
                pltpu.make_async_remote_copy(
                    src_ref=src, dst_ref=z_piece(mg.at[x], where),
                    send_sem=ssem.at[mo_n], recv_sem=rsem.at[mo_n],
                    device_id=at_x(d), device_id_type=MESH,
                ).start()

        mo_cp = Group(mg.at[pl.ds(0, 3)], ssem.at[mo_n], rsem.at[mo_n])
        sent.append(mo_cp)
        spread(mf, z)
        ix_cp.wait_recv()
        for p in range(8):
            iz[p] = (
                ix[x, p].astype(F32)
                + ixr[0, p].astype(F32)
                + ixr[1, p].astype(F32)
                + ixr[2, p].astype(F32)
            ).astype(BF16)
        iz_cp = send_all([(iz.at[(z + d) % 8], izr.at[d - 1], at_z(d)) for d in z_order], izr)
        for cp, ds in zip(mg_cp, (near, far)):
            cp.wait_recv()
            for d in ds:
                spread(z_piece(mg.at[x], (z + 8 - d) % 8), (z + 8 - d) % 8)
        iz_cp.wait_recv()
        total = iz[z].astype(F32)
        for d in range(7):
            total += izr[d].astype(F32)
        jf[...] = total.astype(BF16)
        pl.semaphore_wait(ready, 3)
        jg_cp = send_all(
            [(jf, jg.at[x * 8 + z], at_o(*f)) for f in others], jg.at[pl.ds(0, len(others))]
        )
        jg[x * 8 + z] = jf[...]
        jg_cp.wait_recv()
        l_gin = load(9, jg, gin_hbm)
        mo_cp.wait_recv()
        l_main = load(0, mg, gmain_hbm)
        for cp in sent:
            cp.wait_send()
        l_latent.wait()
        l_gin.wait()
        l_main.wait()

    scratch = [
        ((views, patches), jnp.int32), ((width,), F32), ((own, width), BF16),
        ((CHUNKS, patches, cols), BF16), ((feat, width), BF16), ((width, 3 * width), BF16),
        ((width, width), BF16), ((own, width), BF16), ((2, group, patches), BF16),
        ((CHUNKS, group, cols), BF16), ((CHUNKS, group, cols), BF16), ((CHUNKS, own, cols), F32),
        ((CHUNKS, group, cols), BF16), ((CHUNKS - 1, 2, own, cols // 2), F32),
        ((CHUNKS - 1, 2, own, cols // 2), BF16), ((CHUNKS - 1, 2, own, cols), BF16),
        ((3, own, cols), BF16),
        ((group, width), BF16), ((own, feat), BF16), ((group, vcols), BF16),
        ((own, width), F32), ((own, width), F32), ((group, width), BF16), ((width, group), BF16),
        ((width, 3 * part), BF16), ((group, part), BF16), ((slots, 2 * part), BF16),
        ((4, own, part), BF16), ((group, part), BF16), ((4, heads, width, 256), BF16),
        ((group, part), BF16), ((own, width), BF16),
        ((heads, group, 128), F32), ((heads, group, 128), BF16), ((heads, group, 128), BF16),
        ((heads, group, 256), BF16), ((heads, group, part), BF16), ((4, heads, own, 256), BF16),
        ((part, width), F32), ((orows, width), BF16), ((orows, width), BF16),
        ((heads, 8, orows, part), F32), ((heads, 4, orows, part), BF16),
        ((heads, 4, orows, part), BF16),
        ((4, 4, 24, 2 * part), BF16), ((3, 4, 24, 2 * part), BF16),
        ((4, 4, 24, part), BF16), ((3, 4, 24, part), BF16),
        ((4, 24, 3 * part), BF16), ((4, 24, 3 * part), BF16),
        ((4, 24, width), BF16), ((3, 24, width), BF16),
        ((group, width), BF16), ((2 * own, width), F32), ((own, width), BF16), ((own, width), BF16),
        ((4, 24, width), BF16),
        ((7, 24, width // 2), BF16), ((24, width // 2), BF16), ((4, 4, 24, width), BF16),
        ((4, 8, 8, width // 2), BF16), ((3, 8, 8, width // 2), BF16),
        ((8, 8, width // 2), BF16), ((7, 8, width // 2), BF16),
        ((8, width // 2), BF16), ((objects, 8, width // 2), BF16),
    ]
    return kernel, scratch


def write_out(
    latent_hbm, gin_hbm, gmain_hbm, latent_out, in_out, qkv_out, out_out,
    latent_v, gin_v, gmain_v, in_v, qkv_v, out_v, lsem, osem,
):
    width = latent_v.shape[1]
    half = width // 2
    part = width // 4
    loads = [pltpu.make_async_copy(gmain_hbm.at[r], gmain_v.at[r], lsem.at[r]) for r in range(4)]
    loads.append(pltpu.make_async_copy(gin_hbm, gin_v, lsem.at[4]))
    loads.append(pltpu.make_async_copy(latent_hbm, latent_v, lsem.at[5]))
    for cp in loads:
        cp.start()
    stores = []

    def store(src, dst):
        cp = pltpu.make_async_copy(src, dst, osem.at[len(stores)])
        cp.start()
        stores.append(cp)

    for r in range(4):
        loads[r].wait()
        at = slice(24 * r, 24 * (r + 1))
        for s in range(3):
            for t in range(4):
                for h in range(3):
                    to = width * s + part * t + HEAD_DIM * h
                    fr = part * t + HEAD_DIM * s
                    qkv_v[at, to : to + HEAD_DIM] = gmain_v[r, h, :, fr : fr + HEAD_DIM].astype(F32)
        store(qkv_v.at[pl.ds(24 * r, 24)], qkv_out.at[pl.ds(24 * r, 24)])
        out_v[at, :] = gmain_v[r, 3].astype(F32)
    store(out_v, out_out)
    loads[4].wait()
    for r in range(16):
        for s in range(2):
            in_v[8 * r : 8 * (r + 1), half * s : half * (s + 1)] = gin_v[2 * r + s].astype(F32)
    store(in_v, in_out)
    loads[5].wait()
    store(latent_v, latent_out)
    for cp in stores:
        cp.wait()


def per_device(
    features, projection, active_count, in_weight, norm_gain, qkv_weight, out_weight, cotangent
):
    patches, feat = features.shape[2:]
    own, width = cotangent.shape[1:]
    views = projection.shape[1]
    objects = lax.axis_size("obj")
    kernel, scratch = make_kernel((patches, feat, width, own, objects, views))
    hbm = pl.BlockSpec(memory_space=pl.ANY)
    latent, gin, gmain = pl.pallas_call(
        kernel,
        name="encode",
        out_shape=(
            jax.ShapeDtypeStruct((own, width), BF16),
            jax.ShapeDtypeStruct((objects, 8, width // 2), BF16),
            jax.ShapeDtypeStruct((4, 4, 24, width), BF16),
        ),
        in_specs=[hbm] * 8,
        out_specs=(hbm, hbm, hbm),
        scratch_shapes=[pltpu.VMEM(s, t) for s, t in scratch]
        + [
            pltpu.SMEM((1,), jnp.int32),
            pltpu.SemaphoreType.DMA((56,)),
            pltpu.SemaphoreType.DMA((56,)),
            pltpu.SemaphoreType.DMA((10 + CHUNKS,)),
            pltpu.SemaphoreType.REGULAR,
        ],
        compiler_params=pltpu.CompilerParams(
            collective_id=0, has_side_effects=True, vmem_limit_bytes=62 * 1024 * 1024
        ),
    )(
        features.reshape(patches, feat),
        projection.reshape(views, patches),
        active_count,
        in_weight,
        norm_gain,
        qkv_weight,
        out_weight,
        cotangent.reshape(own, width),
    )
    latent, in_grad, qkv_grad, out_grad = pl.pallas_call(
        write_out,
        name="write_out",
        out_shape=(
            jax.ShapeDtypeStruct((own, width), BF16),
            jax.ShapeDtypeStruct((own, width), F32),
            jax.ShapeDtypeStruct((96, 3 * width), F32),
            jax.ShapeDtypeStruct((96, width), F32),
        ),
        in_specs=[hbm, hbm, hbm],
        out_specs=(hbm, hbm, hbm, hbm),
        scratch_shapes=[
            pltpu.VMEM((own, width), BF16),
            pltpu.VMEM((objects, 8, width // 2), BF16),
            pltpu.VMEM((4, 4, 24, width), BF16),
            pltpu.VMEM((own, width), F32),
            pltpu.VMEM((96, 3 * width), F32),
            pltpu.VMEM((96, width), F32),
            pltpu.SemaphoreType.DMA((6,)),
            pltpu.SemaphoreType.DMA((7,)),
        ],
    )(latent, gin, gmain)
    return (latent[None], in_grad, qkv_grad, out_grad)


def solution(mesh):
    return jax.shard_map(
        per_device,
        mesh=mesh,
        in_specs=(
            P("obj", "view", None, None),
            P("obj", None, None),
            P("obj"),
            P(),
            P(),
            P(),
            P(),
            P("obj", "view", None),
        ),
        out_specs=(P("obj", "view", None), P("view", None), P("view", None), P("view", None)),
        check_vma=False,
    )
```

```python
import jax
import jax.numpy as jnp
from jax import lax
from jax.experimental import pallas as pl
from jax.experimental.pallas import tpu as pltpu
from jax.sharding import PartitionSpec as P

HEAD_DIM = 64
MESH = pl.DeviceIdType.MESH
F32 = jnp.float32
BF16 = jnp.bfloat16
NEG = -1e30
CHUNKS = 4
QROWS = 256


def dot_nn(a, b):
    return lax.dot_general(a, b, (((1,), (0,)), ((), ())), preferred_element_type=F32)


def dot_nt(a, b):
    return lax.dot_general(a, b, (((1,), (1,)), ((), ())), preferred_element_type=F32)


def dot_tn(a, b):
    return lax.dot_general(a, b, (((0,), (0,)), ((), ())), preferred_element_type=F32)


class Group:
    def __init__(self, like, send_sem, recv_sem):
        self.like, self.send_sem, self.recv_sem = like, send_sem, recv_sem

    def wait_send(self):
        pltpu.make_async_copy(self.like, self.like, self.send_sem).wait()

    def wait_recv(self):
        pltpu.make_async_copy(self.like, self.like, self.recv_sem).wait()


def make_kernel(sizes):
    patches, feat, width, own, objects, views = sizes
    chips = 4
    heads = 3
    part = heads * HEAD_DIM
    group = chips * own
    slots = 2 * group
    cols = feat // CHUNKS
    vcols = feat // chips
    orows = part // 2

    def kernel(
        feat_hbm, proj_hbm, count_hbm, in_hbm, gain_hbm, qkv_hbm, out_hbm, cot_hbm,
        latent_hbm, gin_hbm, gmain_hbm,
        proj_ref, gain_ref, latent_v, feat_v, inw, qkvw, outw, cot_v, hot, psend, precv, pown, ysend, psum, rrecv, yrecv, ylast,
        seeds, vox, vcol, base, unit, normed, turned, wown, qs, kvs, gouts, wback, att, afull,
        dkv, dkv_send, dkv_recv, gp, gq, gpr, og, og_send, og_recv,
        qg, qg_send, qg_recv, qx, qxr, qxl, qxlr, qt, qr, ox, oxr, gball, ig, ig_send, ig_recv,
        mz, mzr, mf, mg, ix, ixr, iz, izr, jf, jg,
        count_ref, ssem, rsem, lsem, ready,
    ):
        obj = lax.axis_index("obj")
        view = lax.axis_index("view")
        c = view // 2
        k = view % 2
        z = obj // 4
        x = obj % 4

        def at_y(d):
            return (obj, ((c + d) % 4) * 2 + k)

        def at_x(d):
            return (z * 4 + (x + d) % 4, view)

        def at_z(d):
            return (((z + d) % 8) * 4 + x, view)

        def at_o(dz, dx):
            return (((z + dz) % 8) * 4 + (x + dx) % 4, view)

        others = [(dz, dx) for dz in (4, 3, 5, 2, 6, 1, 7, 0) for dx in (2, 1, 3, 0) if dz or dx]
        mate = (obj, c * 2 + (1 - k))
        used = [0]
        sent = []

        def send(src, dst, device):
            n = used[0]
            used[0] += 1
            cp = pltpu.make_async_remote_copy(
                src_ref=src, dst_ref=dst, send_sem=ssem.at[n], recv_sem=rsem.at[n],
                device_id=device, device_id_type=MESH,
            )
            cp.start()
            sent.append(cp)
            return cp

        def send_all(triples, like):
            n = used[0]
            used[0] += 1
            for src, dst, device in triples:
                pltpu.make_async_remote_copy(
                    src_ref=src, dst_ref=dst, send_sem=ssem.at[n], recv_sem=rsem.at[n],
                    device_id=device, device_id_type=MESH,
                ).start()
            group = Group(like, ssem.at[n], rsem.at[n])
            sent.append(group)
            return group

        def load(n, src, dst):
            cp = pltpu.make_async_copy(src, dst, lsem.at[n])
            cp.start()
            return cp

        def rows_of(d, half=None):
            if half is None:
                return pl.ds(own * d, own)
            return pl.ds(own * d + own // 2 * half, own // 2)

        def gather_start(buf):
            out = {}
            for to, slot, order in ((1, 1, (0, 1)), (3, 3, (1, 0))):
                for half in order:
                    out[slot, half] = send(
                        buf.at[rows_of(0, half)], buf.at[rows_of(slot, half)], at_y(to)
                    )
            return out

        def gather_pass(buf, cps):
            cps[1, 0].wait_recv()
            cps[2, 0] = send(buf.at[rows_of(1, 0)], buf.at[rows_of(2, 0)], at_y(1))
            cps[3, 1].wait_recv()
            cps[2, 1] = send(buf.at[rows_of(3, 1)], buf.at[rows_of(2, 1)], at_y(3))

        def gather_wait(cps, slot):
            for half in ((1,), (0, 1), (0,))[slot - 1]:
                cps[slot, half].wait_recv()

        barrier = pltpu.get_barrier_semaphore()
        peers = [mate]
        peers += [at_y(d) for d in (1, 2, 3)]
        peers += [at_x(d) for d in (1, 2, 3)]
        peers += [at_z(d) for d in range(1, 8)]
        for p in peers:
            pl.semaphore_signal(barrier, 1, device_id=p, device_id_type=MESH)

        l_proj = load(5, proj_hbm, proj_ref)
        l_count = load(6, count_hbm, count_ref)
        l_cot = load(0, cot_hbm, cot_v)
        l_feat = [
            load(10 + j, feat_hbm.at[:, pl.ds(cols * j, cols)], feat_v.at[j]) for j in range(CHUNKS)
        ]
        l_out = load(2, out_hbm, outw)
        l_in = load(3, in_hbm, inw)
        l_gain = load(7, gain_hbm, gain_ref)
        l_qkv = load(4, qkv_hbm, qkvw)

        l_proj.wait()
        l_count.wait()
        count = count_ref[0]
        own_ids = view * own + lax.broadcasted_iota(jnp.int32, (own, 1), 0)
        live = jnp.where(own_ids < count, 1.0, 0.0).astype(F32)
        proj_row = proj_ref[pl.ds(view, 1), :]
        for kk in range(2):
            par = k if kk else 1 - k
            for d in range(4):
                ids = (
                    ((c + 4 - d) % 4) * (2 * own)
                    + par * own
                    + lax.broadcasted_iota(jnp.int32, (own, patches), 0)
                )
                hot[kk, own * d : own * (d + 1), :] = jnp.where(ids == proj_row, 1.0, 0.0).astype(BF16)

        mate_cp, relay_cp, y_cp = [], {}, {}

        def sums(j, kk):
            return dot_nn(hot[kk], feat_v[j])

        last = CHUNKS - 1

        def combine(j):
            raw = sums(j, 1)
            mate_cp[j].wait_recv()
            both = raw + precv[j].astype(F32)
            pown[j] = both[0:own, :]
            ysend[j, own:, :] = both[own:, :].astype(BF16)
            if j == last:
                y_cp[j] = send_all(
                    [(ysend.at[j, rows_of(d)], ylast.at[d - 1], at_y(4 - d)) for d in (2, 3, 1)],
                    ylast,
                )
                return
            relay_cp[j] = send_all(
                [
                    (
                        ysend.at[j, rows_of(2), pl.ds(cols // 2 * s, cols // 2)],
                        rrecv.at[j, s],
                        at_y((1, 3)[s]),
                    )
                    for s in range(2)
                ],
                rrecv.at[j],
            )
            mid = cols // 2
            psum[j, 0] = both[3 * own :, 0:mid]
            psum[j, 1] = both[own : 2 * own, mid:]

        def forward(j):
            relay_cp[j].wait_recv()
            mid = cols // 2
            for s, d in ((0, 3), (1, 1)):
                ysend[j, own * d : own * (d + 1), mid * s : mid * (s + 1)] = (
                    psum[j, s] + rrecv[j, s].astype(F32)
                ).astype(BF16)
            y_cp[j] = send_all(
                [
                    (ysend.at[j, rows_of(d)], yrecv.at[j, s], at_y(4 - d))
                    for s, d in ((0, 3), (1, 1))
                ],
                yrecv.at[j],
            )

        l_cot.wait()
        seeds[0:own, :] = (cot_v[...].astype(F32) * live * (1.0 / objects)).astype(BF16)
        l_feat[0].wait()
        psend[0] = sums(0, 0).astype(BF16)
        pl.semaphore_wait(barrier, len(peers))
        mate_cp.append(send(psend.at[0], precv.at[0], mate))
        for p in range(1, 4):
            pl.semaphore_signal(ready, 1, device_id=at_x(p), device_id_type=MESH)
        s_cp = gather_start(seeds)
        for j in range(1, CHUNKS):
            l_feat[j].wait()
            psend[j] = sums(j, 0).astype(BF16)
            mate_cp.append(send(psend.at[j], precv.at[j], mate))
            combine(j - 1)
            if j == 2:
                gather_pass(seeds, s_cp)
            if j > 1:
                forward(j - 2)
        combine(last)
        forward(last - 1)

        number = jnp.zeros((own, 1), F32)
        for w in range(views):
            same = proj_ref[w : w + 1, :] == view * own + lax.broadcasted_iota(
                jnp.int32, (own, patches), 0
            )
            number += jnp.sum(jnp.where(same, 1.0, 0.0), axis=1, keepdims=True)
        number = jnp.maximum(number, 1.0)

        l_qkv.wait()
        for t in range(3):
            window = qkvw[:, pl.ds(pl.multiple_of(width * t + 128 * ((3 * c) // 2), 128), 256)]

            @pl.when(c % 2 == 0)
            def _():
                wown[:, part * t : part * (t + 1)] = window[:, 0:part]

            @pl.when(c % 2 == 1)
            def _():
                wown[:, part * t : part * (t + 1)] = window[:, 64 : 64 + part]

        for t in range(4):
            for h in range(heads):
                at = part * t + HEAD_DIM * h
                w_q = qkvw[:, at : at + HEAD_DIM]
                wback[t, h, :, 0:128] = jnp.concatenate([w_q, jnp.zeros_like(w_q)], axis=1)
                wback[t, h, :, 128:] = jnp.concatenate(
                    [qkvw[:, s * width + at : s * width + at + HEAD_DIM] for s in (1, 2)], axis=1
                )

        l_out.wait()
        rows = outw[pl.ds(pl.multiple_of(part * c, 64), part), :]

        def pull(d):
            at = slice(own * d, own * (d + 1))
            if d:
                gather_wait(s_cp, d)
            gouts[at, :] = dot_nt(seeds[at, :], rows).astype(BF16)

        for d in (0, 1, 3):
            pull(d)
        for j in range(CHUNKS):
            total = pown[j]
            y_cp[j].wait_recv()
            if j == last:
                for d in range(3):
                    total += ylast[d].astype(F32)
            else:
                total += yrecv[j, 0].astype(F32) + yrecv[j, 1].astype(F32)
            vox[:, cols * j : cols * (j + 1)] = (total / number).astype(BF16)
        l_in.wait()
        base_rows = dot_nn(vox[...], inw[...])
        base[...] = base_rows
        shifted = base_rows - jnp.mean(base_rows, axis=1, keepdims=True)
        spread = jnp.mean(shifted * shifted, axis=1, keepdims=True)
        inverse = lax.rsqrt(spread + 1e-06)
        unit_rows = shifted * inverse
        unit[...] = unit_rows
        l_gain.wait()
        gain = gain_ref[...].reshape(1, width)
        normed[0:own, :] = (unit_rows * gain).astype(BF16)
        n_cp = gather_start(normed)

        kv_n = used[0]
        used[0] += 1

        def share(d):
            pltpu.make_async_remote_copy(
                src_ref=kvs.at[rows_of(d)], dst_ref=kvs.at[pl.ds(group + own * d, own)],
                send_sem=ssem.at[kv_n], recv_sem=rsem.at[kv_n],
                device_id=mate, device_id_type=MESH,
            ).start()

        kv_cp = Group(kvs.at[pl.ds(0, group)], ssem.at[kv_n], rsem.at[kv_n])
        sent.append(kv_cp)

        def project(d):
            at = slice(own * d, own * (d + 1))
            packed = dot_nn(normed[at, :], wown[...])
            qs[at, :] = (packed[:, 0:part] * (HEAD_DIM**-0.5)).astype(BF16)
            kvs[at, :] = packed[:, part : 3 * part].astype(BF16)
            share(d)
            turned[:, at] = normed[at, :].T

        project(0)
        gather_pass(normed, n_cp)
        pull(2)
        for d in (1, 3):
            gather_wait(n_cp, d)
            project(d)
        gather_wait(n_cp, 2)
        project(2)
        v_cp = send_all(
            [
                (
                    vox.at[:, pl.ds(pl.multiple_of(vcols * ((c + d) % 4), 128), vcols)],
                    vcol.at[rows_of(d)],
                    at_y(d),
                )
                for d in (1, 2, 3)
            ],
            vcol.at[pl.ds(0, 3 * own)],
        )
        vcol[0:own, :] = vox[:, pl.ds(pl.multiple_of(vcols * c, 128), vcols)]

        lane = lax.broadcasted_iota(jnp.int32, (1, own), 1)
        pieces = []
        for par in (k, 1 - k):
            for d in range(4):
                ids = ((c + 4 - d) % 4) * (2 * own) + par * own + lane
                pieces.append(jnp.where(ids < count, 0.0, NEG).astype(F32))
        bias = jnp.concatenate(pieces, axis=1)
        kv_cp.wait_recv()

        dkv_cp, g_cp, qg_cp, x_cp = [], [], [], []

        def attend(h):
            hs = slice(HEAD_DIM * h, HEAD_DIM * (h + 1))
            keys = kvs[:, hs]
            values = kvs[:, part + HEAD_DIM * h : part + HEAD_DIM * (h + 1)]
            grad_k = jnp.zeros((slots, HEAD_DIM), F32)
            grad_v = jnp.zeros((slots, HEAD_DIM), F32)
            for b in range(group // QROWS):
                rs = slice(QROWS * b, QROWS * (b + 1))
                q = qs[rs, hs]
                go = gouts[rs, hs]
                s = dot_nt(q, keys) + bias
                e = jnp.exp(s - jnp.max(s, axis=1, keepdims=True))
                w = e * (1.0 / jnp.sum(e, axis=1, keepdims=True))
                p = w.astype(BF16)
                mixed = dot_nn(p, values)
                att[rs, hs] = mixed.astype(BF16)
                delta = jnp.sum(go.astype(F32) * mixed, axis=1, keepdims=True)
                gs = (w * (dot_nt(go, values) - delta)).astype(BF16)
                grad_q = (dot_nn(gs, keys) * (HEAD_DIM**-0.5)).astype(BF16)
                gq[h, rs, 0:HEAD_DIM] = grad_q
                gp[h, rs, 0:128] = jnp.concatenate([grad_q, mixed.astype(BF16)], axis=1)
                grad_k += dot_tn(gs, q)
                grad_v += dot_tn(p, go)
            both = jnp.concatenate([grad_k, grad_v], axis=1)
            dkv_send[h] = both[group:].astype(BF16)
            dkv_cp.append(send(dkv_send.at[h], dkv_recv.at[h], mate))
            dkv[h] = both[0:group]

        def finish(h):
            dkv_cp[h].wait_recv()
            both = dkv[h] + dkv_recv[h].astype(F32)
            both = both.astype(BF16)
            gp[h, :, 128:] = both
            gq[h, :, HEAD_DIM:] = both
            g_cp.append(
                send_all(
                    [(gp.at[h, rows_of(d)], gpr.at[c, h], at_y(4 - d)) for d in (2, 1, 3)],
                    gp.at[h, pl.ds(0, 3 * own)],
                )
            )
            gpr[c, h] = gp[h, 0:own, :]
            whole = dot_nn(turned[...], gq[h])
            for t in range(8):
                qg[h, t] = whole[orows * t : orows * (t + 1), :]
            for t in range(4):
                qg_send[h, t] = qg[h, 2 * t + (1 - k)].astype(BF16)
            qg_cp.append(send(qg_send.at[h], qg_recv.at[h], mate))

        def swap(h):
            qg_cp[h].wait_recv()
            for t in range(4):
                block = (qg[h, 2 * t + k] + qg_recv[h, t].astype(F32)).astype(BF16)
                for r in range(4):
                    piece = block[24 * r : 24 * (r + 1), :]
                    if h < 2:
                        qx[r, t, :, part * h : part * (h + 1)] = piece
                    else:
                        qxl[r, t] = piece
            if h:
                buf, recv = (qx, qxr) if h == 1 else (qxl, qxlr)
                x_cp.append(
                    send_all(
                        [(buf.at[(x + d) % 4], recv.at[d - 1], at_x(d)) for d in (2, 1, 3)], recv
                    )
                )

        def turn():
            for n, (buf, recv) in enumerate(((qx, qxr), (qxl, qxlr))):
                x_cp[n].wait_recv()
                for t in range(4):
                    at = slice(2 * part * n, 2 * part + part * n)
                    qt[t, :, at] = (
                        buf[x, t].astype(F32)
                        + recv[0, t].astype(F32)
                        + recv[1, t].astype(F32)
                        + recv[2, t].astype(F32)
                    ).astype(BF16)
            cp = send_all(
                [(qt.at[(c + d) % 4], qr.at[c], at_y(d)) for d in (2, 1, 3)], qr.at[pl.ds(0, 3)]
            )
            qr[c] = qt[c]
            return cp

        def back(h):
            g_cp[h].wait_recv()
            total = jnp.zeros((own, width), F32)
            for t in range(4):
                at = part * t + HEAD_DIM * h
                afull[:, at : at + HEAD_DIM] = gpr[t, h, :, HEAD_DIM : 2 * HEAD_DIM]
                total += dot_nt(gpr[t, h], wback[t, h])
            return total

        attend(0)
        attend(1)
        finish(0)
        attend(2)
        finish(1)
        swap(0)
        og[...] = dot_tn(att[...], seeds[...])
        og_send[...] = og[pl.ds(pl.multiple_of(orows * (1 - k), 32), orows), :].astype(BF16)
        og_cp = send(og_send, og_recv, mate)
        finish(2)
        swap(1)
        swap(2)
        og_cp.wait_recv()
        og_sum = (
            og[pl.ds(pl.multiple_of(orows * k, 32), orows), :] + og_recv[...].astype(F32)
        ).astype(BF16)
        for r in range(4):
            ox[r] = og_sum[24 * r : 24 * (r + 1), :]
        ox_cp = send_all([(ox.at[(x + d) % 4], oxr.at[d - 1], at_x(d)) for d in (2, 1, 3)], oxr)
        early = back(0) + back(1)
        grad_unit = (early + back(2)) * gain
        unit_rows = unit[...]
        branch_grad = inverse * (
            grad_unit
            - jnp.mean(grad_unit, axis=1, keepdims=True)
            - unit_rows * jnp.mean(grad_unit * unit_rows, axis=1, keepdims=True)
        )
        gball[0:own, :] = (seeds[0:own, :].astype(F32) + branch_grad).astype(BF16)
        b_cp = gather_start(gball)

        t_cp = turn()

        half = width // 2
        z_order = (4, 3, 5, 2, 6, 1, 7)

        def z_piece(buf, where):
            return buf.at[where // 2, :, pl.ds(pl.multiple_of(half * (where % 2), 128), half)]

        gather_pass(gball, b_cp)
        branch = dot_nn(afull[...], outw[...])
        latent_v[...] = (live * (base[...] + branch)).astype(BF16)
        l_latent = load(8, latent_v, latent_hbm)

        ox_cp.wait_recv()
        mz[3] = (
            ox[x].astype(F32) + oxr[0].astype(F32) + oxr[1].astype(F32) + oxr[2].astype(F32)
        ).astype(BF16)
        t_cp.wait_recv()
        for h in range(heads):
            for t in range(4):
                mz[h, :, part * t : part * (t + 1)] = qr[t, :, part * h : part * (h + 1)]
        mz_cp = send_all(
            [(z_piece(mz, (z + d) % 8), mzr.at[d - 1], at_z(d)) for d in z_order], mzr
        )
        v_cp.wait_recv()
        for d in (1, 3, 2):
            gather_wait(b_cp, d)
        ig[...] = dot_tn(vcol[...], gball[...])
        ig_send[...] = ig[pl.ds(pl.multiple_of(own * (1 - k), 128), own), :].astype(BF16)
        ig_cp = send(ig_send, ig_recv, mate)
        ig_cp.wait_recv()
        ig_sum = (
            ig[pl.ds(pl.multiple_of(own * k, 128), own), :] + ig_recv[...].astype(F32)
        ).astype(BF16)
        for r in range(16):
            for s in range(2):
                p = 2 * r + s
                ix[p // 8, p % 8] = ig_sum[8 * r : 8 * (r + 1), half * s : half * (s + 1)]
        ix_cp = send_all([(ix.at[(x + d) % 4], ixr.at[d - 1], at_x(d)) for d in (2, 1, 3)], ixr)

        mz_cp.wait_recv()
        total = z_piece(mz, z)[...].astype(F32)
        for d in range(7):
            total += mzr[d].astype(F32)
        mf[...] = total.astype(BF16)
        near, far = (1, 7, 2, 6), (3, 4, 5)
        mg_cp = [
            send_all([(mf, z_piece(mg.at[x], z), at_z(d)) for d in ds], mzr.at[pl.ds(0, len(ds))])
            for ds in (near, far)
        ]
        mg[x, z // 2, :, pl.ds(pl.multiple_of(half * (z % 2), 128), half)] = mf[...]
        mo_n = used[0]
        used[0] += 1

        def spread(src, where):
            for d in (2, 1, 3):
                pltpu.make_async_remote_copy(
                    src_ref=src, dst_ref=z_piece(mg.at[x], where),
                    send_sem=ssem.at[mo_n], recv_sem=rsem.at[mo_n],
                    device_id=at_x(d), device_id_type=MESH,
                ).start()

        mo_cp = Group(mg.at[pl.ds(0, 3)], ssem.at[mo_n], rsem.at[mo_n])
        sent.append(mo_cp)
        spread(mf, z)
        ix_cp.wait_recv()
        for p in range(8):
            iz[p] = (
                ix[x, p].astype(F32)
                + ixr[0, p].astype(F32)
                + ixr[1, p].astype(F32)
                + ixr[2, p].astype(F32)
            ).astype(BF16)
        iz_cp = send_all([(iz.at[(z + d) % 8], izr.at[d - 1], at_z(d)) for d in z_order], izr)
        for cp, ds in zip(mg_cp, (near, far)):
            cp.wait_recv()
            for d in ds:
                spread(z_piece(mg.at[x], (z + 8 - d) % 8), (z + 8 - d) % 8)
        iz_cp.wait_recv()
        total = iz[z].astype(F32)
        for d in range(7):
            total += izr[d].astype(F32)
        jf[...] = total.astype(BF16)
        pl.semaphore_wait(ready, 3)
        jg_cp = send_all(
            [(jf, jg.at[x * 8 + z], at_o(*f)) for f in others], jg.at[pl.ds(0, len(others))]
        )
        jg[x * 8 + z] = jf[...]
        jg_cp.wait_recv()
        l_gin = load(9, jg, gin_hbm)
        mo_cp.wait_recv()
        l_main = load(0, mg, gmain_hbm)
        for cp in sent:
            cp.wait_send()
        l_latent.wait()
        l_gin.wait()
        l_main.wait()

    scratch = [
        ((views, patches), jnp.int32), ((width,), F32), ((own, width), BF16),
        ((CHUNKS, patches, cols), BF16), ((feat, width), BF16), ((width, 3 * width), BF16),
        ((width, width), BF16), ((own, width), BF16), ((2, group, patches), BF16),
        ((CHUNKS, group, cols), BF16), ((CHUNKS, group, cols), BF16), ((CHUNKS, own, cols), F32),
        ((CHUNKS, group, cols), BF16), ((CHUNKS - 1, 2, own, cols // 2), F32),
        ((CHUNKS - 1, 2, own, cols // 2), BF16), ((CHUNKS - 1, 2, own, cols), BF16),
        ((3, own, cols), BF16),
        ((group, width), BF16), ((own, feat), BF16), ((group, vcols), BF16),
        ((own, width), F32), ((own, width), F32), ((group, width), BF16), ((width, group), BF16),
        ((width, 3 * part), BF16), ((group, part), BF16), ((slots, 2 * part), BF16),
        ((group, part), BF16), ((4, heads, width, 256), BF16),
        ((group, part), BF16), ((own, width), BF16),
        ((heads, group, 128), F32), ((heads, group, 128), BF16), ((heads, group, 128), BF16),
        ((heads, group, 256), BF16), ((heads, group, part), BF16), ((4, heads, own, 256), BF16),
        ((part, width), F32), ((orows, width), BF16), ((orows, width), BF16),
        ((heads, 8, orows, part), F32), ((heads, 4, orows, part), BF16),
        ((heads, 4, orows, part), BF16),
        ((4, 4, 24, 2 * part), BF16), ((3, 4, 24, 2 * part), BF16),
        ((4, 4, 24, part), BF16), ((3, 4, 24, part), BF16),
        ((4, 24, 3 * part), BF16), ((4, 24, 3 * part), BF16),
        ((4, 24, width), BF16), ((3, 24, width), BF16),
        ((group, width), BF16), ((2 * own, width), F32), ((own, width), BF16), ((own, width), BF16),
        ((4, 24, width), BF16),
        ((7, 24, width // 2), BF16), ((24, width // 2), BF16), ((4, 4, 24, width), BF16),
        ((4, 8, 8, width // 2), BF16), ((3, 8, 8, width // 2), BF16),
        ((8, 8, width // 2), BF16), ((7, 8, width // 2), BF16),
        ((8, width // 2), BF16), ((objects, 8, width // 2), BF16),
    ]
    return kernel, scratch


def write_out(
    latent_hbm, gin_hbm, gmain_hbm, latent_out, in_out, qkv_out, out_out,
    latent_v, gin_v, gmain_v, in_v, qkv_v, out_v, lsem, osem,
):
    width = latent_v.shape[1]
    half = width // 2
    part = width // 4
    loads = [pltpu.make_async_copy(gmain_hbm.at[r], gmain_v.at[r], lsem.at[r]) for r in range(4)]
    loads.append(pltpu.make_async_copy(gin_hbm, gin_v, lsem.at[4]))
    loads.append(pltpu.make_async_copy(latent_hbm, latent_v, lsem.at[5]))
    for cp in loads:
        cp.start()
    stores = []

    def store(src, dst):
        cp = pltpu.make_async_copy(src, dst, osem.at[len(stores)])
        cp.start()
        stores.append(cp)

    for r in range(4):
        loads[r].wait()
        at = slice(24 * r, 24 * (r + 1))
        for s in range(3):
            for t in range(4):
                for h in range(3):
                    to = width * s + part * t + HEAD_DIM * h
                    fr = part * t + HEAD_DIM * s
                    qkv_v[at, to : to + HEAD_DIM] = gmain_v[r, h, :, fr : fr + HEAD_DIM].astype(F32)
        store(qkv_v.at[pl.ds(24 * r, 24)], qkv_out.at[pl.ds(24 * r, 24)])
        out_v[at, :] = gmain_v[r, 3].astype(F32)
    store(out_v, out_out)
    loads[4].wait()
    for r in range(16):
        for s in range(2):
            in_v[8 * r : 8 * (r + 1), half * s : half * (s + 1)] = gin_v[2 * r + s].astype(F32)
    store(in_v, in_out)
    loads[5].wait()
    store(latent_v, latent_out)
    for cp in stores:
        cp.wait()


def per_device(
    features, projection, active_count, in_weight, norm_gain, qkv_weight, out_weight, cotangent
):
    patches, feat = features.shape[2:]
    own, width = cotangent.shape[1:]
    views = projection.shape[1]
    objects = lax.axis_size("obj")
    kernel, scratch = make_kernel((patches, feat, width, own, objects, views))
    hbm = pl.BlockSpec(memory_space=pl.ANY)
    latent, gin, gmain = pl.pallas_call(
        kernel,
        name="encode",
        out_shape=(
            jax.ShapeDtypeStruct((own, width), BF16),
            jax.ShapeDtypeStruct((objects, 8, width // 2), BF16),
            jax.ShapeDtypeStruct((4, 4, 24, width), BF16),
        ),
        in_specs=[hbm] * 8,
        out_specs=(hbm, hbm, hbm),
        scratch_shapes=[pltpu.VMEM(s, t) for s, t in scratch]
        + [
            pltpu.SMEM((1,), jnp.int32),
            pltpu.SemaphoreType.DMA((56,)),
            pltpu.SemaphoreType.DMA((56,)),
            pltpu.SemaphoreType.DMA((10 + CHUNKS,)),
            pltpu.SemaphoreType.REGULAR,
        ],
        compiler_params=pltpu.CompilerParams(
            collective_id=0, has_side_effects=True, vmem_limit_bytes=62 * 1024 * 1024
        ),
    )(
        features.reshape(patches, feat),
        projection.reshape(views, patches),
        active_count,
        in_weight,
        norm_gain,
        qkv_weight,
        out_weight,
        cotangent.reshape(own, width),
    )
    latent, in_grad, qkv_grad, out_grad = pl.pallas_call(
        write_out,
        name="write_out",
        out_shape=(
            jax.ShapeDtypeStruct((own, width), BF16),
            jax.ShapeDtypeStruct((own, width), F32),
            jax.ShapeDtypeStruct((96, 3 * width), F32),
            jax.ShapeDtypeStruct((96, width), F32),
        ),
        in_specs=[hbm, hbm, hbm],
        out_specs=(hbm, hbm, hbm, hbm),
        scratch_shapes=[
            pltpu.VMEM((own, width), BF16),
            pltpu.VMEM((objects, 8, width // 2), BF16),
            pltpu.VMEM((4, 4, 24, width), BF16),
            pltpu.VMEM((own, width), F32),
            pltpu.VMEM((96, 3 * width), F32),
            pltpu.VMEM((96, width), F32),
            pltpu.SemaphoreType.DMA((6,)),
            pltpu.SemaphoreType.DMA((7,)),
        ],
    )(latent, gin, gmain)
    return (latent[None], in_grad, qkv_grad, out_grad)


def solution(mesh):
    return jax.shard_map(
        per_device,
        mesh=mesh,
        in_specs=(
            P("obj", "view", None, None),
            P("obj", None, None),
            P("obj"),
            P(),
            P(),
            P(),
            P(),
            P("obj", "view", None),
        ),
        out_specs=(P("obj", "view", None), P("view", None), P("view", None), P("view", None)),
        check_vma=False,
    )
```

```python
import jax
import jax.numpy as jnp
from jax import lax
from jax.experimental import pallas as pl
from jax.experimental.pallas import tpu as pltpu
from jax.sharding import PartitionSpec as P

HEAD_DIM = 64
MESH = pl.DeviceIdType.MESH
F32 = jnp.float32
BF16 = jnp.bfloat16
NEG = -1e30
CHUNKS = 4
QROWS = 256


def dot_nn(a, b):
    return lax.dot_general(a, b, (((1,), (0,)), ((), ())), preferred_element_type=F32)


def dot_nt(a, b):
    return lax.dot_general(a, b, (((1,), (1,)), ((), ())), preferred_element_type=F32)


def dot_tn(a, b):
    return lax.dot_general(a, b, (((0,), (0,)), ((), ())), preferred_element_type=F32)


class Group:
    def __init__(self, like, send_sem, recv_sem):
        self.like, self.send_sem, self.recv_sem = like, send_sem, recv_sem

    def wait_send(self):
        pltpu.make_async_copy(self.like, self.like, self.send_sem).wait()

    def wait_recv(self):
        pltpu.make_async_copy(self.like, self.like, self.recv_sem).wait()


def make_kernel(sizes):
    patches, feat, width, own, objects, views = sizes
    chips = 4
    heads = 3
    part = heads * HEAD_DIM
    group = chips * own
    slots = 2 * group
    cols = feat // CHUNKS
    vcols = feat // chips
    orows = part // 2

    def kernel(
        feat_hbm, proj_hbm, count_hbm, in_hbm, gain_hbm, qkv_hbm, out_hbm, cot_hbm,
        latent_hbm, gin_hbm, gmain_hbm,
        proj_ref, gain_ref, latent_v, feat_v, inw, qkvw, outw, cot_v, hot, psend, precv, pown, ysend, psum, rrecv, yrecv, ylast,
        seeds, vox, vcol, base, unit, normed, turned, wown, qs, kvs, gouts, wback, att, afull,
        dkv, dkv_send, dkv_recv, gp, gq, gpr, og, og_send, og_recv,
        qg, qg_send, qg_recv, qx, qxr, qxl, qxlr, qt, qr, ox, oxr, gball, ig, ig_send, ig_recv,
        mz, mzr, mf, mg, ix, ixr, iz, izr, jf, jg,
        count_ref, ssem, rsem, lsem, ready,
    ):
        obj = lax.axis_index("obj")
        view = lax.axis_index("view")
        c = view // 2
        k = view % 2
        z = obj // 4
        x = obj % 4

        def at_y(d):
            return (obj, ((c + d) % 4) * 2 + k)

        def at_x(d):
            return (z * 4 + (x + d) % 4, view)

        def at_z(d):
            return (((z + d) % 8) * 4 + x, view)

        def at_o(dz, dx):
            return (((z + dz) % 8) * 4 + (x + dx) % 4, view)

        others = [(dz, dx) for dz in (4, 3, 5, 2, 6, 1, 7, 0) for dx in (2, 1, 3, 0) if dz or dx]
        mate = (obj, c * 2 + (1 - k))
        used = [0]
        sent = []

        def send(src, dst, device):
            n = used[0]
            used[0] += 1
            cp = pltpu.make_async_remote_copy(
                src_ref=src, dst_ref=dst, send_sem=ssem.at[n], recv_sem=rsem.at[n],
                device_id=device, device_id_type=MESH,
            )
            cp.start()
            sent.append(cp)
            return cp

        def send_all(triples, like):
            n = used[0]
            used[0] += 1
            for src, dst, device in triples:
                pltpu.make_async_remote_copy(
                    src_ref=src, dst_ref=dst, send_sem=ssem.at[n], recv_sem=rsem.at[n],
                    device_id=device, device_id_type=MESH,
                ).start()
            group = Group(like, ssem.at[n], rsem.at[n])
            sent.append(group)
            return group

        def load(n, src, dst):
            cp = pltpu.make_async_copy(src, dst, lsem.at[n])
            cp.start()
            return cp

        def rows_of(d, half=None):
            if half is None:
                return pl.ds(own * d, own)
            return pl.ds(own * d + own // 2 * half, own // 2)

        def gather_start(buf):
            out = {}
            for to, slot, order in ((1, 1, (0, 1)), (3, 3, (1, 0))):
                for half in order:
                    out[slot, half] = send(
                        buf.at[rows_of(0, half)], buf.at[rows_of(slot, half)], at_y(to)
                    )
            return out

        def gather_pass(buf, cps):
            cps[1, 0].wait_recv()
            cps[2, 0] = send(buf.at[rows_of(1, 0)], buf.at[rows_of(2, 0)], at_y(1))
            cps[3, 1].wait_recv()
            cps[2, 1] = send(buf.at[rows_of(3, 1)], buf.at[rows_of(2, 1)], at_y(3))

        def gather_wait(cps, slot):
            for half in ((1,), (0, 1), (0,))[slot - 1]:
                cps[slot, half].wait_recv()

        barrier = pltpu.get_barrier_semaphore()
        peers = [mate]
        peers += [at_y(d) for d in (1, 2, 3)]
        peers += [at_x(d) for d in (1, 2, 3)]
        peers += [at_z(d) for d in range(1, 8)]
        for p in peers:
            pl.semaphore_signal(barrier, 1, device_id=p, device_id_type=MESH)

        l_proj = load(5, proj_hbm, proj_ref)
        l_count = load(6, count_hbm, count_ref)
        l_cot = load(0, cot_hbm, cot_v)
        l_feat = [
            load(10 + j, feat_hbm.at[:, pl.ds(cols * j, cols)], feat_v.at[j]) for j in range(CHUNKS)
        ]
        l_out = load(2, out_hbm, outw)
        l_in = load(3, in_hbm, inw)
        l_gain = load(7, gain_hbm, gain_ref)
        l_qkv = load(4, qkv_hbm, qkvw)

        l_proj.wait()
        l_count.wait()
        count = count_ref[0]
        own_ids = view * own + lax.broadcasted_iota(jnp.int32, (own, 1), 0)
        live = jnp.where(own_ids < count, 1.0, 0.0).astype(F32)
        proj_row = proj_ref[pl.ds(view, 1), :]
        for kk in range(2):
            par = k if kk else 1 - k
            for d in range(4):
                ids = (
                    ((c + 4 - d) % 4) * (2 * own)
                    + par * own
                    + lax.broadcasted_iota(jnp.int32, (own, patches), 0)
                )
                hot[kk, own * d : own * (d + 1), :] = jnp.where(ids == proj_row, 1.0, 0.0).astype(BF16)

        mate_cp, relay_cp, y_cp = [], {}, {}

        def sums(j, kk):
            return dot_nn(hot[kk], feat_v[j])

        last = CHUNKS - 1

        def combine(j):
            raw = sums(j, 1)
            mate_cp[j].wait_recv()
            both = raw + precv[j].astype(F32)
            pown[j] = both[0:own, :]
            ysend[j, own:, :] = both[own:, :].astype(BF16)
            if j == last:
                y_cp[j] = send_all(
                    [(ysend.at[j, rows_of(d)], ylast.at[d - 1], at_y(4 - d)) for d in (2, 3, 1)],
                    ylast,
                )
                return
            relay_cp[j] = send_all(
                [
                    (
                        ysend.at[j, rows_of(2), pl.ds(cols // 2 * s, cols // 2)],
                        rrecv.at[j, s],
                        at_y((1, 3)[s]),
                    )
                    for s in range(2)
                ],
                rrecv.at[j],
            )
            mid = cols // 2
            psum[j, 0] = both[3 * own :, 0:mid]
            psum[j, 1] = both[own : 2 * own, mid:]

        def forward(j):
            relay_cp[j].wait_recv()
            mid = cols // 2
            for s, d in ((0, 3), (1, 1)):
                ysend[j, own * d : own * (d + 1), mid * s : mid * (s + 1)] = (
                    psum[j, s] + rrecv[j, s].astype(F32)
                ).astype(BF16)
            y_cp[j] = send_all(
                [
                    (ysend.at[j, rows_of(d)], yrecv.at[j, s], at_y(4 - d))
                    for s, d in ((0, 3), (1, 1))
                ],
                yrecv.at[j],
            )

        l_cot.wait()
        seeds[0:own, :] = (cot_v[...].astype(F32) * live * (1.0 / objects)).astype(BF16)
        l_feat[0].wait()
        psend[0] = sums(0, 0).astype(BF16)
        pl.semaphore_wait(barrier, len(peers))
        mate_cp.append(send(psend.at[0], precv.at[0], mate))
        for p in range(1, 4):
            pl.semaphore_signal(ready, 1, device_id=at_x(p), device_id_type=MESH)
        s_cp = gather_start(seeds)
        for j in range(1, CHUNKS):
            l_feat[j].wait()
            psend[j] = sums(j, 0).astype(BF16)
            mate_cp.append(send(psend.at[j], precv.at[j], mate))
            combine(j - 1)
            if j == 2:
                gather_pass(seeds, s_cp)
            if j > 1:
                forward(j - 2)
        combine(last)
        forward(last - 1)

        number = jnp.zeros((own, 1), F32)
        for w in range(views):
            same = proj_ref[w : w + 1, :] == view * own + lax.broadcasted_iota(
                jnp.int32, (own, patches), 0
            )
            number += jnp.sum(jnp.where(same, 1.0, 0.0), axis=1, keepdims=True)
        number = jnp.maximum(number, 1.0)

        l_qkv.wait()
        for t in range(3):
            window = qkvw[:, pl.ds(pl.multiple_of(width * t + 128 * ((3 * c) // 2), 128), 256)]

            @pl.when(c % 2 == 0)
            def _():
                wown[:, part * t : part * (t + 1)] = window[:, 0:part]

            @pl.when(c % 2 == 1)
            def _():
                wown[:, part * t : part * (t + 1)] = window[:, 64 : 64 + part]

        for t in range(4):
            for h in range(heads):
                at = part * t + HEAD_DIM * h
                w_q = qkvw[:, at : at + HEAD_DIM]
                wback[t, h, :, 0:128] = jnp.concatenate([w_q, jnp.zeros_like(w_q)], axis=1)
                wback[t, h, :, 128:] = jnp.concatenate(
                    [qkvw[:, s * width + at : s * width + at + HEAD_DIM] for s in (1, 2)], axis=1
                )

        l_out.wait()
        rows = outw[pl.ds(pl.multiple_of(part * c, 64), part), :]

        def pull(d):
            at = slice(own * d, own * (d + 1))
            if d:
                gather_wait(s_cp, d)
            gouts[at, :] = dot_nt(seeds[at, :], rows).astype(BF16)

        for d in (0, 1, 3):
            pull(d)
        for j in range(CHUNKS):
            total = pown[j]
            y_cp[j].wait_recv()
            if j == last:
                for d in range(3):
                    total += ylast[d].astype(F32)
            else:
                total += yrecv[j, 0].astype(F32) + yrecv[j, 1].astype(F32)
            vox[:, cols * j : cols * (j + 1)] = (total / number).astype(BF16)
        l_in.wait()
        base_rows = dot_nn(vox[...], inw[...])
        base[...] = base_rows
        shifted = base_rows - jnp.mean(base_rows, axis=1, keepdims=True)
        spread = jnp.mean(shifted * shifted, axis=1, keepdims=True)
        inverse = lax.rsqrt(spread + 1e-06)
        unit_rows = shifted * inverse
        unit[...] = unit_rows
        l_gain.wait()
        gain = gain_ref[...].reshape(1, width)
        normed[0:own, :] = (unit_rows * gain).astype(BF16)
        n_cp = gather_start(normed)

        kv_n = used[0]
        used[0] += 1

        def share(d):
            pltpu.make_async_remote_copy(
                src_ref=kvs.at[rows_of(d)], dst_ref=kvs.at[pl.ds(group + own * d, own)],
                send_sem=ssem.at[kv_n], recv_sem=rsem.at[kv_n],
                device_id=mate, device_id_type=MESH,
            ).start()

        kv_cp = Group(kvs.at[pl.ds(0, group)], ssem.at[kv_n], rsem.at[kv_n])
        sent.append(kv_cp)

        def project(d):
            at = slice(own * d, own * (d + 1))
            packed = dot_nn(normed[at, :], wown[...])
            qs[at, :] = (packed[:, 0:part] * (HEAD_DIM**-0.5)).astype(BF16)
            kvs[at, :] = packed[:, part : 3 * part].astype(BF16)
            share(d)
            turned[:, at] = normed[at, :].T

        project(0)
        gather_pass(normed, n_cp)
        pull(2)
        for d in (1, 3):
            gather_wait(n_cp, d)
            project(d)
        gather_wait(n_cp, 2)
        project(2)
        v_cp = send_all(
            [
                (
                    vox.at[:, pl.ds(pl.multiple_of(vcols * ((c + d) % 4), 128), vcols)],
                    vcol.at[rows_of(d)],
                    at_y(d),
                )
                for d in (1, 2, 3)
            ],
            vcol.at[pl.ds(0, 3 * own)],
        )
        vcol[0:own, :] = vox[:, pl.ds(pl.multiple_of(vcols * c, 128), vcols)]

        lane = lax.broadcasted_iota(jnp.int32, (1, own), 1)
        pieces = []
        for par in (k, 1 - k):
            for d in range(4):
                ids = ((c + 4 - d) % 4) * (2 * own) + par * own + lane
                pieces.append(jnp.where(ids < count, 0.0, NEG).astype(F32))
        bias = jnp.concatenate(pieces, axis=1)
        kv_cp.wait_recv()

        dkv_cp, g_cp, qg_cp, x_cp = [], [], [], []

        def attend(h, between=None):
            hs = slice(HEAD_DIM * h, HEAD_DIM * (h + 1))
            keys = kvs[:, hs]
            values = kvs[:, part + HEAD_DIM * h : part + HEAD_DIM * (h + 1)]
            grad_k = jnp.zeros((slots, HEAD_DIM), F32)
            grad_v = jnp.zeros((slots, HEAD_DIM), F32)
            for b in range(group // QROWS):
                rs = slice(QROWS * b, QROWS * (b + 1))
                q = qs[rs, hs]
                go = gouts[rs, hs]
                s = dot_nt(q, keys) + bias
                e = jnp.exp(s - jnp.max(s, axis=1, keepdims=True))
                w = e * (1.0 / jnp.sum(e, axis=1, keepdims=True))
                p = w.astype(BF16)
                mixed = dot_nn(p, values)
                att[rs, hs] = mixed.astype(BF16)
                delta = jnp.sum(go.astype(F32) * mixed, axis=1, keepdims=True)
                gs = (w * (dot_nt(go, values) - delta)).astype(BF16)
                grad_q = (dot_nn(gs, keys) * (HEAD_DIM**-0.5)).astype(BF16)
                gq[h, rs, 0:HEAD_DIM] = grad_q
                gp[h, rs, 0:128] = jnp.concatenate([grad_q, mixed.astype(BF16)], axis=1)
                grad_k += dot_tn(gs, q)
                grad_v += dot_tn(p, go)
                if b == 0 and between is not None:
                    between()
            both = jnp.concatenate([grad_k, grad_v], axis=1)
            dkv_send[h] = both[group:].astype(BF16)
            dkv_cp.append(send(dkv_send.at[h], dkv_recv.at[h], mate))
            dkv[h] = both[0:group]

        def finish(h):
            dkv_cp[h].wait_recv()
            both = dkv[h] + dkv_recv[h].astype(F32)
            both = both.astype(BF16)
            gp[h, :, 128:] = both
            gq[h, :, HEAD_DIM:] = both
            g_cp.append(
                send_all(
                    [(gp.at[h, rows_of(d)], gpr.at[c, h], at_y(4 - d)) for d in (2, 1, 3)],
                    gp.at[h, pl.ds(0, 3 * own)],
                )
            )
            gpr[c, h] = gp[h, 0:own, :]
            whole = dot_nn(turned[...], gq[h])
            for t in range(8):
                qg[h, t] = whole[orows * t : orows * (t + 1), :]
            for t in range(4):
                qg_send[h, t] = qg[h, 2 * t + (1 - k)].astype(BF16)
            qg_cp.append(send(qg_send.at[h], qg_recv.at[h], mate))

        def swap(h):
            qg_cp[h].wait_recv()
            for t in range(4):
                block = (qg[h, 2 * t + k] + qg_recv[h, t].astype(F32)).astype(BF16)
                for r in range(4):
                    piece = block[24 * r : 24 * (r + 1), :]
                    if h < 2:
                        qx[r, t, :, part * h : part * (h + 1)] = piece
                    else:
                        qxl[r, t] = piece
            if h:
                buf, recv = (qx, qxr) if h == 1 else (qxl, qxlr)
                x_cp.append(
                    send_all(
                        [(buf.at[(x + d) % 4], recv.at[d - 1], at_x(d)) for d in (2, 1, 3)], recv
                    )
                )

        def turn():
            for n, (buf, recv) in enumerate(((qx, qxr), (qxl, qxlr))):
                x_cp[n].wait_recv()
                for t in range(4):
                    at = slice(2 * part * n, 2 * part + part * n)
                    qt[t, :, at] = (
                        buf[x, t].astype(F32)
                        + recv[0, t].astype(F32)
                        + recv[1, t].astype(F32)
                        + recv[2, t].astype(F32)
                    ).astype(BF16)
            cp = send_all(
                [(qt.at[(c + d) % 4], qr.at[c], at_y(d)) for d in (2, 1, 3)], qr.at[pl.ds(0, 3)]
            )
            qr[c] = qt[c]
            return cp

        def back(h):
            g_cp[h].wait_recv()
            total = jnp.zeros((own, width), F32)
            for t in range(4):
                at = part * t + HEAD_DIM * h
                afull[:, at : at + HEAD_DIM] = gpr[t, h, :, HEAD_DIM : 2 * HEAD_DIM]
                total += dot_nt(gpr[t, h], wback[t, h])
            return total

        attend(0)
        attend(1, lambda: finish(0))
        attend(2, lambda: finish(1))
        swap(0)
        og[...] = dot_tn(att[...], seeds[...])
        og_send[...] = og[pl.ds(pl.multiple_of(orows * (1 - k), 32), orows), :].astype(BF16)
        og_cp = send(og_send, og_recv, mate)
        finish(2)
        swap(1)
        swap(2)
        og_cp.wait_recv()
        og_sum = (
            og[pl.ds(pl.multiple_of(orows * k, 32), orows), :] + og_recv[...].astype(F32)
        ).astype(BF16)
        for r in range(4):
            ox[r] = og_sum[24 * r : 24 * (r + 1), :]
        ox_cp = send_all([(ox.at[(x + d) % 4], oxr.at[d - 1], at_x(d)) for d in (2, 1, 3)], oxr)
        early = back(0) + back(1)
        grad_unit = (early + back(2)) * gain
        unit_rows = unit[...]
        branch_grad = inverse * (
            grad_unit
            - jnp.mean(grad_unit, axis=1, keepdims=True)
            - unit_rows * jnp.mean(grad_unit * unit_rows, axis=1, keepdims=True)
        )
        gball[0:own, :] = (seeds[0:own, :].astype(F32) + branch_grad).astype(BF16)
        b_cp = gather_start(gball)

        t_cp = turn()

        half = width // 2
        z_order = (4, 3, 5, 2, 6, 1, 7)

        def z_piece(buf, where):
            return buf.at[where // 2, :, pl.ds(pl.multiple_of(half * (where % 2), 128), half)]

        gather_pass(gball, b_cp)
        branch = dot_nn(afull[...], outw[...])
        latent_v[...] = (live * (base[...] + branch)).astype(BF16)
        l_latent = load(8, latent_v, latent_hbm)

        ox_cp.wait_recv()
        mz[3] = (
            ox[x].astype(F32) + oxr[0].astype(F32) + oxr[1].astype(F32) + oxr[2].astype(F32)
        ).astype(BF16)
        t_cp.wait_recv()
        for h in range(heads):
            for t in range(4):
                mz[h, :, part * t : part * (t + 1)] = qr[t, :, part * h : part * (h + 1)]
        mz_cp = send_all(
            [(z_piece(mz, (z + d) % 8), mzr.at[d - 1], at_z(d)) for d in z_order], mzr
        )
        v_cp.wait_recv()
        for d in (1, 3, 2):
            gather_wait(b_cp, d)
        ig[...] = dot_tn(vcol[...], gball[...])
        ig_send[...] = ig[pl.ds(pl.multiple_of(own * (1 - k), 128), own), :].astype(BF16)
        ig_cp = send(ig_send, ig_recv, mate)
        ig_cp.wait_recv()
        ig_sum = (
            ig[pl.ds(pl.multiple_of(own * k, 128), own), :] + ig_recv[...].astype(F32)
        ).astype(BF16)
        for r in range(16):
            for s in range(2):
                p = 2 * r + s
                ix[p // 8, p % 8] = ig_sum[8 * r : 8 * (r + 1), half * s : half * (s + 1)]
        ix_cp = send_all([(ix.at[(x + d) % 4], ixr.at[d - 1], at_x(d)) for d in (2, 1, 3)], ixr)

        mz_cp.wait_recv()
        total = z_piece(mz, z)[...].astype(F32)
        for d in range(7):
            total += mzr[d].astype(F32)
        mf[...] = total.astype(BF16)
        near, far = (1, 7, 2, 6), (3, 4, 5)
        mg_cp = [
            send_all([(mf, z_piece(mg.at[x], z), at_z(d)) for d in ds], mzr.at[pl.ds(0, len(ds))])
            for ds in (near, far)
        ]
        mg[x, z // 2, :, pl.ds(pl.multiple_of(half * (z % 2), 128), half)] = mf[...]
        mo_n = used[0]
        used[0] += 1

        def spread(src, where):
            for d in (2, 1, 3):
                pltpu.make_async_remote_copy(
                    src_ref=src, dst_ref=z_piece(mg.at[x], where),
                    send_sem=ssem.at[mo_n], recv_sem=rsem.at[mo_n],
                    device_id=at_x(d), device_id_type=MESH,
                ).start()

        mo_cp = Group(mg.at[pl.ds(0, 3)], ssem.at[mo_n], rsem.at[mo_n])
        sent.append(mo_cp)
        spread(mf, z)
        ix_cp.wait_recv()
        for p in range(8):
            iz[p] = (
                ix[x, p].astype(F32)
                + ixr[0, p].astype(F32)
                + ixr[1, p].astype(F32)
                + ixr[2, p].astype(F32)
            ).astype(BF16)
        iz_cp = send_all([(iz.at[(z + d) % 8], izr.at[d - 1], at_z(d)) for d in z_order], izr)
        for cp, ds in zip(mg_cp, (near, far)):
            cp.wait_recv()
            for d in ds:
                spread(z_piece(mg.at[x], (z + 8 - d) % 8), (z + 8 - d) % 8)
        iz_cp.wait_recv()
        total = iz[z].astype(F32)
        for d in range(7):
            total += izr[d].astype(F32)
        jf[...] = total.astype(BF16)
        pl.semaphore_wait(ready, 3)
        jg_cp = send_all(
            [(jf, jg.at[x * 8 + z], at_o(*f)) for f in others], jg.at[pl.ds(0, len(others))]
        )
        jg[x * 8 + z] = jf[...]
        jg_cp.wait_recv()
        l_gin = load(9, jg, gin_hbm)
        mo_cp.wait_recv()
        l_main = load(0, mg, gmain_hbm)
        for cp in sent:
            cp.wait_send()
        l_latent.wait()
        l_gin.wait()
        l_main.wait()

    scratch = [
        ((views, patches), jnp.int32), ((width,), F32), ((own, width), BF16),
        ((CHUNKS, patches, cols), BF16), ((feat, width), BF16), ((width, 3 * width), BF16),
        ((width, width), BF16), ((own, width), BF16), ((2, group, patches), BF16),
        ((CHUNKS, group, cols), BF16), ((CHUNKS, group, cols), BF16), ((CHUNKS, own, cols), F32),
        ((CHUNKS, group, cols), BF16), ((CHUNKS - 1, 2, own, cols // 2), F32),
        ((CHUNKS - 1, 2, own, cols // 2), BF16), ((CHUNKS - 1, 2, own, cols), BF16),
        ((3, own, cols), BF16),
        ((group, width), BF16), ((own, feat), BF16), ((group, vcols), BF16),
        ((own, width), F32), ((own, width), F32), ((group, width), BF16), ((width, group), BF16),
        ((width, 3 * part), BF16), ((group, part), BF16), ((slots, 2 * part), BF16),
        ((group, part), BF16), ((4, heads, width, 256), BF16),
        ((group, part), BF16), ((own, width), BF16),
        ((heads, group, 128), F32), ((heads, group, 128), BF16), ((heads, group, 128), BF16),
        ((heads, group, 256), BF16), ((heads, group, part), BF16), ((4, heads, own, 256), BF16),
        ((part, width), F32), ((orows, width), BF16), ((orows, width), BF16),
        ((heads, 8, orows, part), F32), ((heads, 4, orows, part), BF16),
        ((heads, 4, orows, part), BF16),
        ((4, 4, 24, 2 * part), BF16), ((3, 4, 24, 2 * part), BF16),
        ((4, 4, 24, part), BF16), ((3, 4, 24, part), BF16),
        ((4, 24, 3 * part), BF16), ((4, 24, 3 * part), BF16),
        ((4, 24, width), BF16), ((3, 24, width), BF16),
        ((group, width), BF16), ((2 * own, width), F32), ((own, width), BF16), ((own, width), BF16),
        ((4, 24, width), BF16),
        ((7, 24, width // 2), BF16), ((24, width // 2), BF16), ((4, 4, 24, width), BF16),
        ((4, 8, 8, width // 2), BF16), ((3, 8, 8, width // 2), BF16),
        ((8, 8, width // 2), BF16), ((7, 8, width // 2), BF16),
        ((8, width // 2), BF16), ((objects, 8, width // 2), BF16),
    ]
    return kernel, scratch


def write_out(
    latent_hbm, gin_hbm, gmain_hbm, latent_out, in_out, qkv_out, out_out,
    latent_v, gin_v, gmain_v, in_v, qkv_v, out_v, lsem, osem,
):
    width = latent_v.shape[1]
    half = width // 2
    part = width // 4
    loads = [pltpu.make_async_copy(gmain_hbm.at[r], gmain_v.at[r], lsem.at[r]) for r in range(4)]
    loads.append(pltpu.make_async_copy(gin_hbm, gin_v, lsem.at[4]))
    loads.append(pltpu.make_async_copy(latent_hbm, latent_v, lsem.at[5]))
    for cp in loads:
        cp.start()
    stores = []

    def store(src, dst):
        cp = pltpu.make_async_copy(src, dst, osem.at[len(stores)])
        cp.start()
        stores.append(cp)

    for r in range(4):
        loads[r].wait()
        at = slice(24 * r, 24 * (r + 1))
        for s in range(3):
            for t in range(4):
                for h in range(3):
                    to = width * s + part * t + HEAD_DIM * h
                    fr = part * t + HEAD_DIM * s
                    qkv_v[at, to : to + HEAD_DIM] = gmain_v[r, h, :, fr : fr + HEAD_DIM].astype(F32)
        store(qkv_v.at[pl.ds(24 * r, 24)], qkv_out.at[pl.ds(24 * r, 24)])
        out_v[at, :] = gmain_v[r, 3].astype(F32)
    store(out_v, out_out)
    loads[4].wait()
    for r in range(16):
        for s in range(2):
            in_v[8 * r : 8 * (r + 1), half * s : half * (s + 1)] = gin_v[2 * r + s].astype(F32)
    store(in_v, in_out)
    loads[5].wait()
    store(latent_v, latent_out)
    for cp in stores:
        cp.wait()


def per_device(
    features, projection, active_count, in_weight, norm_gain, qkv_weight, out_weight, cotangent
):
    patches, feat = features.shape[2:]
    own, width = cotangent.shape[1:]
    views = projection.shape[1]
    objects = lax.axis_size("obj")
    kernel, scratch = make_kernel((patches, feat, width, own, objects, views))
    hbm = pl.BlockSpec(memory_space=pl.ANY)
    latent, gin, gmain = pl.pallas_call(
        kernel,
        name="encode",
        out_shape=(
            jax.ShapeDtypeStruct((own, width), BF16),
            jax.ShapeDtypeStruct((objects, 8, width // 2), BF16),
            jax.ShapeDtypeStruct((4, 4, 24, width), BF16),
        ),
        in_specs=[hbm] * 8,
        out_specs=(hbm, hbm, hbm),
        scratch_shapes=[pltpu.VMEM(s, t) for s, t in scratch]
        + [
            pltpu.SMEM((1,), jnp.int32),
            pltpu.SemaphoreType.DMA((56,)),
            pltpu.SemaphoreType.DMA((56,)),
            pltpu.SemaphoreType.DMA((10 + CHUNKS,)),
            pltpu.SemaphoreType.REGULAR,
        ],
        compiler_params=pltpu.CompilerParams(
            collective_id=0, has_side_effects=True, vmem_limit_bytes=62 * 1024 * 1024
        ),
    )(
        features.reshape(patches, feat),
        projection.reshape(views, patches),
        active_count,
        in_weight,
        norm_gain,
        qkv_weight,
        out_weight,
        cotangent.reshape(own, width),
    )
    latent, in_grad, qkv_grad, out_grad = pl.pallas_call(
        write_out,
        name="write_out",
        out_shape=(
            jax.ShapeDtypeStruct((own, width), BF16),
            jax.ShapeDtypeStruct((own, width), F32),
            jax.ShapeDtypeStruct((96, 3 * width), F32),
            jax.ShapeDtypeStruct((96, width), F32),
        ),
        in_specs=[hbm, hbm, hbm],
        out_specs=(hbm, hbm, hbm, hbm),
        scratch_shapes=[
            pltpu.VMEM((own, width), BF16),
            pltpu.VMEM((objects, 8, width // 2), BF16),
            pltpu.VMEM((4, 4, 24, width), BF16),
            pltpu.VMEM((own, width), F32),
            pltpu.VMEM((96, 3 * width), F32),
            pltpu.VMEM((96, width), F32),
            pltpu.SemaphoreType.DMA((6,)),
            pltpu.SemaphoreType.DMA((7,)),
        ],
    )(latent, gin, gmain)
    return (latent[None], in_grad, qkv_grad, out_grad)


def solution(mesh):
    return jax.shard_map(
        per_device,
        mesh=mesh,
        in_specs=(
            P("obj", "view", None, None),
            P("obj", None, None),
            P("obj"),
            P(),
            P(),
            P(),
            P(),
            P("obj", "view", None),
        ),
        out_specs=(P("obj", "view", None), P("view", None), P("view", None), P("view", None)),
        check_vma=False,
    )
```

```python
import jax
import jax.numpy as jnp
from jax import lax
from jax.experimental import pallas as pl
from jax.experimental.pallas import tpu as pltpu
from jax.sharding import PartitionSpec as P

HEAD_DIM = 64
MESH = pl.DeviceIdType.MESH
F32 = jnp.float32
BF16 = jnp.bfloat16
NEG = -1e30
CHUNKS = 4
QROWS = 256


def dot_nn(a, b):
    return lax.dot_general(a, b, (((1,), (0,)), ((), ())), preferred_element_type=F32)


def dot_nt(a, b):
    return lax.dot_general(a, b, (((1,), (1,)), ((), ())), preferred_element_type=F32)


def dot_tn(a, b):
    return lax.dot_general(a, b, (((0,), (0,)), ((), ())), preferred_element_type=F32)


class Group:
    def __init__(self, like, send_sem, recv_sem):
        self.like, self.send_sem, self.recv_sem = like, send_sem, recv_sem

    def wait_send(self):
        pltpu.make_async_copy(self.like, self.like, self.send_sem).wait()

    def wait_recv(self):
        pltpu.make_async_copy(self.like, self.like, self.recv_sem).wait()


def make_kernel(sizes):
    patches, feat, width, own, objects, views = sizes
    chips = 4
    heads = 3
    part = heads * HEAD_DIM
    group = chips * own
    slots = 2 * group
    cols = feat // CHUNKS
    vcols = feat // chips
    orows = part // 2

    def kernel(
        feat_hbm, proj_hbm, count_hbm, in_hbm, gain_hbm, qkv_hbm, out_hbm, cot_hbm,
        latent_hbm, gin_hbm, gmain_hbm,
        proj_ref, gain_ref, latent_v, feat_v, inw, qkvw, outw, cot_v, hot, psend, precv, pown, ysend, psum, rrecv, yrecv, ylast,
        seeds, vox, vcol, base, unit, normed, turned, wown, qs, kvs, gouts, wback, att, afull,
        dkv, dkv_send, dkv_recv, gp, gq, gpr, og, og_send, og_recv,
        qg, qg_send, qg_recv, qx, qxr, qxl, qxlr, qt, qr, ox, oxr, gball, ig, ig_send, ig_recv,
        mz, mzr, mf, mg, ix, ixr, iz, izr, jf, jg,
        count_ref, ssem, rsem, lsem, ready,
    ):
        obj = lax.axis_index("obj")
        view = lax.axis_index("view")
        c = view // 2
        k = view % 2
        z = obj // 4
        x = obj % 4

        def at_y(d):
            return (obj, ((c + d) % 4) * 2 + k)

        def at_x(d):
            return (z * 4 + (x + d) % 4, view)

        def at_z(d):
            return (((z + d) % 8) * 4 + x, view)

        def at_o(dz, dx):
            return (((z + dz) % 8) * 4 + (x + dx) % 4, view)

        others = [(dz, dx) for dz in (4, 3, 5, 2, 6, 1, 7, 0) for dx in (2, 1, 3, 0) if dz or dx]
        mate = (obj, c * 2 + (1 - k))
        used = [0]
        sent = []

        def send(src, dst, device):
            n = used[0]
            used[0] += 1
            cp = pltpu.make_async_remote_copy(
                src_ref=src, dst_ref=dst, send_sem=ssem.at[n], recv_sem=rsem.at[n],
                device_id=device, device_id_type=MESH,
            )
            cp.start()
            sent.append(cp)
            return cp

        def send_all(triples, like):
            n = used[0]
            used[0] += 1
            for src, dst, device in triples:
                pltpu.make_async_remote_copy(
                    src_ref=src, dst_ref=dst, send_sem=ssem.at[n], recv_sem=rsem.at[n],
                    device_id=device, device_id_type=MESH,
                ).start()
            group = Group(like, ssem.at[n], rsem.at[n])
            sent.append(group)
            return group

        def load(n, src, dst):
            cp = pltpu.make_async_copy(src, dst, lsem.at[n])
            cp.start()
            return cp

        def rows_of(d, half=None):
            if half is None:
                return pl.ds(own * d, own)
            return pl.ds(own * d + own // 2 * half, own // 2)

        def gather_start(buf):
            out = {}
            for to, slot, order in ((1, 1, (0, 1)), (3, 3, (1, 0))):
                for half in order:
                    out[slot, half] = send(
                        buf.at[rows_of(0, half)], buf.at[rows_of(slot, half)], at_y(to)
                    )
            return out

        def gather_pass(buf, cps):
            cps[1, 0].wait_recv()
            cps[2, 0] = send(buf.at[rows_of(1, 0)], buf.at[rows_of(2, 0)], at_y(1))
            cps[3, 1].wait_recv()
            cps[2, 1] = send(buf.at[rows_of(3, 1)], buf.at[rows_of(2, 1)], at_y(3))

        def gather_wait(cps, slot):
            for half in ((1,), (0, 1), (0,))[slot - 1]:
                cps[slot, half].wait_recv()

        barrier = pltpu.get_barrier_semaphore()
        peers = [mate]
        peers += [at_y(d) for d in (1, 2, 3)]
        peers += [at_x(d) for d in (1, 2, 3)]
        peers += [at_z(d) for d in range(1, 8)]
        for p in peers:
            pl.semaphore_signal(barrier, 1, device_id=p, device_id_type=MESH)

        l_proj = load(5, proj_hbm, proj_ref)
        l_count = load(6, count_hbm, count_ref)
        l_cot = load(0, cot_hbm, cot_v)
        l_feat = [
            load(10 + j, feat_hbm.at[:, pl.ds(cols * j, cols)], feat_v.at[j]) for j in range(CHUNKS)
        ]
        l_out = load(2, out_hbm, outw)
        l_in = load(3, in_hbm, inw)
        l_gain = load(7, gain_hbm, gain_ref)
        l_qkv = load(4, qkv_hbm, qkvw)

        l_proj.wait()
        l_count.wait()
        count = count_ref[0]
        own_ids = view * own + lax.broadcasted_iota(jnp.int32, (own, 1), 0)
        live = jnp.where(own_ids < count, 1.0, 0.0).astype(F32)
        proj_row = proj_ref[pl.ds(view, 1), :]
        for kk in range(2):
            par = k if kk else 1 - k
            for d in range(4):
                ids = (
                    ((c + 4 - d) % 4) * (2 * own)
                    + par * own
                    + lax.broadcasted_iota(jnp.int32, (own, patches), 0)
                )
                hot[kk, own * d : own * (d + 1), :] = jnp.where(ids == proj_row, 1.0, 0.0).astype(BF16)

        mate_cp, relay_cp, y_cp = [], {}, {}

        def sums(j, kk):
            return dot_nn(hot[kk], feat_v[j])

        last = CHUNKS - 1

        def combine(j):
            raw = sums(j, 1)
            mate_cp[j].wait_recv()
            both = raw + precv[j].astype(F32)
            pown[j] = both[0:own, :]
            ysend[j, own:, :] = both[own:, :].astype(BF16)
            if j == last:
                y_cp[j] = send_all(
                    [(ysend.at[j, rows_of(d)], ylast.at[d - 1], at_y(4 - d)) for d in (2, 3, 1)],
                    ylast,
                )
                return
            relay_cp[j] = send_all(
                [
                    (
                        ysend.at[j, rows_of(2), pl.ds(cols // 2 * s, cols // 2)],
                        rrecv.at[j, s],
                        at_y((1, 3)[s]),
                    )
                    for s in range(2)
                ],
                rrecv.at[j],
            )
            mid = cols // 2
            psum[j, 0] = both[3 * own :, 0:mid]
            psum[j, 1] = both[own : 2 * own, mid:]

        def forward(j):
            relay_cp[j].wait_recv()
            mid = cols // 2
            for s, d in ((0, 3), (1, 1)):
                ysend[j, own * d : own * (d + 1), mid * s : mid * (s + 1)] = (
                    psum[j, s] + rrecv[j, s].astype(F32)
                ).astype(BF16)
            y_cp[j] = send_all(
                [
                    (ysend.at[j, rows_of(d)], yrecv.at[j, s], at_y(4 - d))
                    for s, d in ((0, 3), (1, 1))
                ],
                yrecv.at[j],
            )

        l_cot.wait()
        seeds[0:own, :] = (cot_v[...].astype(F32) * live * (1.0 / objects)).astype(BF16)
        l_feat[0].wait()
        psend[0] = sums(0, 0).astype(BF16)
        pl.semaphore_wait(barrier, len(peers))
        mate_cp.append(send(psend.at[0], precv.at[0], mate))
        for p in range(1, 4):
            pl.semaphore_signal(ready, 1, device_id=at_x(p), device_id_type=MESH)
        s_cp = gather_start(seeds)
        for j in range(1, CHUNKS):
            l_feat[j].wait()
            psend[j] = sums(j, 0).astype(BF16)
            mate_cp.append(send(psend.at[j], precv.at[j], mate))
            combine(j - 1)
            if j == 2:
                gather_pass(seeds, s_cp)
            if j > 1:
                forward(j - 2)
        combine(last)
        forward(last - 1)

        number = jnp.zeros((own, 1), F32)
        for w in range(views):
            same = proj_ref[w : w + 1, :] == view * own + lax.broadcasted_iota(
                jnp.int32, (own, patches), 0
            )
            number += jnp.sum(jnp.where(same, 1.0, 0.0), axis=1, keepdims=True)
        number = jnp.maximum(number, 1.0)

        l_qkv.wait()
        for t in range(3):
            window = qkvw[:, pl.ds(pl.multiple_of(width * t + 128 * ((3 * c) // 2), 128), 256)]

            @pl.when(c % 2 == 0)
            def _():
                wown[:, part * t : part * (t + 1)] = window[:, 0:part]

            @pl.when(c % 2 == 1)
            def _():
                wown[:, part * t : part * (t + 1)] = window[:, 64 : 64 + part]

        for t in range(4):
            for h in range(heads):
                at = part * t + HEAD_DIM * h
                w_q = qkvw[:, at : at + HEAD_DIM]
                wback[t, h, :, 0:128] = jnp.concatenate([w_q, jnp.zeros_like(w_q)], axis=1)
                wback[t, h, :, 128:] = jnp.concatenate(
                    [qkvw[:, s * width + at : s * width + at + HEAD_DIM] for s in (1, 2)], axis=1
                )

        l_out.wait()
        rows = outw[pl.ds(pl.multiple_of(part * c, 64), part), :]

        def pull(d):
            at = slice(own * d, own * (d + 1))
            if d:
                gather_wait(s_cp, d)
            gouts[at, :] = dot_nt(seeds[at, :], rows).astype(BF16)

        for d in (0, 1, 3):
            pull(d)
        for j in range(CHUNKS):
            total = pown[j]
            y_cp[j].wait_recv()
            if j == last:
                for d in range(3):
                    total += ylast[d].astype(F32)
            else:
                total += yrecv[j, 0].astype(F32) + yrecv[j, 1].astype(F32)
            vox[:, cols * j : cols * (j + 1)] = (total / number).astype(BF16)
        l_in.wait()
        base_rows = dot_nn(vox[...], inw[...])
        base[...] = base_rows
        shifted = base_rows - jnp.mean(base_rows, axis=1, keepdims=True)
        spread = jnp.mean(shifted * shifted, axis=1, keepdims=True)
        inverse = lax.rsqrt(spread + 1e-06)
        unit_rows = shifted * inverse
        unit[...] = unit_rows
        l_gain.wait()
        gain = gain_ref[...].reshape(1, width)
        normed[0:own, :] = (unit_rows * gain).astype(BF16)
        n_cp = gather_start(normed)

        kv_n = used[0]
        used[0] += 1

        def share(d):
            pltpu.make_async_remote_copy(
                src_ref=kvs.at[rows_of(d)], dst_ref=kvs.at[pl.ds(group + own * d, own)],
                send_sem=ssem.at[kv_n], recv_sem=rsem.at[kv_n],
                device_id=mate, device_id_type=MESH,
            ).start()

        kv_cp = Group(kvs.at[pl.ds(0, group)], ssem.at[kv_n], rsem.at[kv_n])
        sent.append(kv_cp)

        def project(d):
            at = slice(own * d, own * (d + 1))
            packed = dot_nn(normed[at, :], wown[...])
            qs[at, :] = (packed[:, 0:part] * (HEAD_DIM**-0.5)).astype(BF16)
            kvs[at, :] = packed[:, part : 3 * part].astype(BF16)
            share(d)
            turned[:, at] = normed[at, :].T

        project(0)
        gather_pass(normed, n_cp)
        pull(2)
        for d in (1, 3):
            gather_wait(n_cp, d)
            project(d)
        gather_wait(n_cp, 2)
        project(2)
        v_cp = send_all(
            [
                (
                    vox.at[:, pl.ds(pl.multiple_of(vcols * ((c + d) % 4), 128), vcols)],
                    vcol.at[rows_of(d)],
                    at_y(d),
                )
                for d in (1, 2, 3)
            ],
            vcol.at[pl.ds(0, 3 * own)],
        )
        vcol[0:own, :] = vox[:, pl.ds(pl.multiple_of(vcols * c, 128), vcols)]

        lane = lax.broadcasted_iota(jnp.int32, (1, own), 1)
        pieces = []
        for par in (k, 1 - k):
            for d in range(4):
                ids = ((c + 4 - d) % 4) * (2 * own) + par * own + lane
                pieces.append(jnp.where(ids < count, 0.0, NEG).astype(F32))
        bias = jnp.concatenate(pieces, axis=1)
        kv_cp.wait_recv()

        dkv_cp, g_cp, qg_cp, x_cp = [], [], [], []

        def attend(h, between=None):
            hs = slice(HEAD_DIM * h, HEAD_DIM * (h + 1))
            keys = kvs[:, hs]
            values = kvs[:, part + HEAD_DIM * h : part + HEAD_DIM * (h + 1)]
            grad_k = jnp.zeros((slots, HEAD_DIM), F32)
            grad_v = jnp.zeros((slots, HEAD_DIM), F32)
            for b in range(group // QROWS):
                rs = slice(QROWS * b, QROWS * (b + 1))
                q = qs[rs, hs]
                go = gouts[rs, hs]
                s = dot_nt(q, keys) + bias
                e = jnp.exp(s - jnp.max(s, axis=1, keepdims=True))
                w = e * (1.0 / jnp.sum(e, axis=1, keepdims=True))
                p = w.astype(BF16)
                mixed = dot_nn(p, values)
                att[rs, hs] = mixed.astype(BF16)
                delta = jnp.sum(go.astype(F32) * mixed, axis=1, keepdims=True)
                gs = (w * (dot_nt(go, values) - delta)).astype(BF16)
                grad_q = (dot_nn(gs, keys) * (HEAD_DIM**-0.5)).astype(BF16)
                gq[h, rs, 0:HEAD_DIM] = grad_q
                gp[h, rs, 0:128] = jnp.concatenate([grad_q, mixed.astype(BF16)], axis=1)
                grad_k += dot_tn(gs, q)
                grad_v += dot_tn(p, go)
                if b == 0 and between is not None:
                    between()
            both = jnp.concatenate([grad_k, grad_v], axis=1)
            dkv_send[h] = both[group:].astype(BF16)
            dkv_cp.append(send(dkv_send.at[h], dkv_recv.at[h], mate))
            dkv[h] = both[0:group]

        def finish(h):
            dkv_cp[h].wait_recv()
            both = dkv[h] + dkv_recv[h].astype(F32)
            both = both.astype(BF16)
            gp[h, :, 128:] = both
            gq[h, :, HEAD_DIM:] = both
            g_cp.append(
                send_all(
                    [(gp.at[h, rows_of(d)], gpr.at[c, h], at_y(4 - d)) for d in (2, 1, 3)],
                    gp.at[h, pl.ds(0, 3 * own)],
                )
            )
            gpr[c, h] = gp[h, 0:own, :]
            whole = dot_nn(turned[...], gq[h])
            for t in range(8):
                qg[h, t] = whole[orows * t : orows * (t + 1), :]
            for t in range(4):
                qg_send[h, t] = qg[h, 2 * t + (1 - k)].astype(BF16)
            qg_cp.append(send(qg_send.at[h], qg_recv.at[h], mate))

        def swap(h):
            qg_cp[h].wait_recv()
            for t in range(4):
                block = (qg[h, 2 * t + k] + qg_recv[h, t].astype(F32)).astype(BF16)
                for r in range(4):
                    piece = block[24 * r : 24 * (r + 1), :]
                    if h < 2:
                        qx[r, t, :, part * h : part * (h + 1)] = piece
                    else:
                        qxl[r, t] = piece
            if h:
                buf, recv = (qx, qxr) if h == 1 else (qxl, qxlr)
                x_cp.append(
                    send_all(
                        [(buf.at[(x + d) % 4], recv.at[d - 1], at_x(d)) for d in (2, 1, 3)], recv
                    )
                )

        def turn():
            for n, (buf, recv) in enumerate(((qx, qxr), (qxl, qxlr))):
                x_cp[n].wait_recv()
                for t in range(4):
                    at = slice(2 * part * n, 2 * part + part * n)
                    qt[t, :, at] = (
                        buf[x, t].astype(F32)
                        + recv[0, t].astype(F32)
                        + recv[1, t].astype(F32)
                        + recv[2, t].astype(F32)
                    ).astype(BF16)
            cp = send_all(
                [(qt.at[(c + d) % 4], qr.at[c], at_y(d)) for d in (2, 1, 3)], qr.at[pl.ds(0, 3)]
            )
            qr[c] = qt[c]
            return cp

        def back(h):
            g_cp[h].wait_recv()
            total = jnp.zeros((own, width), F32)
            for t in range(4):
                at = part * t + HEAD_DIM * h
                afull[:, at : at + HEAD_DIM] = gpr[t, h, :, HEAD_DIM : 2 * HEAD_DIM]
                total += dot_nt(gpr[t, h], wback[t, h])
            return total

        attend(0)
        attend(1, lambda: finish(0))
        attend(2, lambda: finish(1))
        swap(0)
        og[...] = dot_tn(att[...], seeds[...])
        og_send[...] = og[pl.ds(pl.multiple_of(orows * (1 - k), 32), orows), :].astype(BF16)
        og_cp = send(og_send, og_recv, mate)
        finish(2)
        swap(1)
        swap(2)
        og_cp.wait_recv()
        og_sum = (
            og[pl.ds(pl.multiple_of(orows * k, 32), orows), :] + og_recv[...].astype(F32)
        ).astype(BF16)
        for r in range(4):
            ox[r] = og_sum[24 * r : 24 * (r + 1), :]
        ox_cp = send_all([(ox.at[(x + d) % 4], oxr.at[d - 1], at_x(d)) for d in (2, 1, 3)], oxr)
        early = back(0) + back(1)
        grad_unit = (early + back(2)) * gain
        unit_rows = unit[...]
        branch_grad = inverse * (
            grad_unit
            - jnp.mean(grad_unit, axis=1, keepdims=True)
            - unit_rows * jnp.mean(grad_unit * unit_rows, axis=1, keepdims=True)
        )
        gball[0:own, :] = (seeds[0:own, :].astype(F32) + branch_grad).astype(BF16)
        b_cp = gather_start(gball)

        t_cp = turn()

        half = width // 2
        z_order = (4, 3, 5, 2, 6, 1, 7)

        def z_piece(buf, where):
            return buf.at[where // 2, :, pl.ds(pl.multiple_of(half * (where % 2), 128), half)]

        gather_pass(gball, b_cp)
        branch = dot_nn(afull[...], outw[...])
        latent_v[...] = (live * (base[...] + branch)).astype(BF16)
        l_latent = load(8, latent_v, latent_hbm)

        ox_cp.wait_recv()
        mz[3] = (
            ox[x].astype(F32) + oxr[0].astype(F32) + oxr[1].astype(F32) + oxr[2].astype(F32)
        ).astype(BF16)
        t_cp.wait_recv()
        for h in range(heads):
            for t in range(4):
                mz[h, :, part * t : part * (t + 1)] = qr[t, :, part * h : part * (h + 1)]
        mz_cp = send_all(
            [(z_piece(mz, (z + d) % 8), mzr.at[d - 1], at_z(d)) for d in z_order], mzr
        )
        v_cp.wait_recv()
        for d in (1, 3, 2):
            gather_wait(b_cp, d)
        ig[...] = dot_tn(vcol[...], gball[...])
        ig_send[...] = ig[pl.ds(pl.multiple_of(own * (1 - k), 128), own), :].astype(BF16)
        ig_cp = send(ig_send, ig_recv, mate)
        ig_cp.wait_recv()
        ig_sum = (
            ig[pl.ds(pl.multiple_of(own * k, 128), own), :] + ig_recv[...].astype(F32)
        ).astype(BF16)
        for r in range(16):
            for s in range(2):
                p = 2 * r + s
                ix[p // 8, p % 8] = ig_sum[8 * r : 8 * (r + 1), half * s : half * (s + 1)]
        ix_cp = send_all([(ix.at[(x + d) % 4], ixr.at[d - 1], at_x(d)) for d in (2, 1, 3)], ixr)

        mz_cp.wait_recv()
        total = z_piece(mz, z)[...].astype(F32)
        for d in range(7):
            total += mzr[d].astype(F32)
        mf[...] = total.astype(BF16)
        near, far = (1, 7, 2, 6), (3, 4, 5)
        mg_cp = [
            send_all([(mf, z_piece(mg.at[x], z), at_z(d)) for d in ds], mzr.at[pl.ds(0, len(ds))])
            for ds in (near, far)
        ]
        mg[x, z // 2, :, pl.ds(pl.multiple_of(half * (z % 2), 128), half)] = mf[...]
        mo_n = used[0]
        used[0] += 1

        def spread(src, where):
            for d in (2, 1, 3):
                pltpu.make_async_remote_copy(
                    src_ref=src, dst_ref=z_piece(mg.at[x], where),
                    send_sem=ssem.at[mo_n], recv_sem=rsem.at[mo_n],
                    device_id=at_x(d), device_id_type=MESH,
                ).start()

        mo_cp = Group(mg.at[pl.ds(0, 3)], ssem.at[mo_n], rsem.at[mo_n])
        sent.append(mo_cp)
        spread(mf, z)
        ix_cp.wait_recv()
        for p in range(8):
            iz[p] = (
                ix[x, p].astype(F32)
                + ixr[0, p].astype(F32)
                + ixr[1, p].astype(F32)
                + ixr[2, p].astype(F32)
            ).astype(BF16)
        iz_cp = send_all([(iz.at[(z + d) % 8], izr.at[d - 1], at_z(d)) for d in z_order], izr)
        for cp, ds in zip(mg_cp, (near, far)):
            cp.wait_recv()
            for d in ds:
                spread(z_piece(mg.at[x], (z + 8 - d) % 8), (z + 8 - d) % 8)
        iz_cp.wait_recv()
        total = iz[z].astype(F32)
        for d in range(7):
            total += izr[d].astype(F32)
        jf[...] = total.astype(BF16)
        pl.semaphore_wait(ready, 3)
        jg_cp = send_all(
            [(jf, jg.at[x * 8 + z], at_o(*f)) for f in others], jg.at[pl.ds(0, len(others))]
        )
        jg[x * 8 + z] = jf[...]
        mo_cp.wait_recv()
        l_main = load(0, mg, gmain_hbm)
        jg_cp.wait_recv()
        l_gin = load(9, jg, gin_hbm)
        for cp in sent:
            cp.wait_send()
        l_latent.wait()
        l_gin.wait()
        l_main.wait()

    scratch = [
        ((views, patches), jnp.int32), ((width,), F32), ((own, width), BF16),
        ((CHUNKS, patches, cols), BF16), ((feat, width), BF16), ((width, 3 * width), BF16),
        ((width, width), BF16), ((own, width), BF16), ((2, group, patches), BF16),
        ((CHUNKS, group, cols), BF16), ((CHUNKS, group, cols), BF16), ((CHUNKS, own, cols), F32),
        ((CHUNKS, group, cols), BF16), ((CHUNKS - 1, 2, own, cols // 2), F32),
        ((CHUNKS - 1, 2, own, cols // 2), BF16), ((CHUNKS - 1, 2, own, cols), BF16),
        ((3, own, cols), BF16),
        ((group, width), BF16), ((own, feat), BF16), ((group, vcols), BF16),
        ((own, width), F32), ((own, width), F32), ((group, width), BF16), ((width, group), BF16),
        ((width, 3 * part), BF16), ((group, part), BF16), ((slots, 2 * part), BF16),
        ((group, part), BF16), ((4, heads, width, 256), BF16),
        ((group, part), BF16), ((own, width), BF16),
        ((heads, group, 128), F32), ((heads, group, 128), BF16), ((heads, group, 128), BF16),
        ((heads, group, 256), BF16), ((heads, group, part), BF16), ((4, heads, own, 256), BF16),
        ((part, width), F32), ((orows, width), BF16), ((orows, width), BF16),
        ((heads, 8, orows, part), F32), ((heads, 4, orows, part), BF16),
        ((heads, 4, orows, part), BF16),
        ((4, 4, 24, 2 * part), BF16), ((3, 4, 24, 2 * part), BF16),
        ((4, 4, 24, part), BF16), ((3, 4, 24, part), BF16),
        ((4, 24, 3 * part), BF16), ((4, 24, 3 * part), BF16),
        ((4, 24, width), BF16), ((3, 24, width), BF16),
        ((group, width), BF16), ((2 * own, width), F32), ((own, width), BF16), ((own, width), BF16),
        ((4, 24, width), BF16),
        ((7, 24, width // 2), BF16), ((24, width // 2), BF16), ((4, 4, 24, width), BF16),
        ((4, 8, 8, width // 2), BF16), ((3, 8, 8, width // 2), BF16),
        ((8, 8, width // 2), BF16), ((7, 8, width // 2), BF16),
        ((8, width // 2), BF16), ((objects, 8, width // 2), BF16),
    ]
    return kernel, scratch


def write_out(
    latent_hbm, gin_hbm, gmain_hbm, latent_out, in_out, qkv_out, out_out,
    latent_v, gin_v, gmain_v, in_v, qkv_v, out_v, lsem, osem,
):
    width = latent_v.shape[1]
    half = width // 2
    part = width // 4
    loads = [pltpu.make_async_copy(gmain_hbm.at[r], gmain_v.at[r], lsem.at[r]) for r in range(4)]
    loads.append(pltpu.make_async_copy(gin_hbm, gin_v, lsem.at[4]))
    loads.append(pltpu.make_async_copy(latent_hbm, latent_v, lsem.at[5]))
    for cp in loads:
        cp.start()
    stores = []

    def store(src, dst):
        cp = pltpu.make_async_copy(src, dst, osem.at[len(stores)])
        cp.start()
        stores.append(cp)

    for r in range(4):
        loads[r].wait()
        at = slice(24 * r, 24 * (r + 1))
        for s in range(3):
            for t in range(4):
                for h in range(3):
                    to = width * s + part * t + HEAD_DIM * h
                    fr = part * t + HEAD_DIM * s
                    qkv_v[at, to : to + HEAD_DIM] = gmain_v[r, h, :, fr : fr + HEAD_DIM].astype(F32)
        store(qkv_v.at[pl.ds(24 * r, 24)], qkv_out.at[pl.ds(24 * r, 24)])
        out_v[at, :] = gmain_v[r, 3].astype(F32)
    store(out_v, out_out)
    loads[4].wait()
    for r in range(16):
        for s in range(2):
            in_v[8 * r : 8 * (r + 1), half * s : half * (s + 1)] = gin_v[2 * r + s].astype(F32)
    store(in_v, in_out)
    loads[5].wait()
    store(latent_v, latent_out)
    for cp in stores:
        cp.wait()


def per_device(
    features, projection, active_count, in_weight, norm_gain, qkv_weight, out_weight, cotangent
):
    patches, feat = features.shape[2:]
    own, width = cotangent.shape[1:]
    views = projection.shape[1]
    objects = lax.axis_size("obj")
    kernel, scratch = make_kernel((patches, feat, width, own, objects, views))
    hbm = pl.BlockSpec(memory_space=pl.ANY)
    latent, gin, gmain = pl.pallas_call(
        kernel,
        name="encode",
        out_shape=(
            jax.ShapeDtypeStruct((own, width), BF16),
            jax.ShapeDtypeStruct((objects, 8, width // 2), BF16),
            jax.ShapeDtypeStruct((4, 4, 24, width), BF16),
        ),
        in_specs=[hbm] * 8,
        out_specs=(hbm, hbm, hbm),
        scratch_shapes=[pltpu.VMEM(s, t) for s, t in scratch]
        + [
            pltpu.SMEM((1,), jnp.int32),
            pltpu.SemaphoreType.DMA((56,)),
            pltpu.SemaphoreType.DMA((56,)),
            pltpu.SemaphoreType.DMA((10 + CHUNKS,)),
            pltpu.SemaphoreType.REGULAR,
        ],
        compiler_params=pltpu.CompilerParams(
            collective_id=0, has_side_effects=True, vmem_limit_bytes=62 * 1024 * 1024
        ),
    )(
        features.reshape(patches, feat),
        projection.reshape(views, patches),
        active_count,
        in_weight,
        norm_gain,
        qkv_weight,
        out_weight,
        cotangent.reshape(own, width),
    )
    latent, in_grad, qkv_grad, out_grad = pl.pallas_call(
        write_out,
        name="write_out",
        out_shape=(
            jax.ShapeDtypeStruct((own, width), BF16),
            jax.ShapeDtypeStruct((own, width), F32),
            jax.ShapeDtypeStruct((96, 3 * width), F32),
            jax.ShapeDtypeStruct((96, width), F32),
        ),
        in_specs=[hbm, hbm, hbm],
        out_specs=(hbm, hbm, hbm, hbm),
        scratch_shapes=[
            pltpu.VMEM((own, width), BF16),
            pltpu.VMEM((objects, 8, width // 2), BF16),
            pltpu.VMEM((4, 4, 24, width), BF16),
            pltpu.VMEM((own, width), F32),
            pltpu.VMEM((96, 3 * width), F32),
            pltpu.VMEM((96, width), F32),
            pltpu.SemaphoreType.DMA((6,)),
            pltpu.SemaphoreType.DMA((7,)),
        ],
    )(latent, gin, gmain)
    return (latent[None], in_grad, qkv_grad, out_grad)


def solution(mesh):
    return jax.shard_map(
        per_device,
        mesh=mesh,
        in_specs=(
            P("obj", "view", None, None),
            P("obj", None, None),
            P("obj"),
            P(),
            P(),
            P(),
            P(),
            P("obj", "view", None),
        ),
        out_specs=(P("obj", "view", None), P("view", None), P("view", None), P("view", None)),
        check_vma=False,
    )
```
